32 devices in a mesh: slab: 4 (over y, core), filt: 8 (over z, x).
Axes of the slice: x: 2, y: 2, z: 4, core: 2. Of those that a mesh axis runs over, the one named last changes fastest.
Arguments:
- volume: float32 [512, 32, 256], P('filt', 'slab'), may hold values from -6 to 6
- filters: float32 [27, 512, 512], P(None, 'filt'), may hold values from -0.0546875 to 0.0546875
- out_grad: float32 [512, 32, 256], P('filt', 'slab'), may hold values from -6 to 6
Outputs:
- activated: float32 [512, 32, 256], P('filt', 'slab')
- input_grad: float32 [512, 32, 256], P('filt', 'slab')
- weight_grad: float32 [27, 512, 512], P(None, 'filt')
The draws below stay inside these ranges and needn't reach their ends.
All inputs are finite; a program needn't handle non-finite values.
Results may differ from the reference program's by a relative error of at most 0.00012.
Values sent between devices are 32-bit elements; how exact they have to be, the bound alone decides.
No kernel may reach another device: no remote copies, remote signals or barrier semaphores. Data moves between devices by JAX's collectives and lax.ppermute only.
A program may use at most 128 MiB of HBM per device.

```python
import jax
import jax.numpy as jnp
from jax import lax

C = 512
TAPS = 27
HEIGHT = 16
WIDTH = 16
DEPTH = 32


def level_of(key, shape, cuts, smallest, largest):
    def one(axis_at, parts):
        steps = jax.random.uniform(jax.random.fold_in(jax.random.fold_in(key, 6), axis_at), (parts,), jnp.float32, smallest / len(cuts), largest / len(cuts))
        return jnp.repeat(jnp.exp(steps), shape[axis_at] // parts).reshape((-1,) + (1,) * (len(shape) - axis_at - 1))

    factor_of = one(*cuts[0])
    for cut in cuts[1:]:
        factor_of = factor_of * one(*cut)
    return factor_of


def noise(key, extent, spread, limit, cuts=(), held_as=jnp.bfloat16):
    gain = level_of(key, extent, cuts, -0.22, 0.18) if cuts else 1.0
    entries = jax.random.normal(key, extent, jnp.float32) * spread * gain
    return jnp.minimum(jnp.maximum(entries, -limit), limit).astype(held_as)


def setup_inputs(seed: int = 0) -> dict:
    arg_keys = jax.random.split(jax.random.key(seed), 4)
    return {
        "volume": noise(arg_keys[0], (C, DEPTH, HEIGHT * WIDTH), 1.0, 6.0, ((0, 8), (1, 4)), jnp.float32),
        "filters": noise(arg_keys[1], (TAPS, C, C), (TAPS * C) ** -0.5, 0.0546875, ((1, 8),), jnp.float32),
        "out_grad": noise(arg_keys[2], (C, DEPTH, HEIGHT * WIDTH), 1.0, 6.0, ((0, 8), (1, 4)), jnp.float32),
    }


def convolve(inputs, kernel):
    return lax.conv_general_dilated(inputs, kernel, (1, 1, 1), [(1, 1), (1, 1), (1, 1)], dimension_numbers=('NCDHW', 'OIDHW', 'NCDHW'), precision=lax.Precision.HIGHEST)

def reference(volume, filters, out_grad):
    inputs = volume.reshape(1, C, DEPTH, HEIGHT, WIDTH)
    kernel = filters.reshape(3, 3, 3, C, C).transpose(3, 4, 0, 1, 2)
    preact, pullback = jax.vjp(convolve, inputs, kernel)
    positive = jnp.maximum(preact, 0.0)
    activated = positive * positive
    pre_grad = 2.0 * positive * out_grad.reshape(preact.shape)
    grad_inputs, grad_kernel = pullback(pre_grad)
    voxels = DEPTH * HEIGHT * WIDTH
    weight_grad = grad_kernel.transpose(2, 3, 4, 0, 1).reshape(TAPS, C, C) / jnp.sqrt(jnp.float32(voxels))
    return (activated.reshape(C, DEPTH, HEIGHT * WIDTH), grad_inputs.reshape(C, DEPTH, HEIGHT * WIDTH), weight_grad)
```

```python
import functools
import math

import jax
import jax.numpy as jnp
from jax import lax
from jax.experimental import pallas as pl
from jax.experimental.pallas import tpu as pltpu
from jax.sharding import PartitionSpec as P

WIDTH = 16


f32 = jnp.float32
bf16 = jnp.bfloat16


def parts_of(x):
    high = x.astype(bf16)
    low = (x - high.astype(f32)).astype(bf16)
    return high, low


def dot(a, b):
    return lax.dot_general(a, b, (((1,), (0,)), ((), ())), preferred_element_type=f32)


def dot_t(a, b):
    return lax.dot_general(a, b, (((1,), (1,)), ((), ())), preferred_element_type=f32)


def whole(shape):
    return pl.BlockSpec(shape, lambda *_: (0,) * len(shape))


def limit():
    return pltpu.CompilerParams(vmem_limit_bytes=28 * 2**20)


def cost(flops, moved):
    return pl.CostEstimate(flops=int(flops), bytes_accessed=int(moved), transcendentals=0)


def moved(x, down, across):
    size = x.shape[-1]
    place = lax.broadcasted_iota(jnp.int32, x.shape, 1)
    if across:
        column = place % WIDTH + across
        rolled = pltpu.roll(x, (-across) % size, 1)
        x = jnp.where((column >= 0) & (column < WIDTH), rolled, 0.0)
    if down:
        target = place + down * WIDTH
        rolled = pltpu.roll(x, (-down * WIDTH) % size, 1)
        x = jnp.where((target >= 0) & (target < size), rolled, 0.0)
    return x


def prepare_kernel(chan, filters, ahead, back_high, back_low):
    taps, out_rows, lanes = filters.shape
    third = taps * out_rows // 3
    for a in range(3):
        x = filters[a * 9 : (a + 1) * 9].reshape(third, lanes)
        high, low = parts_of(x)
        for k in range(lanes // chan):
            at = slice(k * chan, (k + 1) * chan)
            ahead[a, k] = jnp.concatenate([high[:, at], low[:, at], high[:, at]], axis=1)
    turned = [filters[a * 9 : (a + 1) * 9].reshape(third, lanes).T for a in (2, 1, 0)]
    high, low = parts_of(jnp.concatenate(turned, axis=1))
    back_high[...] = high
    back_low[...] = low


def prepare(filters, chan):
    taps, out_rows, channels = filters.shape
    lanes = min(128, channels)
    each = lanes // chan
    return pl.pallas_call(
        functools.partial(prepare_kernel, chan),
        grid=(channels // lanes,),
        in_specs=[pl.BlockSpec((taps, out_rows, lanes), lambda i: (0, 0, i))],
        out_specs=[
            pl.BlockSpec((3, each, 9 * out_rows, 3 * chan), lambda i: (0, i, 0, 0)),
            pl.BlockSpec((lanes, taps * out_rows), lambda i: (i, 0)),
            pl.BlockSpec((lanes, taps * out_rows), lambda i: (i, 0)),
        ],
        out_shape=[
            jax.ShapeDtypeStruct((3, channels // chan, 9 * out_rows, 3 * chan), bf16),
            jax.ShapeDtypeStruct((channels, taps * out_rows), bf16),
            jax.ShapeDtypeStruct((channels, taps * out_rows), bf16),
        ],
        cost_estimate=cost(0, 5 * 4 * filters.size),
        compiler_params=limit(),
        name="prepare",
    )(filters)


def rims_kernel(*refs):
    blocks, (last, top) = refs[:-2], refs[-2:]
    at = 0
    for block in blocks:
        rows, depth, _ = block.shape
        planes = jnp.swapaxes(block[...], 0, 1)
        last[at : at + rows] = planes[depth - 1]
        top[at : at + rows] = planes[0]
        at += rows


def rims(blocks):
    rows = sum(b.shape[0] for b in blocks)
    shape = jax.ShapeDtypeStruct((rows, blocks[0].shape[2]), f32)
    return pl.pallas_call(
        rims_kernel,
        out_shape=[shape, shape],
        cost_estimate=cost(0, 4 * sum(b.size for b in blocks)),
        compiler_params=limit(),
        name="rims",
    )(*blocks)


def forward_kernel(counts, first, where, *refs):
    blocks = refs[: sum(counts)]
    refs = refs[sum(counts) :]
    below, above = refs[:2]
    sources = len(counts)
    weights = refs[2 : 2 + sources]
    rest = refs[2 + sources :]
    if first:
        total_out, high_all, low_all, field, high_part, low_part, sems = rest
        total_in = None
    else:
        total_in, _, _, total_out, high_all, low_all, field, high_part, low_part, sems = rest
    depth, out_rows, area = total_out.shape
    chan = field.shape[2] // 3
    copies = []
    begin = 0
    for k, pieces in enumerate(counts):

        def put(plane, x):
            high, low = parts_of(x)
            field[k, plane, 0:chan] = high
            field[k, plane, chan : 2 * chan] = high
            field[k, plane, 2 * chan : 3 * chan] = low
            high_part[k, :, plane * area : (plane + 1) * area] = high
            low_part[k, :, plane * area : (plane + 1) * area] = low

        put(0, below[k * chan : (k + 1) * chan])
        put(depth + 1, above[k * chan : (k + 1) * chan])
        loaded = [jnp.swapaxes(b[...], 0, 1) for b in blocks[begin : begin + pieces]]
        begin += pieces
        for plane in range(depth):
            rows = [b[plane] for b in loaded]
            put(plane + 1, rows[0] if pieces == 1 else jnp.concatenate(rows, axis=0))
        at = pl.ds(pl.multiple_of(where[k] * chan, chan), chan)
        for part, target, n in ((high_part, high_all, 0), (low_part, low_all, 1)):
            copies.append(pltpu.make_async_copy(part.at[k], target.at[at], sems.at[k, n]))
            copies[-1].start()

    for plane in range(depth):
        answer = None
        for a in range(3):
            for k in range(sources):
                term = dot(weights[k][a, 0], field[k, plane + a])
                answer = term if answer is None else answer + term
        rows = []
        for b in range(3):
            row = None
            for c in range(3):
                at = (3 * b + c) * out_rows
                term = moved(answer[at : at + out_rows], 0, c - 1)
                row = term if row is None else row + term
            rows.append(moved(row, b - 1, 0))
        total = rows[0] + rows[1] + rows[2]
        if total_in is not None:
            total = total + total_in[plane]
        total_out[plane] = total
    for copy in copies:
        copy.wait()


def forward(where, sets, below, above, weights, carry, sizes):
    depth, chan, area, channels, out_rows = sizes
    counts = tuple(len(s) for s in sets)
    blocks = [b for s in sets for b in s]
    first = carry is None
    lanes = (depth + 2) * area
    keep = pl.BlockSpec(memory_space=pl.ANY)

    def at_source(k):
        return pl.BlockSpec((3, 1) + weights.shape[2:], lambda i, s: (0, s[k], 0, 0))

    in_specs = [whole(b.shape) for b in blocks] + [whole(below.shape), whole(above.shape)]
    in_specs += [at_source(k) for k in range(len(sets))]
    args = blocks + [below, above] + [weights] * len(sets)
    aliases = {}
    if not first:
        base = len(args) + 1
        in_specs += [whole((depth, out_rows, area)), keep, keep]
        args += list(carry)
        aliases = {base: 0, base + 1: 1, base + 2: 2}
    return pl.pallas_call(
        functools.partial(forward_kernel, counts, first),
        grid_spec=pltpu.PrefetchScalarGridSpec(
            num_scalar_prefetch=1,
            grid=(1,),
            in_specs=in_specs,
            out_specs=[whole((depth, out_rows, area)), keep, keep],
            scratch_shapes=[
                pltpu.VMEM((len(sets), depth + 2, 3 * chan, area), bf16),
                pltpu.VMEM((len(sets), chan, lanes), bf16),
                pltpu.VMEM((len(sets), chan, lanes), bf16),
                pltpu.SemaphoreType.DMA((len(sets), 2)),
            ],
        ),
        out_shape=[
            jax.ShapeDtypeStruct((depth, out_rows, area), f32),
            jax.ShapeDtypeStruct((channels, lanes), bf16),
            jax.ShapeDtypeStruct((channels, lanes), bf16),
        ],
        input_output_aliases=aliases,
        cost_estimate=cost(
            len(sets) * 2 * 81 * out_rows * chan * depth * area, len(sets) * 8 * chan * lanes
        ),
        compiler_params=limit(),
        name="forward",
    )(where, *args)


def middle_kernel(total, grad, active_out, spread_out):
    depth, out_rows, area = total.shape
    positives = jnp.maximum(total[...], 0.0)
    active_out[...] = jnp.swapaxes(positives * positives, 0, 1)
    grads = jnp.swapaxes(grad[...], 0, 1)
    nothing = jnp.zeros((9 * out_rows, area), bf16)
    for part in range(2):
        spread_out[part, 0] = nothing
        spread_out[part, depth + 1] = nothing
    for plane in range(depth):
        pre_grad = 2.0 * positives[plane] * grads[plane]
        for c in range(3):
            across = moved(pre_grad, 0, 1 - c)
            for b in range(3):
                high, low = parts_of(moved(across, 1 - b, 0))
                at = (3 * b + c) * out_rows
                spread_out[0, plane + 1, at : at + out_rows] = high
                spread_out[1, plane + 1, at : at + out_rows] = low


def middle(total, grad):
    depth, out_rows, area = total.shape
    return pl.pallas_call(
        middle_kernel,
        out_shape=[
            jax.ShapeDtypeStruct((out_rows, depth, area), f32),
            jax.ShapeDtypeStruct((2, depth + 2, 9 * out_rows, area), bf16),
        ],
        cost_estimate=cost(0, 4 * 18 * out_rows * depth * area),
        compiler_params=limit(),
        name="middle",
    )(total, grad)


def inner_kernel(begin, planes, spread, high, low, out):
    deep = high.shape[1]
    count, chan, _ = out.shape
    area = spread.shape[3]
    for plane in range(begin, begin + planes):
        near = spread[0, plane : plane + 3].reshape(deep, area)
        far = spread[1, plane : plane + 3].reshape(deep, area)
        value = dot(high[...], near) + dot(high[...], far) + dot(low[...], near)
        lanes = slice((plane - begin) * area, (plane - begin + 1) * area)
        out[:, :, lanes] = value.reshape(count, chan, area)


def outer_kernel(spread, high, low, below, above):
    depth = spread.shape[1] - 2
    third = high.shape[1] // 3
    for out, plane, at in ((below, 1, 2 * third), (above, depth, 0)):
        lanes = slice(at, at + third)
        value = dot(high[:, lanes], spread[0, plane]) + dot(high[:, lanes], spread[1, plane])
        value = value + dot(low[:, lanes], spread[0, plane])
        out[...] = value.reshape(out.shape)


def inner_terms(begin, planes, spread, high, low, chan):
    channels, deep = high.shape
    area = spread.shape[3]
    return pl.pallas_call(
        functools.partial(inner_kernel, begin, planes),
        out_shape=jax.ShapeDtypeStruct((channels // chan, chan, planes * area), f32),
        cost_estimate=cost(6 * channels * deep * planes * area, 2 * spread.size + 4 * high.size),
        compiler_params=limit(),
        name="inner_terms",
    )(spread, high, low)


def outer_terms(spread, high, low, chan):
    channels, deep = high.shape
    shape = jax.ShapeDtypeStruct((channels // chan, chan, spread.shape[3]), f32)
    return pl.pallas_call(
        outer_kernel,
        out_shape=[shape, shape],
        cost_estimate=cost(4 * channels * deep * spread.shape[3], spread.size),
        compiler_params=limit(),
        name="outer_terms",
    )(spread, high, low)


def filter_kernel(tap, where, spread, high, low, keep_out, send_out, total):
    depth = spread.shape[1] - 2
    rows, area = spread.shape[2:]
    half = rows // 2
    channels = high.shape[0]
    step = min(256, channels)
    for at in range(0, channels, step):
        value = None
        for plane in range(depth):
            lanes = slice((tap + plane) * area, (tap + plane + 1) * area)
            right = high[at : at + step, lanes]
            term = dot_t(spread[0, plane + 1], right) + dot_t(spread[1, plane + 1], right)
            term = term + dot_t(spread[0, plane + 1], low[at : at + step, lanes])
            value = term if value is None else value + term
        total[:, at : at + step] = value
    mine = pl.multiple_of(where[0] * half, half)
    other = pl.multiple_of((1 - where[0]) * half, half)
    keep_out[...] = total[pl.ds(mine, half), :]
    send_out[...] = total[pl.ds(other, half), :]


def filter_terms(tap, side, spread, high, low):
    rows = spread.shape[2]
    channels = high.shape[0]
    return pl.pallas_call(
        functools.partial(filter_kernel, tap),
        grid_spec=pltpu.PrefetchScalarGridSpec(
            num_scalar_prefetch=1,
            grid=(1,),
            in_specs=[whole(spread.shape), whole(high.shape), whole(low.shape)],
            out_specs=[whole((rows // 2, channels))] * 2,
            scratch_shapes=[pltpu.VMEM((rows, channels), f32)],
        ),
        out_shape=[jax.ShapeDtypeStruct((rows // 2, channels), f32)] * 2,
        cost_estimate=cost(6 * rows * high.size, 4 * high.size + 2 * spread.size),
        compiler_params=limit(),
        name="filter_terms",
    )(side, spread, high, low)


def place_kernel(scale, where, *refs):
    mine, other, out = refs[0], refs[1], refs[-1]
    half = mine.shape[0]
    out[0, pl.ds(pl.multiple_of(where[0] * half, half), half), :] = mine[...] / scale
    out[0, pl.ds(pl.multiple_of((1 - where[0]) * half, half), half), :] = other[...] / scale


def place(tap, side, mine, other, carry, scale):
    half, channels = mine.shape
    args = [mine, other]
    in_specs = [whole(mine.shape)] * 2
    aliases = {}
    if carry is not None:
        args.append(carry)
        in_specs.append(pl.BlockSpec(memory_space=pl.ANY))
        aliases = {3: 0}
    return pl.pallas_call(
        functools.partial(place_kernel, scale),
        grid_spec=pltpu.PrefetchScalarGridSpec(
            num_scalar_prefetch=1,
            grid=(1,),
            in_specs=in_specs,
            out_specs=pl.BlockSpec((1, 2 * half, channels), lambda i, s: (tap, 0, 0)),
        ),
        out_shape=jax.ShapeDtypeStruct((3, 2 * half, channels), f32),
        input_output_aliases=aliases,
        cost_estimate=cost(0, 16 * half * channels),
        compiler_params=limit(),
        name="place",
    )(side, *args)


def local_sum(inner, rim, first):
    value, rim = inner[0], rim[0]
    area = rim.shape[1]
    width = value.shape[1]
    if first:
        return jnp.concatenate([value[:, :area] + rim, value[:, area:]], axis=1)
    return jnp.concatenate([value[:, : width - area], value[:, width - area :] + rim], axis=1)


def opening_kernel(first, where, inner, rim, up_out, down_out):
    value = local_sum(inner, rim, first)
    half = value.shape[0] // 2
    up_out[...] = value[:half]
    down_out[...] = value[half:]


def running_kernel(first, where, up_inner, up_rim, down_inner, down_rim, up, down, up_out, down_out):
    value = local_sum(up_inner, up_rim, first)
    size = up.shape[0]
    up_out[0:size] = value[0:size] + up[...]
    if size < value.shape[0]:
        up_out[size:] = value[size:]
    value = local_sum(down_inner, down_rim, first)
    rest = value.shape[0] - size
    down_out[rest:] = value[rest:] + down[...]
    if rest:
        down_out[0:rest] = value[0:rest]


def closing_kernel(where, *refs):
    chains, out = (refs[0:4], refs[4:8]), refs[8]
    area = out.shape[2]
    values = []
    for first, (inner, rim, up, down) in zip((True, False), chains):
        value = local_sum(inner, rim, first) + up[...] + down[...]
        values += [value[:, at : at + area] for at in range(0, value.shape[1], area)]
    out[...] = jnp.swapaxes(jnp.stack(values), 0, 1)


def summed(kernel, where, pieces, outs, name):
    specs, args = [], []
    for piece in pieces:
        if isinstance(piece, tuple):
            array, k = piece
            specs.append(pl.BlockSpec((1,) + array.shape[1:], lambda i, s, k=k: (s[k], 0, 0)))
            args.append(array)
        else:
            specs.append(whole(piece.shape))
            args.append(piece)
    return pl.pallas_call(
        kernel,
        grid_spec=pltpu.PrefetchScalarGridSpec(
            num_scalar_prefetch=1,
            grid=(1,),
            in_specs=specs,
            out_specs=[whole(o) for o in outs],
        ),
        out_shape=[jax.ShapeDtypeStruct(o, f32) for o in outs],
        cost_estimate=cost(0, sum(12 * math.prod(o) for o in outs)),
        compiler_params=limit(),
        name=name,
    )(where, *args)


def shards(volume, filters, out_grad):
    chan, depth, area = volume.shape
    out_rows = filters.shape[1]
    channels = filters.shape[2]
    count = lax.axis_size("filt")
    slabs = lax.axis_size("slab")
    sizes = (depth, chan, area, channels, out_rows)

    order = list(range(0, count, 2)) + list(range(1, count, 2))[::-1]
    ring_up = [(order[i], order[(i + 1) % count]) for i in range(count)]
    ring_down = [(b, a) for a, b in ring_up]
    spot = [order.index(i) for i in range(count)]
    around = jnp.array(order, jnp.int32)
    here = jnp.array(spot, jnp.int32)[lax.axis_index("filt")]

    def device_at(step):
        return around[(here + step) % count]

    def send(x, pairs):
        return lax.ppermute(x, "filt", pairs)

    deeper = [(i, i + 1) for i in range(slabs - 1)]
    shallower = [(b, a) for a, b in deeper]

    ahead, back_high, back_low = prepare(filters, chan)

    half = count // 2
    carry = None
    up = down = volume
    for step in range(half + 1):
        if step == 0:
            sets, distances = [[volume]], [0]
        elif step < half:
            up, down = send(up, ring_up), send(down, ring_down)
            sets, distances = [[up], [down]], [-step, step]
        else:
            up = send(up[: chan // 2], ring_up)
            down = send(down[chan // 2 :], ring_down)
            sets, distances = [[up, down]], [half]
        last, top = rims([b for blocks in sets for b in blocks])
        below = lax.ppermute(last, "slab", deeper)
        above = lax.ppermute(top, "slab", shallower)
        where = jnp.stack([device_at(d) for d in distances])
        carry = forward(where, sets, below, above, ahead, carry, sizes)

    total, high_field, low_field = carry
    activated, spread = middle(total, out_grad)

    below, above = outer_terms(spread, back_high, back_low, chan)
    from_above = lax.ppermute(below, "slab", shallower)
    from_below = lax.ppermute(above, "slab", deeper)
    run = depth // 2
    inner = [inner_terms(c * run, run, spread, back_high, back_low, chan) for c in range(2)]
    edge = [from_below, from_above]

    position = lax.axis_index("slab")
    side = (position % 2).astype(jnp.int32).reshape(1)
    scale = math.sqrt(depth * slabs * area)

    def swap(x, bit):
        return lax.ppermute(x, "slab", [(i, i ^ bit) for i in range(slabs)])

    weight_grad = None
    for tap in range(3):
        keep, give = filter_terms(tap, side, spread, high_field, low_field)
        keep = keep + swap(give, 1)
        bit = 2
        while bit < slabs:
            keep = keep + swap(keep, bit)
            bit *= 2
        weight_grad = place(tap, side, keep, swap(keep, 1), weight_grad, scale)

    piece = (chan, run * area)
    part = (chan // 2, run * area)
    flows = []
    where = device_at(half).reshape(1)
    for c in range(2):
        kernel = functools.partial(opening_kernel, c == 0)
        flows.append(summed(kernel, where, [(inner[c], 0), (edge[c], 0)], [part, part], "opening"))
    for step in range(half - 1, 0, -1):
        where = jnp.stack([device_at(step), device_at(-step)])
        for c in range(2):
            up, down = flows[c]
            up, down = send(up, ring_up), send(down, ring_down)
            kernel = functools.partial(running_kernel, c == 0)
            pieces = [(inner[c], 0), (edge[c], 0), (inner[c], 1), (edge[c], 1), up, down]
            flows[c] = summed(kernel, where, pieces, [piece, piece], "running")
    pieces = []
    for c in range(2):
        up, down = flows[c]
        pieces += [(inner[c], 0), (edge[c], 0), send(up, ring_up), send(down, ring_down)]
    (input_grad,) = summed(
        closing_kernel, device_at(0).reshape(1), pieces, [(chan, depth, area)], "closing"
    )
    return activated, input_grad, weight_grad.reshape(filters.shape)


def solution(mesh):
    placed = (P("filt", "slab", None), P(None, "filt", None), P("filt", "slab", None))
    return jax.shard_map(
        shards,
        mesh=mesh,
        in_specs=placed,
        out_specs=(P("filt", "slab", None), P("filt", "slab", None), P(None, "filt", None)),
        check_vma=False,
    )
```

```python
import functools
import math

import jax
import jax.numpy as jnp
from jax import lax
from jax.experimental import pallas as pl
from jax.experimental.pallas import tpu as pltpu
from jax.sharding import PartitionSpec as P


WIDTH = 16


f32 = jnp.float32
bf16 = jnp.bfloat16


def parts_of(x):
    high = x.astype(bf16)
    low = (x - high.astype(f32)).astype(bf16)
    return high, low


def dot(a, b):
    return lax.dot_general(a, b, (((1,), (0,)), ((), ())), preferred_element_type=f32)


def dot_t(a, b):
    return lax.dot_general(a, b, (((1,), (1,)), ((), ())), preferred_element_type=f32)


def whole(shape):
    return pl.BlockSpec(shape, lambda *_: (0,) * len(shape))


def limit():
    return pltpu.CompilerParams(vmem_limit_bytes=28 * 2**20)


def cost(flops, moved):
    return pl.CostEstimate(flops=int(flops), bytes_accessed=int(moved), transcendentals=0)


def moved(x, down, across):
    size = x.shape[-1]
    place = lax.broadcasted_iota(jnp.int32, x.shape, 1)
    if across:
        column = place % WIDTH + across
        rolled = pltpu.roll(x, (-across) % size, 1)
        x = jnp.where((column >= 0) & (column < WIDTH), rolled, 0.0)
    if down:
        target = place + down * WIDTH
        rolled = pltpu.roll(x, (-down * WIDTH) % size, 1)
        x = jnp.where((target >= 0) & (target < size), rolled, 0.0)
    return x


def prepare_kernel(chan, filters, ahead, back_high, back_low):
    taps, out_rows, lanes = filters.shape
    third = taps * out_rows // 3
    for a in range(3):
        x = filters[a * 9 : (a + 1) * 9].reshape(third, lanes)
        high, low = parts_of(x)
        for k in range(lanes // chan):
            at = slice(k * chan, (k + 1) * chan)
            ahead[a, k] = jnp.concatenate([high[:, at], low[:, at], high[:, at]], axis=1)
    turned = [filters[a * 9 : (a + 1) * 9].reshape(third, lanes).T for a in (2, 1, 0)]
    high, low = parts_of(jnp.concatenate(turned, axis=1))
    back_high[...] = high
    back_low[...] = low


def prepare(filters, chan):
    taps, out_rows, channels = filters.shape
    lanes = min(128, channels)
    each = lanes // chan
    return pl.pallas_call(
        functools.partial(prepare_kernel, chan),
        grid=(channels // lanes,),
        in_specs=[pl.BlockSpec((taps, out_rows, lanes), lambda i: (0, 0, i))],
        out_specs=[
            pl.BlockSpec((3, each, 9 * out_rows, 3 * chan), lambda i: (0, i, 0, 0)),
            pl.BlockSpec((lanes, taps * out_rows), lambda i: (i, 0)),
            pl.BlockSpec((lanes, taps * out_rows), lambda i: (i, 0)),
        ],
        out_shape=[
            jax.ShapeDtypeStruct((3, channels // chan, 9 * out_rows, 3 * chan), bf16),
            jax.ShapeDtypeStruct((channels, taps * out_rows), bf16),
            jax.ShapeDtypeStruct((channels, taps * out_rows), bf16),
        ],
        cost_estimate=cost(0, 5 * 4 * filters.size),
        name="prepare",
    )(filters)


def rims_kernel(*refs):
    blocks, (last, top) = refs[:-2], refs[-2:]
    at = 0
    for block in blocks:
        rows, depth, _ = block.shape
        planes = jnp.swapaxes(block[...], 0, 1)
        last[at : at + rows] = planes[depth - 1]
        top[at : at + rows] = planes[0]
        at += rows


def rims(blocks):
    rows = sum(b.shape[0] for b in blocks)
    shape = jax.ShapeDtypeStruct((rows, blocks[0].shape[2]), f32)
    return pl.pallas_call(
        rims_kernel,
        out_shape=[shape, shape],
        cost_estimate=cost(0, 4 * sum(b.size for b in blocks)),
        name="rims",
    )(*blocks)


def gathered(answer, out_rows):
    rows = []
    for b in range(3):
        row = None
        for c in range(3):
            at = (3 * b + c) * out_rows
            term = moved(answer[at : at + out_rows], 0, c - 1)
            row = term if row is None else row + term
        rows.append(moved(row, b - 1, 0))
    return rows[0] + rows[1] + rows[2]


def tripled(x):
    high, low = parts_of(x)
    return jnp.concatenate([high, high, low], axis=0)


def forward_kernel(counts, places, rim_places, first, ring, *refs):
    refs = list(refs)

    def take(n):
        taken = refs[:n]
        del refs[:n]
        return taken

    blocks = take(sum(counts))
    weights = take(len(counts))
    rims_in = take(2) if rim_places else []
    rim_weights = take(2 * len(rim_places))
    total_in = None if first else take(3)[0]
    total_out, high_all, low_all, field, high_part, low_part, high_rim, low_rim, sems = refs
    depth, out_rows, area = total_out.shape
    chan = field.shape[2] // 3
    copies = []

    def keep(part, target, place, lanes):
        at = pl.ds(pl.multiple_of(ring[place] * chan, chan), chan)
        copies.append(pltpu.make_async_copy(part, target.at[at, lanes], sems.at[len(copies)]))
        copies[-1].start()

    begin = 0
    for k, pieces in enumerate(counts):
        loaded = [jnp.swapaxes(b[...], 0, 1) for b in blocks[begin : begin + pieces]]
        begin += pieces
        for plane in range(depth):
            rows = [b[plane] for b in loaded]
            x = rows[0] if pieces == 1 else jnp.concatenate(rows, axis=0)
            high, low = parts_of(x)
            field[k, plane, 0:chan] = high
            field[k, plane, chan : 2 * chan] = high
            field[k, plane, 2 * chan : 3 * chan] = low
            high_part[k, :, plane * area : (plane + 1) * area] = high
            low_part[k, :, plane * area : (plane + 1) * area] = low
        lanes = pl.ds(area, depth * area)
        keep(high_part.at[k], high_all, places[k], lanes)
        keep(low_part.at[k], low_all, places[k], lanes)
    for n, rim in enumerate(rims_in):
        lanes = pl.ds(n * (depth + 1) * area, area)
        for k in range(len(rim_places)):
            high, low = parts_of(rim[k * chan : (k + 1) * chan])
            high_rim[n, k] = high
            low_rim[n, k] = low
            keep(high_rim.at[n, k], high_all, rim_places[k], lanes)
            keep(low_rim.at[n, k], low_all, rim_places[k], lanes)

    for plane in range(depth):
        terms = []
        for a in range(3):
            if 0 <= plane + a - 1 < depth:
                for k in range(len(counts)):
                    terms.append((weights[k][a, 0], field[k, plane + a - 1]))
        for n, edge in enumerate((0, depth - 1)):
            if plane == edge:
                for k in range(len(rim_places)):
                    right = tripled(rims_in[n][k * chan : (k + 1) * chan])
                    terms.append((rim_weights[2 * k + n][0, 0], right))
        answer = None
        for left, right in terms:
            term = dot(left, right)
            answer = term if answer is None else answer + term
        total = gathered(answer, out_rows)
        if total_in is not None:
            total = total + total_in[plane]
        total_out[plane] = total
    for copy in copies:
        copy.wait()


def rim_weights_of(weights, place):
    shape = (1, 1) + weights.shape[2:]
    return [
        pl.BlockSpec(shape, lambda i, s, a=a: (a, s[place], 0, 0)) for a in (0, 2)
    ]


def forward(ring, sets, places, rim_places, outer, weights, carry, sizes):
    depth, chan, area, channels, out_rows = sizes
    counts = tuple(len(s) for s in sets)
    blocks = [b for s in sets for b in s]
    first = carry is None
    lanes = (depth + 2) * area
    keep = pl.BlockSpec(memory_space=pltpu.HBM)
    in_specs = [whole(b.shape) for b in blocks]
    args = list(blocks)
    for place in places:
        shape = (3, 1) + weights.shape[2:]
        in_specs.append(pl.BlockSpec(shape, lambda i, s, p=place: (0, s[p], 0, 0)))
        args.append(weights)
    if rim_places:
        in_specs += [whole(o.shape) for o in outer]
        args += list(outer)
        for place in rim_places:
            in_specs += rim_weights_of(weights, place)
            args += [weights] * 2
    aliases = {}
    if not first:
        base = len(args) + 1
        in_specs += [whole((depth, out_rows, area)), keep, keep]
        args += list(carry)
        aliases = {base: 0, base + 1: 1, base + 2: 2}
    rims_held = max(1, len(rim_places))
    return pl.pallas_call(
        functools.partial(forward_kernel, counts, places, rim_places, first),
        grid_spec=pltpu.PrefetchScalarGridSpec(
            num_scalar_prefetch=1,
            grid=(1,),
            in_specs=in_specs,
            out_specs=[whole((depth, out_rows, area)), keep, keep],
            scratch_shapes=[
                pltpu.VMEM((len(sets), depth, 3 * chan, area), bf16),
                pltpu.VMEM((len(sets), chan, depth * area), bf16),
                pltpu.VMEM((len(sets), chan, depth * area), bf16),
                pltpu.VMEM((2, rims_held, chan, area), bf16),
                pltpu.VMEM((2, rims_held, chan, area), bf16),
                pltpu.SemaphoreType.DMA((2 * len(sets) + 4 * rims_held,)),
            ],
        ),
        out_shape=[
            jax.ShapeDtypeStruct((depth, out_rows, area), f32),
            jax.ShapeDtypeStruct((channels, lanes), bf16),
            jax.ShapeDtypeStruct((channels, lanes), bf16),
        ],
        input_output_aliases=aliases,
        cost_estimate=cost(
            len(sets) * 2 * 81 * out_rows * chan * depth * area, len(sets) * 8 * chan * lanes
        ),
        name="forward",
    )(ring, *args)


def middle_kernel(chan, ring, total, grad, below, above, left_below, left_above, *refs):
    active_out, spread_out, high_all, low_all, high_rim, low_rim, sems = refs[2:]
    depth, out_rows, area = total.shape
    copies = []
    rim_sums = []
    for n, (rim, left) in enumerate(((below, left_below), (above, left_above))):
        high, low = parts_of(rim[...])
        high_rim[n] = high
        low_rim[n] = low
        at = pl.ds(pl.multiple_of(ring[high_all.shape[0] // chan // 2] * chan, chan), chan)
        lanes = pl.ds(n * (depth + 1) * area, area)
        for m, (part, target) in enumerate(((high_rim, high_all), (low_rim, low_all))):
            copy = pltpu.make_async_copy(part.at[n], target.at[at, lanes], sems.at[n, m])
            copy.start()
            copies.append(copy)
        rim_sums.append(gathered(dot(left[0, 0], tripled(rim[...])), out_rows))
    positives = []
    for plane in range(depth):
        value = total[plane]
        if plane == 0:
            value = value + rim_sums[0]
        if plane == depth - 1:
            value = value + rim_sums[1]
        positives.append(jnp.maximum(value, 0.0))
    positives = jnp.stack(positives)
    active_out[...] = jnp.swapaxes(positives * positives, 0, 1)
    grads = jnp.swapaxes(grad[...], 0, 1)
    nothing = jnp.zeros((9 * out_rows, area), bf16)
    for part in range(2):
        spread_out[part, 0] = nothing
        spread_out[part, depth + 1] = nothing
    for plane in range(depth):
        pre_grad = 2.0 * positives[plane] * grads[plane]
        for c in range(3):
            across = moved(pre_grad, 0, 1 - c)
            for b in range(3):
                high, low = parts_of(moved(across, 1 - b, 0))
                at = (3 * b + c) * out_rows
                spread_out[0, plane + 1, at : at + out_rows] = high
                spread_out[1, plane + 1, at : at + out_rows] = low
    for copy in copies:
        copy.wait()


def middle(ring, carry, grad, outer, weights, chan):
    total, high_all, low_all = carry
    depth, out_rows, area = total.shape
    keep = pl.BlockSpec(memory_space=pltpu.HBM)
    half = high_all.shape[0] // chan // 2
    return pl.pallas_call(
        functools.partial(middle_kernel, chan),
        grid_spec=pltpu.PrefetchScalarGridSpec(
            num_scalar_prefetch=1,
            grid=(1,),
            in_specs=[whole(x.shape) for x in (total, grad, *outer)]
            + rim_weights_of(weights, half)
            + [keep, keep],
            out_specs=[
                whole((out_rows, depth, area)),
                whole((2, depth + 2, 9 * out_rows, area)),
                keep,
                keep,
            ],
            scratch_shapes=[
                pltpu.VMEM((2, chan, area), bf16),
                pltpu.VMEM((2, chan, area), bf16),
                pltpu.SemaphoreType.DMA((2, 2)),
            ],
        ),
        out_shape=[
            jax.ShapeDtypeStruct((out_rows, depth, area), f32),
            jax.ShapeDtypeStruct((2, depth + 2, 9 * out_rows, area), bf16),
            jax.ShapeDtypeStruct(high_all.shape, bf16),
            jax.ShapeDtypeStruct(low_all.shape, bf16),
        ],
        input_output_aliases={7: 2, 8: 3},
        cost_estimate=cost(0, 4 * 18 * out_rows * depth * area),
        compiler_params=limit(),
        name="middle",
    )(ring, total, grad, *outer, weights, weights, high_all, low_all)


def inner_kernel(begin, planes, spread, high, low, out):
    deep = high.shape[1]
    count, chan, _ = out.shape
    area = spread.shape[3]
    for plane in range(begin, begin + planes):
        near = spread[0, plane : plane + 3].reshape(deep, area)
        far = spread[1, plane : plane + 3].reshape(deep, area)
        value = dot(high[...], near) + dot(high[...], far) + dot(low[...], near)
        lanes = slice((plane - begin) * area, (plane - begin + 1) * area)
        out[:, :, lanes] = value.reshape(count, chan, area)


def outer_kernel(spread, high, low, below, above):
    depth = spread.shape[1] - 2
    third = high.shape[1] // 3
    for out, plane, at in ((below, 1, 2 * third), (above, depth, 0)):
        lanes = slice(at, at + third)
        value = dot(high[:, lanes], spread[0, plane]) + dot(high[:, lanes], spread[1, plane])
        value = value + dot(low[:, lanes], spread[0, plane])
        out[...] = value.reshape(out.shape)


def inner_terms(begin, planes, spread, high, low, chan):
    channels, deep = high.shape
    area = spread.shape[3]
    return pl.pallas_call(
        functools.partial(inner_kernel, begin, planes),
        out_shape=jax.ShapeDtypeStruct((channels // chan, chan, planes * area), f32),
        cost_estimate=cost(6 * channels * deep * planes * area, 2 * spread.size + 4 * high.size),
        compiler_params=limit(),
        name="inner_terms",
    )(spread, high, low)


def outer_terms(spread, high, low, chan):
    channels, deep = high.shape
    shape = jax.ShapeDtypeStruct((channels // chan, chan, spread.shape[3]), f32)
    return pl.pallas_call(
        outer_kernel,
        out_shape=[shape, shape],
        cost_estimate=cost(4 * channels * deep * spread.shape[3], spread.size),
        compiler_params=limit(),
        name="outer_terms",
    )(spread, high, low)


def filter_kernel(tap, ring, spread, high, low, keep_out, send_out, total):
    depth = spread.shape[1] - 2
    rows, area = spread.shape[2:]
    half = rows // 2
    channels = high.shape[0]
    step = min(256, channels)
    for at in range(0, channels, step):
        value = None
        for plane in range(depth):
            lanes = slice((tap + plane) * area, (tap + plane + 1) * area)
            right = high[at : at + step, lanes]
            term = dot_t(spread[0, plane + 1], right) + dot_t(spread[1, plane + 1], right)
            term = term + dot_t(spread[0, plane + 1], low[at : at + step, lanes])
            value = term if value is None else value + term
        total[:, at : at + step] = value
    side = ring[ring.shape[0] - 1]
    mine = pl.multiple_of(side * half, half)
    other = pl.multiple_of((1 - side) * half, half)
    keep_out[...] = total[pl.ds(mine, half), :]
    send_out[...] = total[pl.ds(other, half), :]


def filter_terms(tap, ring, spread, high, low):
    rows = spread.shape[2]
    channels = high.shape[0]
    return pl.pallas_call(
        functools.partial(filter_kernel, tap),
        grid_spec=pltpu.PrefetchScalarGridSpec(
            num_scalar_prefetch=1,
            grid=(1,),
            in_specs=[whole(spread.shape), whole(high.shape), whole(low.shape)],
            out_specs=[whole((rows // 2, channels))] * 2,
            scratch_shapes=[pltpu.VMEM((rows, channels), f32)],
        ),
        out_shape=[jax.ShapeDtypeStruct((rows // 2, channels), f32)] * 2,
        cost_estimate=cost(6 * rows * high.size, 4 * high.size + 2 * spread.size),
        compiler_params=limit(),
        name="filter_terms",
    )(ring, spread, high, low)


def place_kernel(scale, ring, *refs):
    mine, other, out = refs[0], refs[1], refs[-1]
    half = mine.shape[0]
    side = ring[ring.shape[0] - 1]
    out[0, pl.ds(pl.multiple_of(side * half, half), half), :] = mine[...] / scale
    out[0, pl.ds(pl.multiple_of((1 - side) * half, half), half), :] = other[...] / scale


def place(tap, ring, mine, other, carry, scale):
    half, channels = mine.shape
    args = [mine, other]
    in_specs = [whole(mine.shape)] * 2
    aliases = {}
    if carry is not None:
        args.append(carry)
        in_specs.append(pl.BlockSpec(memory_space=pl.ANY))
        aliases = {3: 0}
    return pl.pallas_call(
        functools.partial(place_kernel, scale),
        grid_spec=pltpu.PrefetchScalarGridSpec(
            num_scalar_prefetch=1,
            grid=(1,),
            in_specs=in_specs,
            out_specs=pl.BlockSpec((1, 2 * half, channels), lambda i, s: (tap, 0, 0)),
        ),
        out_shape=jax.ShapeDtypeStruct((3, 2 * half, channels), f32),
        input_output_aliases=aliases,
        cost_estimate=cost(0, 16 * half * channels),
        compiler_params=limit(),
        name="place",
    )(ring, *args)


def local_sum(inner, rim, first):
    value, rim = inner[0], rim[0]
    area = rim.shape[1]
    width = value.shape[1]
    if first:
        return jnp.concatenate([value[:, :area] + rim, value[:, area:]], axis=1)
    return jnp.concatenate([value[:, : width - area], value[:, width - area :] + rim], axis=1)


def opening_kernel(first, ring, inner, rim, up_out, down_out):
    value = local_sum(inner, rim, first)
    half = value.shape[0] // 2
    up_out[...] = value[:half]
    down_out[...] = value[half:]


def running_kernel(first, ring, up_inner, up_rim, down_inner, down_rim, up, down, up_out, down_out):
    value = local_sum(up_inner, up_rim, first)
    size = up.shape[0]
    up_out[0:size] = value[0:size] + up[...]
    if size < value.shape[0]:
        up_out[size:] = value[size:]
    value = local_sum(down_inner, down_rim, first)
    rest = value.shape[0] - size
    down_out[rest:] = value[rest:] + down[...]
    if rest:
        down_out[0:rest] = value[0:rest]


def closing_kernel(ring, *refs):
    chains, out = (refs[0:4], refs[4:8]), refs[8]
    area = out.shape[2]
    values = []
    for first, (inner, rim, up, down) in zip((True, False), chains):
        value = local_sum(inner, rim, first) + up[...] + down[...]
        values += [value[:, at : at + area] for at in range(0, value.shape[1], area)]
    out[...] = jnp.swapaxes(jnp.stack(values), 0, 1)


def summed(kernel, ring, pieces, outs):
    specs, args = [], []
    for piece in pieces:
        if isinstance(piece, tuple):
            array, k = piece
            specs.append(pl.BlockSpec((1,) + array.shape[1:], lambda i, s, k=k: (s[k], 0, 0)))
            args.append(array)
        else:
            specs.append(whole(piece.shape))
            args.append(piece)
    return pl.pallas_call(
        kernel,
        grid_spec=pltpu.PrefetchScalarGridSpec(
            num_scalar_prefetch=1,
            grid=(1,),
            in_specs=specs,
            out_specs=[whole(o) for o in outs],
        ),
        out_shape=[jax.ShapeDtypeStruct(o, f32) for o in outs],
        cost_estimate=cost(0, sum(12 * math.prod(o) for o in outs)),
        compiler_params=limit(),
    )(ring, *args)


def shards(volume, filters, out_grad):
    chan, depth, area = volume.shape
    out_rows = filters.shape[1]
    channels = filters.shape[2]
    count = lax.axis_size("filt")
    slabs = lax.axis_size("slab")
    sizes = (depth, chan, area, channels, out_rows)

    order = list(range(0, count, 2)) + list(range(1, count, 2))[::-1]
    ring_up = [(order[i], order[(i + 1) % count]) for i in range(count)]
    ring_down = [(b, a) for a, b in ring_up]
    rows = [
        [order[(order.index(f) + k) % count] for k in range(count)] + [s % 2]
        for s in range(slabs)
        for f in range(count)
    ]
    here = lax.axis_index("slab") * count + lax.axis_index("filt")
    ring = lax.dynamic_index_in_dim(jnp.array(rows, jnp.int32), here, 0, keepdims=False)

    def send(x, pairs):
        return lax.ppermute(x, "filt", pairs)

    deeper = [(i, i + 1) for i in range(slabs - 1)]
    shallower = [(b, a) for a, b in deeper]
    half = count // 2

    ahead, back_high, back_low = prepare(filters, chan)

    carry = None
    up = down = volume
    rim_places, outer = (), None
    for step in range(half + 1):
        if step == 0:
            sets, places = [[volume]], (0,)
        elif step < half:
            up, down = send(up, ring_up), send(down, ring_down)
            sets, places = [[up], [down]], (count - step, step)
        else:
            up = send(up[: chan // 2], ring_up)
            down = send(down[chan // 2 :], ring_down)
            sets, places = [[up, down]], (half,)
        last, top = rims([b for blocks in sets for b in blocks])
        carry = forward(ring, sets, places, rim_places, outer, ahead, carry, sizes)
        outer = lax.ppermute(last, "slab", deeper), lax.ppermute(top, "slab", shallower)
        rim_places = places

    activated, spread, high_field, low_field = middle(ring, carry, out_grad, outer, ahead, chan)

    below, above = outer_terms(spread, back_high, back_low, chan)
    from_above = lax.ppermute(below, "slab", shallower)
    from_below = lax.ppermute(above, "slab", deeper)
    run = depth // 2
    inner = []
    for c in range(2):
        inner.append(inner_terms(c * run, run, spread, back_high, back_low, chan))
    edge = [from_below, from_above]

    scale = math.sqrt(depth * slabs * area)

    def swap(x, bit):
        return lax.ppermute(x, "slab", [(i, i ^ bit) for i in range(slabs)])

    weight_grad = None
    for tap in range(3):
        keep, give = filter_terms(tap, ring, spread, high_field, low_field)
        keep = keep + swap(give, 1)
        bit = 2
        while bit < slabs:
            keep = keep + swap(keep, bit)
            bit *= 2
        other = swap(keep, 1)
        weight_grad = place(tap, ring, keep, other, weight_grad, scale)

    piece = (chan, run * area)
    part = (chan // 2, run * area)
    flows = []
    for c in range(2):
        kernel = functools.partial(opening_kernel, c == 0)
        flows.append(summed(kernel, ring, [(inner[c], half), (edge[c], half)], [part, part]))
    for step in range(half - 1, 0, -1):
        for c in range(2):
            up, down = flows[c]
            up, down = send(up, ring_up), send(down, ring_down)
            kernel = functools.partial(running_kernel, c == 0)
            pieces = [(x, p) for p in (step, count - step) for x in (inner[c], edge[c])]
            flows[c] = summed(kernel, ring, pieces + [up, down], [piece, piece])
    pieces = []
    for c in range(2):
        up, down = flows[c]
        pieces += [(inner[c], 0), (edge[c], 0), send(up, ring_up), send(down, ring_down)]
    (input_grad,) = summed(closing_kernel, ring, pieces, [(chan, depth, area)])
    return activated, input_grad, weight_grad.reshape(filters.shape)


def solution(mesh):
    placed = (P("filt", "slab", None), P(None, "filt", None), P("filt", "slab", None))

    def step(*args):
        return shards(*args)

    step = jax.shard_map(
        step,
        mesh=mesh,
        in_specs=placed,
        out_specs=(P("filt", "slab", None), P("filt", "slab", None), P(None, "filt", None)),
        check_vma=False,
    )
    return step
```

```python
import functools
import math

import jax
import jax.numpy as jnp
from jax import lax
from jax.experimental import pallas as pl
from jax.experimental.pallas import tpu as pltpu
from jax.sharding import PartitionSpec as P


WIDTH = 16


f32 = jnp.float32
bf16 = jnp.bfloat16


def parts_of(x):
    high = x.astype(bf16)
    low = (x - high.astype(f32)).astype(bf16)
    return high, low


def dot(a, b):
    return lax.dot_general(a, b, (((1,), (0,)), ((), ())), preferred_element_type=f32)


def dot_t(a, b):
    return lax.dot_general(a, b, (((1,), (1,)), ((), ())), preferred_element_type=f32)


def beside(ring, n, rim):
    return jnp.where(ring[ring.shape[0] - 3 + n] > 0, rim, 0.0)


def whole(shape):
    return pl.BlockSpec(shape, lambda *_: (0,) * len(shape))


def limit():
    return pltpu.CompilerParams(vmem_limit_bytes=28 * 2**20)


def cost(flops, moved):
    return pl.CostEstimate(flops=int(flops), bytes_accessed=int(moved), transcendentals=0)


def moved(x, down, across):
    size = x.shape[-1]
    place = lax.broadcasted_iota(jnp.int32, x.shape, 1)
    if across:
        column = place % WIDTH + across
        rolled = pltpu.roll(x, (-across) % size, 1)
        x = jnp.where((column >= 0) & (column < WIDTH), rolled, 0.0)
    if down:
        target = place + down * WIDTH
        rolled = pltpu.roll(x, (-down * WIDTH) % size, 1)
        x = jnp.where((target >= 0) & (target < size), rolled, 0.0)
    return x


def prepare_kernel(chan, filters, ahead, back_high, back_low):
    taps, out_rows, lanes = filters.shape
    third = taps * out_rows // 3
    for a in range(3):
        x = filters[a * 9 : (a + 1) * 9].reshape(third, lanes)
        high, low = parts_of(x)
        for k in range(lanes // chan):
            at = slice(k * chan, (k + 1) * chan)
            ahead[a, k] = jnp.concatenate([high[:, at], low[:, at], high[:, at]], axis=1)
    turned = [filters[a * 9 : (a + 1) * 9].reshape(third, lanes).T for a in (2, 1, 0)]
    high, low = parts_of(jnp.concatenate(turned, axis=1))
    back_high[...] = high
    back_low[...] = low


def prepare(filters, chan):
    taps, out_rows, channels = filters.shape
    lanes = min(128, channels)
    each = lanes // chan
    return pl.pallas_call(
        functools.partial(prepare_kernel, chan),
        grid=(channels // lanes,),
        in_specs=[pl.BlockSpec((taps, out_rows, lanes), lambda i: (0, 0, i))],
        out_specs=[
            pl.BlockSpec((3, each, 9 * out_rows, 3 * chan), lambda i: (0, i, 0, 0)),
            pl.BlockSpec((lanes, taps * out_rows), lambda i: (i, 0)),
            pl.BlockSpec((lanes, taps * out_rows), lambda i: (i, 0)),
        ],
        out_shape=[
            jax.ShapeDtypeStruct((3, channels // chan, 9 * out_rows, 3 * chan), bf16),
            jax.ShapeDtypeStruct((channels, taps * out_rows), bf16),
            jax.ShapeDtypeStruct((channels, taps * out_rows), bf16),
        ],
        cost_estimate=cost(0, 5 * 4 * filters.size),
        name="prepare",
    )(filters)


def rims_kernel(*refs):
    blocks, (last, top) = refs[:-2], refs[-2:]
    at = 0
    for block in blocks:
        rows, depth, _ = block.shape
        planes = jnp.swapaxes(block[...], 0, 1)
        last[at : at + rows] = planes[depth - 1]
        top[at : at + rows] = planes[0]
        at += rows


def rims(blocks):
    rows = sum(b.shape[0] for b in blocks)
    shape = jax.ShapeDtypeStruct((rows, blocks[0].shape[2]), f32)
    return pl.pallas_call(
        rims_kernel,
        out_shape=[shape, shape],
        cost_estimate=cost(0, 4 * sum(b.size for b in blocks)),
        compiler_params=limit(),
        name="rims",
    )(*blocks)


def gathered(answer, out_rows):
    rows = []
    for b in range(3):
        row = None
        for c in range(3):
            at = (3 * b + c) * out_rows
            term = moved(answer[at : at + out_rows], 0, c - 1)
            row = term if row is None else row + term
        rows.append(moved(row, b - 1, 0))
    return rows[0] + rows[1] + rows[2]


def tripled(x):
    high, low = parts_of(x)
    return jnp.concatenate([high, high, low], axis=0)


def forward_kernel(counts, places, rim_places, first, ring, *refs):
    refs = list(refs)

    def take(n):
        taken = refs[:n]
        del refs[:n]
        return taken

    blocks = take(sum(counts))
    (source,) = take(1)
    rims_in = take(2) if rim_places else []
    total_in = None if first else take(3)[0]
    total_out, high_all, low_all, field, high_part, low_part, high_rim, low_rim = take(8)
    weights, rim_weights, sems, fetch_sems = refs
    fetches = [
        pltpu.make_async_copy(source.at[:, ring[place]], weights.at[k], fetch_sems.at[k])
        for k, place in enumerate(places)
    ]
    for k, place in enumerate(rim_places):
        for n in range(2):
            sem = fetch_sems.at[len(fetches)]
            fetches.append(
                pltpu.make_async_copy(source.at[2 * n, ring[place]], rim_weights.at[n, k], sem)
            )
    for fetch in fetches:
        fetch.start()
    depth, out_rows, area = total_out.shape
    chan = field.shape[2] // 3
    copies = []

    def keep(part, target, place, lanes):
        at = pl.ds(pl.multiple_of(ring[place] * chan, chan), chan)
        copies.append(pltpu.make_async_copy(part, target.at[at, lanes], sems.at[len(copies)]))
        copies[-1].start()

    begin = 0
    for k, pieces in enumerate(counts):
        loaded = [jnp.swapaxes(b[...], 0, 1) for b in blocks[begin : begin + pieces]]
        begin += pieces
        for plane in range(depth):
            rows = [b[plane] for b in loaded]
            x = rows[0] if pieces == 1 else jnp.concatenate(rows, axis=0)
            high, low = parts_of(x)
            field[k, plane, 0:chan] = high
            field[k, plane, chan : 2 * chan] = high
            field[k, plane, 2 * chan : 3 * chan] = low
            high_part[k, :, plane * area : (plane + 1) * area] = high
            low_part[k, :, plane * area : (plane + 1) * area] = low
        lanes = pl.ds(area, depth * area)
        keep(high_part.at[k], high_all, places[k], lanes)
        keep(low_part.at[k], low_all, places[k], lanes)
    for n, rim in enumerate(rims_in):
        lanes = pl.ds(n * (depth + 1) * area, area)
        for k in range(len(rim_places)):
            high, low = parts_of(beside(ring, n, rim[k * chan : (k + 1) * chan]))
            high_rim[n, k] = high
            low_rim[n, k] = low
            keep(high_rim.at[n, k], high_all, rim_places[k], lanes)
            keep(low_rim.at[n, k], low_all, rim_places[k], lanes)

    for fetch in fetches:
        fetch.wait()
    for plane in range(depth):
        terms = []
        for a in range(3):
            if 0 <= plane + a - 1 < depth:
                for k in range(len(counts)):
                    terms.append((weights[k, a], field[k, plane + a - 1]))
        for n, edge in enumerate((0, depth - 1)):
            if plane == edge:
                for k in range(len(rim_places)):
                    right = [high_rim[n, k], high_rim[n, k], low_rim[n, k]]
                    terms.append((rim_weights[n, k], jnp.concatenate(right, axis=0)))
        answer = None
        for left, right in terms:
            term = dot(left, right)
            answer = term if answer is None else answer + term
        total = gathered(answer, out_rows)
        if total_in is not None:
            total = total + total_in[plane]
        total_out[plane] = total
    for copy in copies:
        copy.wait()


def forward(ring, sets, places, rim_places, outer, weights, carry, sizes):
    depth, chan, area, channels, out_rows = sizes
    counts = tuple(len(s) for s in sets)
    blocks = [b for s in sets for b in s]
    first = carry is None
    lanes = (depth + 2) * area
    keep = pl.BlockSpec(memory_space=pltpu.HBM)
    in_specs = [whole(b.shape) for b in blocks]
    args = list(blocks)
    in_specs.append(keep)
    args.append(weights)
    if rim_places:
        in_specs += [whole(o.shape) for o in outer]
        args += list(outer)
    aliases = {}
    if not first:
        base = len(args) + 1
        in_specs += [whole((depth, out_rows, area)), keep, keep]
        args += list(carry)
        aliases = {base: 0, base + 1: 1, base + 2: 2}
    rims_held = max(1, len(rim_places))
    return pl.pallas_call(
        functools.partial(forward_kernel, counts, places, rim_places, first),
        grid_spec=pltpu.PrefetchScalarGridSpec(
            num_scalar_prefetch=1,
            grid=(1,),
            in_specs=in_specs,
            out_specs=[whole((depth, out_rows, area)), keep, keep],
            scratch_shapes=[
                pltpu.VMEM((len(sets), depth, 3 * chan, area), bf16),
                pltpu.VMEM((len(sets), chan, depth * area), bf16),
                pltpu.VMEM((len(sets), chan, depth * area), bf16),
                pltpu.VMEM((2, rims_held, chan, area), bf16),
                pltpu.VMEM((2, rims_held, chan, area), bf16),
                pltpu.VMEM((len(sets), 3) + weights.shape[2:], bf16),
                pltpu.VMEM((2, rims_held) + weights.shape[2:], bf16),
                pltpu.SemaphoreType.DMA((2 * len(sets) + 4 * rims_held,)),
                pltpu.SemaphoreType.DMA((len(sets) + 2 * rims_held,)),
            ],
        ),
        out_shape=[
            jax.ShapeDtypeStruct((depth, out_rows, area), f32),
            jax.ShapeDtypeStruct((channels, lanes), bf16),
            jax.ShapeDtypeStruct((channels, lanes), bf16),
        ],
        input_output_aliases=aliases,
        cost_estimate=cost(
            len(sets) * 2 * 81 * out_rows * chan * depth * area, len(sets) * 8 * chan * lanes
        ),
        compiler_params=limit(),
        name="forward",
    )(ring, *args)


def middle_kernel(chan, ring, total, grad, below, above, source, *refs):
    active_out, spread_out, high_all, low_all, high_rim, low_rim, weights, sems, fetch_sems = refs[2:]
    depth, out_rows, area = total.shape
    copies = []
    rim_sums = []
    opposite = ring[high_all.shape[0] // chan // 2]
    fetches = [
        pltpu.make_async_copy(source.at[2 * n, opposite], weights.at[n], fetch_sems.at[n])
        for n in range(2)
    ]
    for fetch in fetches:
        fetch.start()
    for n, rim in enumerate((below, above)):
        value = beside(ring, n, rim[...])
        high, low = parts_of(value)
        high_rim[n] = high
        low_rim[n] = low
        at = pl.ds(pl.multiple_of(opposite * chan, chan), chan)
        lanes = pl.ds(n * (depth + 1) * area, area)
        for m, (part, target) in enumerate(((high_rim, high_all), (low_rim, low_all))):
            copy = pltpu.make_async_copy(part.at[n], target.at[at, lanes], sems.at[n, m])
            copy.start()
            copies.append(copy)
        fetches[n].wait()
        rim_sums.append(gathered(dot(weights[n], tripled(value)), out_rows))
    positives = []
    for plane in range(depth):
        value = total[plane]
        if plane == 0:
            value = value + rim_sums[0]
        if plane == depth - 1:
            value = value + rim_sums[1]
        positives.append(jnp.maximum(value, 0.0))
    positives = jnp.stack(positives)
    active_out[...] = jnp.swapaxes(positives * positives, 0, 1)
    grads = jnp.swapaxes(grad[...], 0, 1)
    nothing = jnp.zeros((9 * out_rows, area), bf16)
    for part in range(2):
        spread_out[part, 0] = nothing
        spread_out[part, depth + 1] = nothing
    for plane in range(depth):
        pre_grad = 2.0 * positives[plane] * grads[plane]
        for c in range(3):
            across = moved(pre_grad, 0, 1 - c)
            for b in range(3):
                high, low = parts_of(moved(across, 1 - b, 0))
                at = (3 * b + c) * out_rows
                spread_out[0, plane + 1, at : at + out_rows] = high
                spread_out[1, plane + 1, at : at + out_rows] = low
    for copy in copies:
        copy.wait()


def middle(ring, carry, grad, outer, weights, chan):
    total, high_all, low_all = carry
    depth, out_rows, area = total.shape
    keep = pl.BlockSpec(memory_space=pltpu.HBM)
    return pl.pallas_call(
        functools.partial(middle_kernel, chan),
        grid_spec=pltpu.PrefetchScalarGridSpec(
            num_scalar_prefetch=1,
            grid=(1,),
            in_specs=[whole(x.shape) for x in (total, grad, *outer)]
            + [keep, keep, keep],
            out_specs=[
                whole((out_rows, depth, area)),
                whole((2, depth + 2, 9 * out_rows, area)),
                keep,
                keep,
            ],
            scratch_shapes=[
                pltpu.VMEM((2, chan, area), bf16),
                pltpu.VMEM((2, chan, area), bf16),
                pltpu.VMEM((2,) + weights.shape[2:], bf16),
                pltpu.SemaphoreType.DMA((2, 2)),
                pltpu.SemaphoreType.DMA((2,)),
            ],
        ),
        out_shape=[
            jax.ShapeDtypeStruct((out_rows, depth, area), f32),
            jax.ShapeDtypeStruct((2, depth + 2, 9 * out_rows, area), bf16),
            jax.ShapeDtypeStruct(high_all.shape, bf16),
            jax.ShapeDtypeStruct(low_all.shape, bf16),
        ],
        input_output_aliases={6: 2, 7: 3},
        cost_estimate=cost(0, 4 * 18 * out_rows * depth * area),
        compiler_params=limit(),
        name="middle",
    )(ring, total, grad, *outer, weights, high_all, low_all)


def inner_kernel(begin, planes, spread, high, low, out):
    deep = high.shape[1]
    count, chan, _ = out.shape
    area = spread.shape[3]
    for plane in range(begin, begin + planes):
        near = spread[0, plane : plane + 3].reshape(deep, area)
        far = spread[1, plane : plane + 3].reshape(deep, area)
        value = dot(high[...], near) + dot(high[...], far) + dot(low[...], near)
        lanes = slice((plane - begin) * area, (plane - begin + 1) * area)
        out[:, :, lanes] = value.reshape(count, chan, area)


def outer_kernel(spread, high, low, below, above):
    depth = spread.shape[1] - 2
    third = high.shape[1] // 3
    for out, plane, at in ((below, 1, 2 * third), (above, depth, 0)):
        lanes = slice(at, at + third)
        value = dot(high[:, lanes], spread[0, plane]) + dot(high[:, lanes], spread[1, plane])
        value = value + dot(low[:, lanes], spread[0, plane])
        out[...] = value.reshape(out.shape)


def inner_terms(begin, planes, spread, high, low, chan):
    channels, deep = high.shape
    area = spread.shape[3]
    return pl.pallas_call(
        functools.partial(inner_kernel, begin, planes),
        out_shape=jax.ShapeDtypeStruct((channels // chan, chan, planes * area), f32),
        cost_estimate=cost(6 * channels * deep * planes * area, 2 * spread.size + 4 * high.size),
        compiler_params=limit(),
        name="inner_terms",
    )(spread, high, low)


def outer_terms(spread, high, low, chan):
    channels, deep = high.shape
    shape = jax.ShapeDtypeStruct((channels // chan, chan, spread.shape[3]), f32)
    return pl.pallas_call(
        outer_kernel,
        out_shape=[shape, shape],
        cost_estimate=cost(4 * channels * deep * spread.shape[3], spread.size),
        compiler_params=limit(),
        name="outer_terms",
    )(spread, high, low)


def filter_kernel(tap, ring, spread, high, low, keep_out, send_out, total):
    depth = spread.shape[1] - 2
    rows, area = spread.shape[2:]
    half = rows // 2
    channels = high.shape[0]
    step = min(256, channels)
    for at in range(0, channels, step):
        value = None
        for plane in range(depth):
            lanes = slice((tap + plane) * area, (tap + plane + 1) * area)
            right = high[at : at + step, lanes]
            term = dot_t(spread[0, plane + 1], right) + dot_t(spread[1, plane + 1], right)
            term = term + dot_t(spread[0, plane + 1], low[at : at + step, lanes])
            value = term if value is None else value + term
        total[:, at : at + step] = value
    side = ring[ring.shape[0] - 1]
    mine = pl.multiple_of(side * half, half)
    other = pl.multiple_of((1 - side) * half, half)
    keep_out[...] = total[pl.ds(mine, half), :]
    send_out[...] = total[pl.ds(other, half), :]


def filter_terms(tap, ring, spread, high, low):
    rows = spread.shape[2]
    channels = high.shape[0]
    return pl.pallas_call(
        functools.partial(filter_kernel, tap),
        grid_spec=pltpu.PrefetchScalarGridSpec(
            num_scalar_prefetch=1,
            grid=(1,),
            in_specs=[whole(spread.shape), whole(high.shape), whole(low.shape)],
            out_specs=[whole((rows // 2, channels))] * 2,
            scratch_shapes=[pltpu.VMEM((rows, channels), f32)],
        ),
        out_shape=[jax.ShapeDtypeStruct((rows // 2, channels), f32)] * 2,
        cost_estimate=cost(6 * rows * high.size, 4 * high.size + 2 * spread.size),
        compiler_params=limit(),
        name="filter_terms",
    )(ring, spread, high, low)


def place_kernel(scale, ring, *refs):
    mine, other, out = refs[0], refs[1], refs[-1]
    half = mine.shape[0]
    side = ring[ring.shape[0] - 1]
    out[0, pl.ds(pl.multiple_of(side * half, half), half), :] = mine[...] / scale
    out[0, pl.ds(pl.multiple_of((1 - side) * half, half), half), :] = other[...] / scale


def place(tap, ring, mine, other, carry, scale):
    half, channels = mine.shape
    args = [mine, other]
    in_specs = [whole(mine.shape)] * 2
    aliases = {}
    if carry is not None:
        args.append(carry)
        in_specs.append(pl.BlockSpec(memory_space=pl.ANY))
        aliases = {3: 0}
    return pl.pallas_call(
        functools.partial(place_kernel, scale),
        grid_spec=pltpu.PrefetchScalarGridSpec(
            num_scalar_prefetch=1,
            grid=(1,),
            in_specs=in_specs,
            out_specs=pl.BlockSpec((1, 2 * half, channels), lambda i, s: (tap, 0, 0)),
        ),
        out_shape=jax.ShapeDtypeStruct((3, 2 * half, channels), f32),
        input_output_aliases=aliases,
        cost_estimate=cost(0, 16 * half * channels),
        compiler_params=limit(),
        name="place",
    )(ring, *args)


def local_sum(ring, inner, rim, first):
    value, rim = inner[0], beside(ring, 0 if first else 1, rim[0])
    area = rim.shape[1]
    width = value.shape[1]
    if first:
        return jnp.concatenate([value[:, :area] + rim, value[:, area:]], axis=1)
    return jnp.concatenate([value[:, : width - area], value[:, width - area :] + rim], axis=1)


def opening_kernel(first, ring, inner, rim, up_out, down_out):
    value = local_sum(ring, inner, rim, first)
    half = value.shape[0] // 2
    up_out[...] = value[:half]
    down_out[...] = value[half:]


def running_kernel(first, ring, up_inner, up_rim, down_inner, down_rim, up, down, up_out, down_out):
    value = local_sum(ring, up_inner, up_rim, first)
    size = up.shape[0]
    up_out[0:size] = value[0:size] + up[...]
    if size < value.shape[0]:
        up_out[size:] = value[size:]
    value = local_sum(ring, down_inner, down_rim, first)
    rest = value.shape[0] - size
    down_out[rest:] = value[rest:] + down[...]
    if rest:
        down_out[0:rest] = value[0:rest]


def closing_kernel(ring, *refs):
    chains, out = (refs[0:4], refs[4:8]), refs[8]
    area = out.shape[2]
    values = []
    for first, (inner, rim, up, down) in zip((True, False), chains):
        value = local_sum(ring, inner, rim, first) + up[...] + down[...]
        values += [value[:, at : at + area] for at in range(0, value.shape[1], area)]
    out[...] = jnp.swapaxes(jnp.stack(values), 0, 1)


def summed(kernel, ring, pieces, outs):
    specs, args = [], []
    for piece in pieces:
        if isinstance(piece, tuple):
            array, k = piece
            specs.append(pl.BlockSpec((1,) + array.shape[1:], lambda i, s, k=k: (s[k], 0, 0)))
            args.append(array)
        else:
            specs.append(whole(piece.shape))
            args.append(piece)
    return pl.pallas_call(
        kernel,
        grid_spec=pltpu.PrefetchScalarGridSpec(
            num_scalar_prefetch=1,
            grid=(1,),
            in_specs=specs,
            out_specs=[whole(o) for o in outs],
        ),
        out_shape=[jax.ShapeDtypeStruct(o, f32) for o in outs],
        cost_estimate=cost(0, sum(12 * math.prod(o) for o in outs)),
        compiler_params=limit(),
    )(ring, *args)


def shards(volume, filters, out_grad):
    chan, depth, area = volume.shape
    out_rows = filters.shape[1]
    channels = filters.shape[2]
    count = lax.axis_size("filt")
    slabs = lax.axis_size("slab")
    sizes = (depth, chan, area, channels, out_rows)

    order = list(range(0, count, 2)) + list(range(1, count, 2))[::-1]
    ring_up = [(order[i], order[(i + 1) % count]) for i in range(count)]
    ring_down = [(b, a) for a, b in ring_up]
    rows = [
        [order[(order.index(f) + k) % count] for k in range(count)]
        + [int(s > 0), int(s < slabs - 1), s % 2]
        for s in range(slabs)
        for f in range(count)
    ]
    here = lax.axis_index("slab") * count + lax.axis_index("filt")
    ring = lax.dynamic_index_in_dim(jnp.array(rows, jnp.int32), here, 0, keepdims=False)

    def send(x, pairs):
        return lax.ppermute(x, "filt", pairs)

    deeper = [(i, (i + 1) % slabs) for i in range(slabs)]
    shallower = [(b, a) for a, b in deeper]
    half = count // 2

    ahead, back_high, back_low = prepare(filters, chan)
    ahead = pltpu.with_memory_space_constraint(ahead, pltpu.HBM)

    carry = None
    up = down = volume
    rim_places, outer = (), None
    for step in range(half + 1):
        if step == 0:
            sets, places = [[volume]], (0,)
        elif step < half:
            up, down = send(up, ring_up), send(down, ring_down)
            sets, places = [[up], [down]], (count - step, step)
        else:
            up = send(up[: chan // 2], ring_up)
            down = send(down[chan // 2 :], ring_down)
            sets, places = [[up, down]], (half,)
        last, top = rims([b for blocks in sets for b in blocks])
        carry = forward(ring, sets, places, rim_places, outer, ahead, carry, sizes)
        outer = lax.ppermute(last, "slab", deeper), lax.ppermute(top, "slab", shallower)
        rim_places = places

    activated, spread, high_field, low_field = middle(ring, carry, out_grad, outer, ahead, chan)

    below, above = outer_terms(spread, back_high, back_low, chan)
    from_above = lax.ppermute(below, "slab", shallower)
    from_below = lax.ppermute(above, "slab", deeper)
    run = depth // 2
    inner = []
    for c in range(2):
        inner.append(inner_terms(c * run, run, spread, back_high, back_low, chan))
    edge = [from_below, from_above]

    scale = math.sqrt(depth * slabs * area)

    def swap(x, bit):
        return lax.ppermute(x, "slab", [(i, i ^ bit) for i in range(slabs)])

    weight_grad = None
    for tap in range(3):
        keep, give = filter_terms(tap, ring, spread, high_field, low_field)
        keep = keep + swap(give, 1)
        bit = 2
        while bit < slabs:
            keep = keep + swap(keep, bit)
            bit *= 2
        other = swap(keep, 1)
        weight_grad = place(tap, ring, keep, other, weight_grad, scale)

    piece = (chan, run * area)
    part = (chan // 2, run * area)
    flows = []
    for c in range(2):
        kernel = functools.partial(opening_kernel, c == 0)
        flows.append(summed(kernel, ring, [(inner[c], half), (edge[c], half)], [part, part]))
    for step in range(half - 1, 0, -1):
        for c in range(2):
            up, down = flows[c]
            up, down = send(up, ring_up), send(down, ring_down)
            kernel = functools.partial(running_kernel, c == 0)
            pieces = [(x, p) for p in (step, count - step) for x in (inner[c], edge[c])]
            flows[c] = summed(kernel, ring, pieces + [up, down], [piece, piece])
    pieces = []
    for c in range(2):
        up, down = flows[c]
        pieces += [(inner[c], 0), (edge[c], 0), send(up, ring_up), send(down, ring_down)]
    (input_grad,) = summed(closing_kernel, ring, pieces, [(chan, depth, area)])
    return activated, input_grad, weight_grad.reshape(filters.shape)


def solution(mesh):
    placed = (P("filt", "slab", None), P(None, "filt", None), P("filt", "slab", None))

    def step(*args):
        return shards(*args)

    step = jax.shard_map(
        step,
        mesh=mesh,
        in_specs=placed,
        out_specs=(P("filt", "slab", None), P("filt", "slab", None), P(None, "filt", None)),
        check_vma=False,
    )
    return step
```

```python
import functools
import math

import jax
import jax.numpy as jnp
from jax import lax
from jax.experimental import pallas as pl
from jax.experimental.pallas import tpu as pltpu
from jax.sharding import PartitionSpec as P


WIDTH = 16


f32 = jnp.float32
bf16 = jnp.bfloat16


def parts_of(x):
    high = x.astype(bf16)
    low = (x - high.astype(f32)).astype(bf16)
    return high, low


def dot(a, b):
    return lax.dot_general(a, b, (((1,), (0,)), ((), ())), preferred_element_type=f32)


def dot_t(a, b):
    return lax.dot_general(a, b, (((1,), (1,)), ((), ())), preferred_element_type=f32)


def beside(ring, n, rim):
    return jnp.where(ring[ring.shape[0] - 3 + n] > 0, rim, 0.0)


def whole(shape):
    return pl.BlockSpec(shape, lambda *_: (0,) * len(shape))


def limit():
    return pltpu.CompilerParams(vmem_limit_bytes=28 * 2**20)


def cost(flops, moved):
    return pl.CostEstimate(flops=int(flops), bytes_accessed=int(moved), transcendentals=0)


def moved(x, down, across):
    size = x.shape[-1]
    place = lax.broadcasted_iota(jnp.int32, x.shape, 1)
    if across:
        column = place % WIDTH + across
        rolled = pltpu.roll(x, (-across) % size, 1)
        x = jnp.where((column >= 0) & (column < WIDTH), rolled, 0.0)
    if down:
        target = place + down * WIDTH
        rolled = pltpu.roll(x, (-down * WIDTH) % size, 1)
        x = jnp.where((target >= 0) & (target < size), rolled, 0.0)
    return x


def prepare_kernel(chan, filters, ahead, back_high, back_low):
    taps, out_rows, lanes = filters.shape
    third = taps * out_rows // 3
    for a in range(3):
        x = filters[a * 9 : (a + 1) * 9].reshape(third, lanes)
        high, low = parts_of(x)
        for k in range(lanes // chan):
            at = slice(k * chan, (k + 1) * chan)
            ahead[a, k] = jnp.concatenate([high[:, at], low[:, at], high[:, at]], axis=1)
    turned = [filters[a * 9 : (a + 1) * 9].reshape(third, lanes).T for a in (2, 1, 0)]
    high, low = parts_of(jnp.concatenate(turned, axis=1))
    back_high[...] = high
    back_low[...] = low


def prepare(filters, chan):
    taps, out_rows, channels = filters.shape
    lanes = min(128, channels)
    each = lanes // chan
    return pl.pallas_call(
        functools.partial(prepare_kernel, chan),
        grid=(channels // lanes,),
        in_specs=[pl.BlockSpec((taps, out_rows, lanes), lambda i: (0, 0, i))],
        out_specs=[
            pl.BlockSpec((3, each, 9 * out_rows, 3 * chan), lambda i: (0, i, 0, 0)),
            pl.BlockSpec((lanes, taps * out_rows), lambda i: (i, 0)),
            pl.BlockSpec((lanes, taps * out_rows), lambda i: (i, 0)),
        ],
        out_shape=[
            jax.ShapeDtypeStruct((3, channels // chan, 9 * out_rows, 3 * chan), bf16),
            jax.ShapeDtypeStruct((channels, taps * out_rows), bf16),
            jax.ShapeDtypeStruct((channels, taps * out_rows), bf16),
        ],
        cost_estimate=cost(0, 5 * 4 * filters.size),
        name="prepare",
    )(filters)


def rims_kernel(*refs):
    blocks, (last, top) = refs[:-2], refs[-2:]
    at = 0
    for block in blocks:
        rows, depth, _ = block.shape
        planes = jnp.swapaxes(block[...], 0, 1)
        last[at : at + rows] = planes[depth - 1]
        top[at : at + rows] = planes[0]
        at += rows


def rims(blocks):
    rows = sum(b.shape[0] for b in blocks)
    shape = jax.ShapeDtypeStruct((rows, blocks[0].shape[2]), f32)
    return pl.pallas_call(
        rims_kernel,
        out_shape=[shape, shape],
        cost_estimate=cost(0, 4 * sum(b.size for b in blocks)),
        compiler_params=limit(),
        name="rims",
    )(*blocks)


def gathered(answer, out_rows):
    rows = []
    for b in range(3):
        row = None
        for c in range(3):
            at = (3 * b + c) * out_rows
            term = moved(answer[at : at + out_rows], 0, c - 1)
            row = term if row is None else row + term
        rows.append(moved(row, b - 1, 0))
    return rows[0] + rows[1] + rows[2]


def tripled(x):
    high, low = parts_of(x)
    return jnp.concatenate([high, high, low], axis=0)


def forward_kernel(counts, places, rim_places, first, ring, *refs):
    refs = list(refs)

    def take(n):
        taken = refs[:n]
        del refs[:n]
        return taken

    blocks = take(sum(counts))
    (source,) = take(1)
    rims_in = take(2) if rim_places else []
    total_in = None if first else take(3)[0]
    total_out, high_all, low_all, field, high_part, low_part, high_rim, low_rim = take(8)
    weights, rim_weights, sems, fetch_sems = refs
    fetches = [
        pltpu.make_async_copy(source.at[:, ring[place]], weights.at[k], fetch_sems.at[k])
        for k, place in enumerate(places)
    ]
    for k, place in enumerate(rim_places):
        for n in range(2):
            sem = fetch_sems.at[len(fetches)]
            fetches.append(
                pltpu.make_async_copy(source.at[2 * n, ring[place]], rim_weights.at[n, k], sem)
            )
    for fetch in fetches:
        fetch.start()
    depth, out_rows, area = total_out.shape
    chan = field.shape[2] // 3
    copies = []

    def keep(part, target, place, lanes):
        at = pl.ds(pl.multiple_of(ring[place] * chan, chan), chan)
        copies.append(pltpu.make_async_copy(part, target.at[at, lanes], sems.at[len(copies)]))
        copies[-1].start()

    begin = 0
    for k, pieces in enumerate(counts):
        loaded = [jnp.swapaxes(b[...], 0, 1) for b in blocks[begin : begin + pieces]]
        begin += pieces
        for plane in range(depth):
            rows = [b[plane] for b in loaded]
            x = rows[0] if pieces == 1 else jnp.concatenate(rows, axis=0)
            high, low = parts_of(x)
            field[k, plane, 0:chan] = high
            field[k, plane, chan : 2 * chan] = high
            field[k, plane, 2 * chan : 3 * chan] = low
            high_part[k, :, plane * area : (plane + 1) * area] = high
            low_part[k, :, plane * area : (plane + 1) * area] = low
        lanes = pl.ds(area, depth * area)
        keep(high_part.at[k], high_all, places[k], lanes)
        keep(low_part.at[k], low_all, places[k], lanes)
    for n, rim in enumerate(rims_in):
        lanes = pl.ds(n * (depth + 1) * area, area)
        for k in range(len(rim_places)):
            high, low = parts_of(beside(ring, n, rim[k * chan : (k + 1) * chan]))
            high_rim[n, k] = high
            low_rim[n, k] = low
            keep(high_rim.at[n, k], high_all, rim_places[k], lanes)
            keep(low_rim.at[n, k], low_all, rim_places[k], lanes)

    for fetch in fetches:
        fetch.wait()
    for plane in range(depth):
        terms = []
        for a in range(3):
            if 0 <= plane + a - 1 < depth:
                for k in range(len(counts)):
                    terms.append((weights[k, a], field[k, plane + a - 1]))
        for n, edge in enumerate((0, depth - 1)):
            if plane == edge:
                for k in range(len(rim_places)):
                    right = [high_rim[n, k], high_rim[n, k], low_rim[n, k]]
                    terms.append((rim_weights[n, k], jnp.concatenate(right, axis=0)))
        answer = None
        for left, right in terms:
            term = dot(left, right)
            answer = term if answer is None else answer + term
        total = gathered(answer, out_rows)
        if total_in is not None:
            total = total + total_in[plane]
        total_out[plane] = total
    for copy in copies:
        copy.wait()


def forward(ring, sets, places, rim_places, outer, weights, carry, sizes):
    depth, chan, area, channels, out_rows = sizes
    counts = tuple(len(s) for s in sets)
    blocks = [b for s in sets for b in s]
    first = carry is None
    lanes = (depth + 2) * area
    keep = pl.BlockSpec(memory_space=pltpu.HBM)
    in_specs = [whole(b.shape) for b in blocks]
    args = list(blocks)
    in_specs.append(keep)
    args.append(weights)
    if rim_places:
        in_specs += [whole(o.shape) for o in outer]
        args += list(outer)
    aliases = {}
    if not first:
        base = len(args) + 1
        in_specs += [whole((depth, out_rows, area)), keep, keep]
        args += list(carry)
        aliases = {base: 0, base + 1: 1, base + 2: 2}
    rims_held = max(1, len(rim_places))
    return pl.pallas_call(
        functools.partial(forward_kernel, counts, places, rim_places, first),
        grid_spec=pltpu.PrefetchScalarGridSpec(
            num_scalar_prefetch=1,
            grid=(1,),
            in_specs=in_specs,
            out_specs=[whole((depth, out_rows, area)), keep, keep],
            scratch_shapes=[
                pltpu.VMEM((len(sets), depth, 3 * chan, area), bf16),
                pltpu.VMEM((len(sets), chan, depth * area), bf16),
                pltpu.VMEM((len(sets), chan, depth * area), bf16),
                pltpu.VMEM((2, rims_held, chan, area), bf16),
                pltpu.VMEM((2, rims_held, chan, area), bf16),
                pltpu.VMEM((len(sets), 3) + weights.shape[2:], bf16),
                pltpu.VMEM((2, rims_held) + weights.shape[2:], bf16),
                pltpu.SemaphoreType.DMA((2 * len(sets) + 4 * rims_held,)),
                pltpu.SemaphoreType.DMA((len(sets) + 2 * rims_held,)),
            ],
        ),
        out_shape=[
            jax.ShapeDtypeStruct((depth, out_rows, area), f32),
            jax.ShapeDtypeStruct((channels, lanes), bf16),
            jax.ShapeDtypeStruct((channels, lanes), bf16),
        ],
        input_output_aliases=aliases,
        cost_estimate=cost(
            len(sets) * 2 * 81 * out_rows * chan * depth * area, len(sets) * 8 * chan * lanes
        ),
        compiler_params=limit(),
        name="forward",
    )(ring, *args)


def middle_kernel(chan, ring, total, grad, below, above, source, *refs):
    active_out, spread_out, high_all, low_all, high_rim, low_rim, weights, sems, fetch_sems = refs[2:]
    depth, out_rows, area = total.shape
    copies = []
    rim_sums = []
    opposite = ring[high_all.shape[0] // chan // 2]
    fetches = [
        pltpu.make_async_copy(source.at[2 * n, opposite], weights.at[n], fetch_sems.at[n])
        for n in range(2)
    ]
    for fetch in fetches:
        fetch.start()
    for n, rim in enumerate((below, above)):
        value = beside(ring, n, rim[...])
        high, low = parts_of(value)
        high_rim[n] = high
        low_rim[n] = low
        at = pl.ds(pl.multiple_of(opposite * chan, chan), chan)
        lanes = pl.ds(n * (depth + 1) * area, area)
        for m, (part, target) in enumerate(((high_rim, high_all), (low_rim, low_all))):
            copy = pltpu.make_async_copy(part.at[n], target.at[at, lanes], sems.at[n, m])
            copy.start()
            copies.append(copy)
        fetches[n].wait()
        rim_sums.append(gathered(dot(weights[n], tripled(value)), out_rows))
    positives = []
    for plane in range(depth):
        value = total[plane]
        if plane == 0:
            value = value + rim_sums[0]
        if plane == depth - 1:
            value = value + rim_sums[1]
        positives.append(jnp.maximum(value, 0.0))
    positives = jnp.stack(positives)
    active_out[...] = jnp.swapaxes(positives * positives, 0, 1)
    grads = jnp.swapaxes(grad[...], 0, 1)
    nothing = jnp.zeros((9 * out_rows, area), bf16)
    for part in range(2):
        spread_out[part, 0] = nothing
        spread_out[part, depth + 1] = nothing
    for plane in range(depth):
        pre_grad = 2.0 * positives[plane] * grads[plane]
        for c in range(3):
            across = moved(pre_grad, 0, 1 - c)
            for b in range(3):
                high, low = parts_of(moved(across, 1 - b, 0))
                at = (3 * b + c) * out_rows
                spread_out[0, plane + 1, at : at + out_rows] = high
                spread_out[1, plane + 1, at : at + out_rows] = low
    for copy in copies:
        copy.wait()


def middle(ring, carry, grad, outer, weights, chan):
    total, high_all, low_all = carry
    depth, out_rows, area = total.shape
    keep = pl.BlockSpec(memory_space=pltpu.HBM)
    return pl.pallas_call(
        functools.partial(middle_kernel, chan),
        grid_spec=pltpu.PrefetchScalarGridSpec(
            num_scalar_prefetch=1,
            grid=(1,),
            in_specs=[whole(x.shape) for x in (total, grad, *outer)]
            + [keep, keep, keep],
            out_specs=[
                whole((out_rows, depth, area)),
                whole((2, depth + 2, 9 * out_rows, area)),
                keep,
                keep,
            ],
            scratch_shapes=[
                pltpu.VMEM((2, chan, area), bf16),
                pltpu.VMEM((2, chan, area), bf16),
                pltpu.VMEM((2,) + weights.shape[2:], bf16),
                pltpu.SemaphoreType.DMA((2, 2)),
                pltpu.SemaphoreType.DMA((2,)),
            ],
        ),
        out_shape=[
            jax.ShapeDtypeStruct((out_rows, depth, area), f32),
            jax.ShapeDtypeStruct((2, depth + 2, 9 * out_rows, area), bf16),
            jax.ShapeDtypeStruct(high_all.shape, bf16),
            jax.ShapeDtypeStruct(low_all.shape, bf16),
        ],
        input_output_aliases={6: 2, 7: 3},
        cost_estimate=cost(0, 4 * 18 * out_rows * depth * area),
        compiler_params=limit(),
        name="middle",
    )(ring, total, grad, *outer, weights, high_all, low_all)


def inner_kernel(begin, planes, spread, high, low, out):
    deep = high.shape[1]
    count, chan, _ = out.shape
    area = spread.shape[3]
    group = 2 - planes % 2

    def some(i, nothing):
        for j in range(group):
            near = spread[0, pl.ds(begin + i * group + j, 3)].reshape(deep, area)
            far = spread[1, pl.ds(begin + i * group + j, 3)].reshape(deep, area)
            value = dot(high[...], near) + dot(high[...], far) + dot(low[...], near)
            lanes = pl.ds(pl.multiple_of((i * group + j) * area, area), area)
            out[:, :, lanes] = value.reshape(count, chan, area)
        return nothing

    lax.fori_loop(0, planes // group, some, 0)


def outer_kernel(spread, high, low, below, above):
    depth = spread.shape[1] - 2
    third = high.shape[1] // 3
    for out, plane, at in ((below, 1, 2 * third), (above, depth, 0)):
        lanes = slice(at, at + third)
        value = dot(high[:, lanes], spread[0, plane]) + dot(high[:, lanes], spread[1, plane])
        value = value + dot(low[:, lanes], spread[0, plane])
        out[...] = value.reshape(out.shape)


def inner_terms(begin, planes, spread, high, low, chan):
    channels, deep = high.shape
    area = spread.shape[3]
    return pl.pallas_call(
        functools.partial(inner_kernel, begin, planes),
        out_shape=jax.ShapeDtypeStruct((channels // chan, chan, planes * area), f32),
        cost_estimate=cost(6 * channels * deep * planes * area, 2 * spread.size + 4 * high.size),
        compiler_params=limit(),
        name="inner_terms",
    )(spread, high, low)


def outer_terms(spread, high, low, chan):
    channels, deep = high.shape
    shape = jax.ShapeDtypeStruct((channels // chan, chan, spread.shape[3]), f32)
    return pl.pallas_call(
        outer_kernel,
        out_shape=[shape, shape],
        cost_estimate=cost(4 * channels * deep * spread.shape[3], spread.size),
        compiler_params=limit(),
        name="outer_terms",
    )(spread, high, low)


def filter_kernel(tap, ring, spread, high, low, keep_out, send_out, total):
    depth = spread.shape[1] - 2
    rows, area = spread.shape[2:]
    half = rows // 2
    channels = high.shape[0]
    step = min(256, channels)
    for at in range(0, channels, step):
        value = None
        for plane in range(depth):
            lanes = slice((tap + plane) * area, (tap + plane + 1) * area)
            right = high[at : at + step, lanes]
            term = dot_t(spread[0, plane + 1], right) + dot_t(spread[1, plane + 1], right)
            term = term + dot_t(spread[0, plane + 1], low[at : at + step, lanes])
            value = term if value is None else value + term
        total[:, at : at + step] = value
    side = ring[ring.shape[0] - 1]
    mine = pl.multiple_of(side * half, half)
    other = pl.multiple_of((1 - side) * half, half)
    keep_out[...] = total[pl.ds(mine, half), :]
    send_out[...] = total[pl.ds(other, half), :]


def filter_terms(tap, ring, spread, high, low):
    rows = spread.shape[2]
    channels = high.shape[0]
    return pl.pallas_call(
        functools.partial(filter_kernel, tap),
        grid_spec=pltpu.PrefetchScalarGridSpec(
            num_scalar_prefetch=1,
            grid=(1,),
            in_specs=[whole(spread.shape), whole(high.shape), whole(low.shape)],
            out_specs=[whole((rows // 2, channels))] * 2,
            scratch_shapes=[pltpu.VMEM((rows, channels), f32)],
        ),
        out_shape=[jax.ShapeDtypeStruct((rows // 2, channels), f32)] * 2,
        cost_estimate=cost(6 * rows * high.size, 4 * high.size + 2 * spread.size),
        compiler_params=limit(),
        name="filter_terms",
    )(ring, spread, high, low)


def place_kernel(scale, ring, *refs):
    mine, other, out = refs[0], refs[1], refs[-1]
    half = mine.shape[0]
    side = ring[ring.shape[0] - 1]
    out[0, pl.ds(pl.multiple_of(side * half, half), half), :] = mine[...] / scale
    out[0, pl.ds(pl.multiple_of((1 - side) * half, half), half), :] = other[...] / scale


def place(tap, ring, mine, other, carry, scale):
    half, channels = mine.shape
    args = [mine, other]
    in_specs = [whole(mine.shape)] * 2
    aliases = {}
    if carry is not None:
        args.append(carry)
        in_specs.append(pl.BlockSpec(memory_space=pl.ANY))
        aliases = {3: 0}
    return pl.pallas_call(
        functools.partial(place_kernel, scale),
        grid_spec=pltpu.PrefetchScalarGridSpec(
            num_scalar_prefetch=1,
            grid=(1,),
            in_specs=in_specs,
            out_specs=pl.BlockSpec((1, 2 * half, channels), lambda i, s: (tap, 0, 0)),
        ),
        out_shape=jax.ShapeDtypeStruct((3, 2 * half, channels), f32),
        input_output_aliases=aliases,
        cost_estimate=cost(0, 16 * half * channels),
        compiler_params=limit(),
        name="place",
    )(ring, *args)


def local_sum(ring, inner, rim, first):
    value, rim = inner[0], beside(ring, 0 if first else 1, rim[0])
    area = rim.shape[1]
    width = value.shape[1]
    if first:
        return jnp.concatenate([value[:, :area] + rim, value[:, area:]], axis=1)
    return jnp.concatenate([value[:, : width - area], value[:, width - area :] + rim], axis=1)


def opening_kernel(first, ring, inner, rim, up_out, down_out):
    value = local_sum(ring, inner, rim, first)
    half = value.shape[0] // 2
    up_out[...] = value[:half]
    down_out[...] = value[half:]


def running_kernel(first, ring, up_inner, up_rim, down_inner, down_rim, up, down, up_out, down_out):
    value = local_sum(ring, up_inner, up_rim, first)
    size = up.shape[0]
    up_out[0:size] = value[0:size] + up[...]
    if size < value.shape[0]:
        up_out[size:] = value[size:]
    value = local_sum(ring, down_inner, down_rim, first)
    rest = value.shape[0] - size
    down_out[rest:] = value[rest:] + down[...]
    if rest:
        down_out[0:rest] = value[0:rest]


def closing_kernel(ring, *refs):
    chains, out = (refs[0:4], refs[4:8]), refs[8]
    area = out.shape[2]
    values = []
    for first, (inner, rim, up, down) in zip((True, False), chains):
        value = local_sum(ring, inner, rim, first) + up[...] + down[...]
        values += [value[:, at : at + area] for at in range(0, value.shape[1], area)]
    out[...] = jnp.swapaxes(jnp.stack(values), 0, 1)


def summed(kernel, ring, pieces, outs):
    specs, args = [], []
    for piece in pieces:
        if isinstance(piece, tuple):
            array, k = piece
            specs.append(pl.BlockSpec((1,) + array.shape[1:], lambda i, s, k=k: (s[k], 0, 0)))
            args.append(array)
        else:
            specs.append(whole(piece.shape))
            args.append(piece)
    return pl.pallas_call(
        kernel,
        grid_spec=pltpu.PrefetchScalarGridSpec(
            num_scalar_prefetch=1,
            grid=(1,),
            in_specs=specs,
            out_specs=[whole(o) for o in outs],
        ),
        out_shape=[jax.ShapeDtypeStruct(o, f32) for o in outs],
        cost_estimate=cost(0, sum(12 * math.prod(o) for o in outs)),
        compiler_params=limit(),
    )(ring, *args)


def shards(volume, filters, out_grad):
    chan, depth, area = volume.shape
    out_rows = filters.shape[1]
    channels = filters.shape[2]
    count = lax.axis_size("filt")
    slabs = lax.axis_size("slab")
    sizes = (depth, chan, area, channels, out_rows)

    order = list(range(0, count, 2)) + list(range(1, count, 2))[::-1]
    ring_up = [(order[i], order[(i + 1) % count]) for i in range(count)]
    ring_down = [(b, a) for a, b in ring_up]
    rows = [
        [order[(order.index(f) + k) % count] for k in range(count)]
        + [int(s > 0), int(s < slabs - 1), s % 2]
        for s in range(slabs)
        for f in range(count)
    ]
    here = lax.axis_index("slab") * count + lax.axis_index("filt")
    ring = lax.dynamic_index_in_dim(jnp.array(rows, jnp.int32), here, 0, keepdims=False)

    def send(x, pairs):
        return lax.ppermute(x, "filt", pairs)

    deeper = [(i, (i + 1) % slabs) for i in range(slabs)]
    shallower = [(b, a) for a, b in deeper]
    half = count // 2

    ahead, back_high, back_low = prepare(filters, chan)
    ahead = pltpu.with_memory_space_constraint(ahead, pltpu.HBM)

    carry = None
    up = down = volume
    rim_places, outer = (), None
    for step in range(half + 1):
        if step == 0:
            sets, places = [[volume]], (0,)
        elif step < half:
            up, down = send(up, ring_up), send(down, ring_down)
            sets, places = [[up], [down]], (count - step, step)
        else:
            up = send(up[: chan // 2], ring_up)
            down = send(down[chan // 2 :], ring_down)
            sets, places = [[up, down]], (half,)
        last, top = rims([b for blocks in sets for b in blocks])
        carry = forward(ring, sets, places, rim_places, outer, ahead, carry, sizes)
        outer = lax.ppermute(last, "slab", deeper), lax.ppermute(top, "slab", shallower)
        rim_places = places

    activated, spread, high_field, low_field = middle(ring, carry, out_grad, outer, ahead, chan)

    below, above = outer_terms(spread, back_high, back_low, chan)
    from_above = lax.ppermute(below, "slab", shallower)
    from_below = lax.ppermute(above, "slab", deeper)
    run = depth // 2
    inner = []
    for c in range(2):
        inner.append(inner_terms(c * run, run, spread, back_high, back_low, chan))
    edge = [from_below, from_above]

    scale = math.sqrt(depth * slabs * area)

    def swap(x, bit):
        return lax.ppermute(x, "slab", [(i, i ^ bit) for i in range(slabs)])

    weight_grad = None
    for tap in range(3):
        keep, give = filter_terms(tap, ring, spread, high_field, low_field)
        keep = keep + swap(give, 1)
        bit = 2
        while bit < slabs:
            keep = keep + swap(keep, bit)
            bit *= 2
        other = swap(keep, 1)
        weight_grad = place(tap, ring, keep, other, weight_grad, scale)

    piece = (chan, run * area)
    part = (chan // 2, run * area)
    flows = []
    for c in range(2):
        kernel = functools.partial(opening_kernel, c == 0)
        flows.append(summed(kernel, ring, [(inner[c], half), (edge[c], half)], [part, part]))
    for step in range(half - 1, 0, -1):
        for c in range(2):
            up, down = flows[c]
            up, down = send(up, ring_up), send(down, ring_down)
            kernel = functools.partial(running_kernel, c == 0)
            pieces = [(x, p) for p in (step, count - step) for x in (inner[c], edge[c])]
            flows[c] = summed(kernel, ring, pieces + [up, down], [piece, piece])
    pieces = []
    for c in range(2):
        up, down = flows[c]
        pieces += [(inner[c], 0), (edge[c], 0), send(up, ring_up), send(down, ring_down)]
    (input_grad,) = summed(closing_kernel, ring, pieces, [(chan, depth, area)])
    return activated, input_grad, weight_grad.reshape(filters.shape)


def solution(mesh):
    placed = (P("filt", "slab", None), P(None, "filt", None), P("filt", "slab", None))

    def step(*args):
        return shards(*args)

    step = jax.shard_map(
        step,
        mesh=mesh,
        in_specs=placed,
        out_specs=(P("filt", "slab", None), P("filt", "slab", None), P(None, "filt", None)),
        check_vma=False,
    )
    return step
```

```python
import functools
import math

import jax
import jax.numpy as jnp
from jax import lax
from jax.experimental import pallas as pl
from jax.experimental.pallas import tpu as pltpu
from jax.sharding import PartitionSpec as P


WIDTH = 16


f32 = jnp.float32
bf16 = jnp.bfloat16


def parts_of(x):
    high = x.astype(bf16)
    low = (x - high.astype(f32)).astype(bf16)
    return high, low


def dot(a, b):
    return lax.dot_general(a, b, (((1,), (0,)), ((), ())), preferred_element_type=f32)


def dot_t(a, b):
    return lax.dot_general(a, b, (((1,), (1,)), ((), ())), preferred_element_type=f32)


def beside(ring, n, rim):
    return jnp.where(ring[ring.shape[0] - 3 + n] > 0, rim, 0.0)


def whole(shape):
    return pl.BlockSpec(shape, lambda *_: (0,) * len(shape))


def limit():
    return pltpu.CompilerParams(vmem_limit_bytes=28 * 2**20)


def cost(flops, moved):
    return pl.CostEstimate(flops=int(flops), bytes_accessed=int(moved), transcendentals=0)


def moved(x, down, across):
    size = x.shape[-1]
    place = lax.broadcasted_iota(jnp.int32, x.shape, 1)
    if across:
        column = place % WIDTH + across
        rolled = pltpu.roll(x, (-across) % size, 1)
        x = jnp.where((column >= 0) & (column < WIDTH), rolled, 0.0)
    if down:
        target = place + down * WIDTH
        rolled = pltpu.roll(x, (-down * WIDTH) % size, 1)
        x = jnp.where((target >= 0) & (target < size), rolled, 0.0)
    return x


def prepare_kernel(chan, filters, ahead, back_high, back_low):
    taps, out_rows, lanes = filters.shape
    third = taps * out_rows // 3
    for a in range(3):
        x = filters[a * 9 : (a + 1) * 9].reshape(third, lanes)
        high, low = parts_of(x)
        for k in range(lanes // chan):
            at = slice(k * chan, (k + 1) * chan)
            ahead[a, k] = jnp.concatenate([high[:, at], low[:, at], high[:, at]], axis=1)
    turned = [filters[a * 9 : (a + 1) * 9].reshape(third, lanes).T for a in (2, 1, 0)]
    high, low = parts_of(jnp.concatenate(turned, axis=1))
    back_high[...] = high
    back_low[...] = low


def prepare(filters, chan):
    taps, out_rows, channels = filters.shape
    lanes = min(128, channels)
    each = lanes // chan
    return pl.pallas_call(
        functools.partial(prepare_kernel, chan),
        grid=(channels // lanes,),
        in_specs=[pl.BlockSpec((taps, out_rows, lanes), lambda i: (0, 0, i))],
        out_specs=[
            pl.BlockSpec((3, each, 9 * out_rows, 3 * chan), lambda i: (0, i, 0, 0)),
            pl.BlockSpec((lanes, taps * out_rows), lambda i: (i, 0)),
            pl.BlockSpec((lanes, taps * out_rows), lambda i: (i, 0)),
        ],
        out_shape=[
            jax.ShapeDtypeStruct((3, channels // chan, 9 * out_rows, 3 * chan), bf16),
            jax.ShapeDtypeStruct((channels, taps * out_rows), bf16),
            jax.ShapeDtypeStruct((channels, taps * out_rows), bf16),
        ],
        cost_estimate=cost(0, 5 * 4 * filters.size),
        name="prepare",
    )(filters)


def rims_kernel(*refs):
    blocks, (last, top) = refs[:-2], refs[-2:]
    at = 0
    for block in blocks:
        rows, depth, _ = block.shape
        planes = jnp.swapaxes(block[...], 0, 1)
        last[at : at + rows] = planes[depth - 1]
        top[at : at + rows] = planes[0]
        at += rows


def rims(blocks):
    rows = sum(b.shape[0] for b in blocks)
    shape = jax.ShapeDtypeStruct((rows, blocks[0].shape[2]), f32)
    return pl.pallas_call(
        rims_kernel,
        out_shape=[shape, shape],
        cost_estimate=cost(0, 4 * sum(b.size for b in blocks)),
        compiler_params=limit(),
        name="rims",
    )(*blocks)


def gathered(answer, out_rows):
    rows = []
    for b in range(3):
        row = None
        for c in range(3):
            at = (3 * b + c) * out_rows
            term = moved(answer[at : at + out_rows], 0, c - 1)
            row = term if row is None else row + term
        rows.append(moved(row, b - 1, 0))
    return rows[0] + rows[1] + rows[2]


def forward_kernel(counts, places, rim_places, first, ring, *refs):
    refs = list(refs)

    def take(n):
        taken = refs[:n]
        del refs[:n]
        return taken

    blocks = take(sum(counts))
    (source,) = take(1)
    rims_in = take(2) if rim_places else []
    total_in = None if first else take(3)[0]
    total_out, high_all, low_all, field, high_part, low_part, high_rim, low_rim = take(8)
    weights, rim_weights, sems, fetch_sems = refs
    fetches = [
        pltpu.make_async_copy(source.at[:, ring[place]], weights.at[k], fetch_sems.at[k])
        for k, place in enumerate(places)
    ]
    for k, place in enumerate(rim_places):
        for n in range(2):
            sem = fetch_sems.at[len(fetches)]
            fetches.append(
                pltpu.make_async_copy(source.at[2 * n, ring[place]], rim_weights.at[n, k], sem)
            )
    for fetch in fetches:
        fetch.start()
    depth, out_rows, area = total_out.shape
    chan = field.shape[2] // 3
    copies = []

    def keep(part, target, place, lanes):
        at = pl.ds(pl.multiple_of(ring[place] * chan, chan), chan)
        copies.append(pltpu.make_async_copy(part, target.at[at, lanes], sems.at[len(copies)]))
        copies[-1].start()

    begin = 0
    for k, pieces in enumerate(counts):
        loaded = [jnp.swapaxes(b[...], 0, 1) for b in blocks[begin : begin + pieces]]
        begin += pieces
        for plane in range(depth):
            rows = [b[plane] for b in loaded]
            x = rows[0] if pieces == 1 else jnp.concatenate(rows, axis=0)
            high, low = parts_of(x)
            field[k, plane, 0:chan] = high
            field[k, plane, chan : 2 * chan] = high
            field[k, plane, 2 * chan : 3 * chan] = low
            high_part[k, :, plane * area : (plane + 1) * area] = high
            low_part[k, :, plane * area : (plane + 1) * area] = low
        lanes = pl.ds(area, depth * area)
        keep(high_part.at[k], high_all, places[k], lanes)
        keep(low_part.at[k], low_all, places[k], lanes)
    for n, rim in enumerate(rims_in):
        lanes = pl.ds(n * (depth + 1) * area, area)
        for k in range(len(rim_places)):
            high, low = parts_of(beside(ring, n, rim[k * chan : (k + 1) * chan]))
            high_rim[n, k] = high
            low_rim[n, k] = low
            keep(high_rim.at[n, k], high_all, rim_places[k], lanes)
            keep(low_rim.at[n, k], low_all, rim_places[k], lanes)

    for fetch in fetches:
        fetch.wait()
    for plane in range(depth):
        terms = []
        for a in range(3):
            if 0 <= plane + a - 1 < depth:
                for k in range(len(counts)):
                    terms.append((weights[k, a], field[k, plane + a - 1]))
        for n, edge in enumerate((0, depth - 1)):
            if plane == edge:
                for k in range(len(rim_places)):
                    right = [high_rim[n, k], high_rim[n, k], low_rim[n, k]]
                    terms.append((rim_weights[n, k], jnp.concatenate(right, axis=0)))
        answer = None
        for left, right in terms:
            term = dot(left, right)
            answer = term if answer is None else answer + term
        total = gathered(answer, out_rows)
        if total_in is not None:
            total = total + total_in[plane]
        total_out[plane] = total
    for copy in copies:
        copy.wait()


def forward(ring, sets, places, rim_places, outer, weights, carry, sizes):
    depth, chan, area, channels, out_rows = sizes
    counts = tuple(len(s) for s in sets)
    blocks = [b for s in sets for b in s]
    first = carry is None
    lanes = (depth + 2) * area
    keep = pl.BlockSpec(memory_space=pltpu.HBM)
    in_specs = [whole(b.shape) for b in blocks]
    args = list(blocks)
    in_specs.append(keep)
    args.append(weights)
    if rim_places:
        in_specs += [whole(o.shape) for o in outer]
        args += list(outer)
    aliases = {}
    if not first:
        base = len(args) + 1
        in_specs += [whole((depth, out_rows, area)), keep, keep]
        args += list(carry)
        aliases = {base: 0, base + 1: 1, base + 2: 2}
    rims_held = max(1, len(rim_places))
    return pl.pallas_call(
        functools.partial(forward_kernel, counts, places, rim_places, first),
        grid_spec=pltpu.PrefetchScalarGridSpec(
            num_scalar_prefetch=1,
            grid=(1,),
            in_specs=in_specs,
            out_specs=[whole((depth, out_rows, area)), keep, keep],
            scratch_shapes=[
                pltpu.VMEM((len(sets), depth, 3 * chan, area), bf16),
                pltpu.VMEM((len(sets), chan, depth * area), bf16),
                pltpu.VMEM((len(sets), chan, depth * area), bf16),
                pltpu.VMEM((2, rims_held, chan, area), bf16),
                pltpu.VMEM((2, rims_held, chan, area), bf16),
                pltpu.VMEM((len(sets), 3) + weights.shape[2:], bf16),
                pltpu.VMEM((2, rims_held) + weights.shape[2:], bf16),
                pltpu.SemaphoreType.DMA((2 * len(sets) + 4 * rims_held,)),
                pltpu.SemaphoreType.DMA((len(sets) + 2 * rims_held,)),
            ],
        ),
        out_shape=[
            jax.ShapeDtypeStruct((depth, out_rows, area), f32),
            jax.ShapeDtypeStruct((channels, lanes), bf16),
            jax.ShapeDtypeStruct((channels, lanes), bf16),
        ],
        input_output_aliases=aliases,
        cost_estimate=cost(
            len(sets) * 2 * 81 * out_rows * chan * depth * area, len(sets) * 8 * chan * lanes
        ),
        compiler_params=limit(),
        name="forward",
    )(ring, *args)


def middle_kernel(places, ring, total, grad, below, above, source, *refs):
    active_out, spread_out, high_all, low_all, high_rim, low_rim, weights, sems, fetch_sems = refs[2:]
    depth, out_rows, area = total.shape
    chan = below.shape[0] // len(places)
    copies = []
    rim_sums = []
    fetches = {}
    for n in range(2):
        for k, place in enumerate(places):
            fetches[n, k] = pltpu.make_async_copy(
                source.at[2 * n, ring[place]], weights.at[n, k], fetch_sems.at[n, k]
            )
            fetches[n, k].start()
    for n, rim in enumerate((below, above)):
        answer = None
        for k, place in enumerate(places):
            value = beside(ring, n, rim[k * chan : (k + 1) * chan])
            high, low = parts_of(value)
            high_rim[n, k] = high
            low_rim[n, k] = low
            at = pl.ds(pl.multiple_of(ring[place] * chan, chan), chan)
            lanes = pl.ds(n * (depth + 1) * area, area)
            for m, (part, target) in enumerate(((high_rim, high_all), (low_rim, low_all))):
                copy = pltpu.make_async_copy(part.at[n, k], target.at[at, lanes], sems.at[n, k, m])
                copy.start()
                copies.append(copy)
            fetches[n, k].wait()
            term = dot(weights[n, k], jnp.concatenate([high, high, low], axis=0))
            answer = term if answer is None else answer + term
        rim_sums.append(gathered(answer, out_rows))
    positives = []
    for plane in range(depth):
        value = total[plane]
        if plane == 0:
            value = value + rim_sums[0]
        if plane == depth - 1:
            value = value + rim_sums[1]
        positives.append(jnp.maximum(value, 0.0))
    positives = jnp.stack(positives)
    active_out[...] = jnp.swapaxes(positives * positives, 0, 1)
    grads = jnp.swapaxes(grad[...], 0, 1)
    nothing = jnp.zeros((9 * out_rows, area), bf16)
    for part in range(2):
        spread_out[part, 0] = nothing
        spread_out[part, depth + 1] = nothing
    for plane in range(depth):
        pre_grad = 2.0 * positives[plane] * grads[plane]
        for c in range(3):
            across = moved(pre_grad, 0, 1 - c)
            for b in range(3):
                high, low = parts_of(moved(across, 1 - b, 0))
                at = (3 * b + c) * out_rows
                spread_out[0, plane + 1, at : at + out_rows] = high
                spread_out[1, plane + 1, at : at + out_rows] = low
    for copy in copies:
        copy.wait()


def middle(ring, carry, grad, places, outer, weights, chan):
    total, high_all, low_all = carry
    depth, out_rows, area = total.shape
    keep = pl.BlockSpec(memory_space=pltpu.HBM)
    return pl.pallas_call(
        functools.partial(middle_kernel, places),
        grid_spec=pltpu.PrefetchScalarGridSpec(
            num_scalar_prefetch=1,
            grid=(1,),
            in_specs=[whole(x.shape) for x in (total, grad, *outer)]
            + [keep, keep, keep],
            out_specs=[
                whole((out_rows, depth, area)),
                whole((2, depth + 2, 9 * out_rows, area)),
                keep,
                keep,
            ],
            scratch_shapes=[
                pltpu.VMEM((2, len(places), chan, area), bf16),
                pltpu.VMEM((2, len(places), chan, area), bf16),
                pltpu.VMEM((2, len(places)) + weights.shape[2:], bf16),
                pltpu.SemaphoreType.DMA((2, len(places), 2)),
                pltpu.SemaphoreType.DMA((2, len(places))),
            ],
        ),
        out_shape=[
            jax.ShapeDtypeStruct((out_rows, depth, area), f32),
            jax.ShapeDtypeStruct((2, depth + 2, 9 * out_rows, area), bf16),
            jax.ShapeDtypeStruct(high_all.shape, bf16),
            jax.ShapeDtypeStruct(low_all.shape, bf16),
        ],
        input_output_aliases={6: 2, 7: 3},
        cost_estimate=cost(0, 4 * 18 * out_rows * depth * area),
        compiler_params=limit(),
        name="middle",
    )(ring, total, grad, *outer, weights, high_all, low_all)


def inner_kernel(begin, planes, spread, high, low, out):
    deep = high.shape[1]
    count, chan, _ = out.shape
    area = spread.shape[3]
    group = 2 - planes % 2

    def some(i, nothing):
        for j in range(group):
            near = spread[0, pl.ds(begin + i * group + j, 3)].reshape(deep, area)
            far = spread[1, pl.ds(begin + i * group + j, 3)].reshape(deep, area)
            value = dot(high[...], near) + dot(high[...], far) + dot(low[...], near)
            lanes = pl.ds(pl.multiple_of((i * group + j) * area, area), area)
            out[:, :, lanes] = value.reshape(count, chan, area)
        return nothing

    lax.fori_loop(0, planes // group, some, 0)


def outer_kernel(spread, high, low, below, above):
    depth = spread.shape[1] - 2
    third = high.shape[1] // 3
    for out, plane, at in ((below, 1, 2 * third), (above, depth, 0)):
        lanes = slice(at, at + third)
        value = dot(high[:, lanes], spread[0, plane]) + dot(high[:, lanes], spread[1, plane])
        value = value + dot(low[:, lanes], spread[0, plane])
        out[...] = value.reshape(out.shape)


def inner_terms(begin, planes, spread, high, low, chan):
    channels, deep = high.shape
    area = spread.shape[3]
    return pl.pallas_call(
        functools.partial(inner_kernel, begin, planes),
        out_shape=jax.ShapeDtypeStruct((channels // chan, chan, planes * area), f32),
        cost_estimate=cost(6 * channels * deep * planes * area, 2 * spread.size + 4 * high.size),
        compiler_params=limit(),
        name="inner_terms",
    )(spread, high, low)


def outer_terms(spread, high, low, chan):
    channels, deep = high.shape
    shape = jax.ShapeDtypeStruct((channels // chan, chan, spread.shape[3]), f32)
    return pl.pallas_call(
        outer_kernel,
        out_shape=[shape, shape],
        cost_estimate=cost(4 * channels * deep * spread.shape[3], spread.size),
        compiler_params=limit(),
        name="outer_terms",
    )(spread, high, low)


def filter_kernel(tap, ring, spread, high, low, keep_out, send_out, total):
    depth = spread.shape[1] - 2
    rows, area = spread.shape[2:]
    half = rows // 2
    channels = high.shape[0]
    step = min(256, channels)
    for at in range(0, channels, step):
        value = None
        for plane in range(depth):
            lanes = slice((tap + plane) * area, (tap + plane + 1) * area)
            right = high[at : at + step, lanes]
            term = dot_t(spread[0, plane + 1], right) + dot_t(spread[1, plane + 1], right)
            term = term + dot_t(spread[0, plane + 1], low[at : at + step, lanes])
            value = term if value is None else value + term
        total[:, at : at + step] = value
    side = ring[ring.shape[0] - 1]
    mine = pl.multiple_of(side * half, half)
    other = pl.multiple_of((1 - side) * half, half)
    keep_out[...] = total[pl.ds(mine, half), :]
    send_out[...] = total[pl.ds(other, half), :]


def filter_terms(tap, ring, spread, high, low):
    rows = spread.shape[2]
    channels = high.shape[0]
    return pl.pallas_call(
        functools.partial(filter_kernel, tap),
        grid_spec=pltpu.PrefetchScalarGridSpec(
            num_scalar_prefetch=1,
            grid=(1,),
            in_specs=[whole(spread.shape), whole(high.shape), whole(low.shape)],
            out_specs=[whole((rows // 2, channels))] * 2,
            scratch_shapes=[pltpu.VMEM((rows, channels), f32)],
        ),
        out_shape=[jax.ShapeDtypeStruct((rows // 2, channels), f32)] * 2,
        cost_estimate=cost(6 * rows * high.size, 4 * high.size + 2 * spread.size),
        compiler_params=limit(),
        name="filter_terms",
    )(ring, spread, high, low)


def place_kernel(scale, ring, *refs):
    mine, other, out = refs[0], refs[1], refs[-1]
    half = mine.shape[0]
    side = ring[ring.shape[0] - 1]
    out[0, pl.ds(pl.multiple_of(side * half, half), half), :] = mine[...] / scale
    out[0, pl.ds(pl.multiple_of((1 - side) * half, half), half), :] = other[...] / scale


def place(tap, ring, mine, other, carry, scale):
    half, channels = mine.shape
    args = [mine, other]
    in_specs = [whole(mine.shape)] * 2
    aliases = {}
    if carry is not None:
        args.append(carry)
        in_specs.append(pl.BlockSpec(memory_space=pl.ANY))
        aliases = {3: 0}
    return pl.pallas_call(
        functools.partial(place_kernel, scale),
        grid_spec=pltpu.PrefetchScalarGridSpec(
            num_scalar_prefetch=1,
            grid=(1,),
            in_specs=in_specs,
            out_specs=pl.BlockSpec((1, 2 * half, channels), lambda i, s: (tap, 0, 0)),
        ),
        out_shape=jax.ShapeDtypeStruct((3, 2 * half, channels), f32),
        input_output_aliases=aliases,
        cost_estimate=cost(0, 16 * half * channels),
        compiler_params=limit(),
        name="place",
    )(ring, *args)


def local_sum(ring, inner, rim, first):
    value, rim = inner[0], beside(ring, 0 if first else 1, rim[0])
    area = rim.shape[1]
    width = value.shape[1]
    if first:
        return jnp.concatenate([value[:, :area] + rim, value[:, area:]], axis=1)
    return jnp.concatenate([value[:, : width - area], value[:, width - area :] + rim], axis=1)


def opening_kernel(first, ring, inner, rim, up_out, down_out):
    value = local_sum(ring, inner, rim, first)
    half = value.shape[0] // 2
    up_out[...] = value[:half]
    down_out[...] = value[half:]


def running_kernel(first, ring, up_inner, up_rim, down_inner, down_rim, up, down, up_out, down_out):
    value = local_sum(ring, up_inner, up_rim, first)
    size = up.shape[0]
    up_out[0:size] = value[0:size] + up[...]
    if size < value.shape[0]:
        up_out[size:] = value[size:]
    value = local_sum(ring, down_inner, down_rim, first)
    rest = value.shape[0] - size
    down_out[rest:] = value[rest:] + down[...]
    if rest:
        down_out[0:rest] = value[0:rest]


def closing_kernel(ring, *refs):
    chains, out = (refs[0:4], refs[4:8]), refs[8]
    area = out.shape[2]
    values = []
    for first, (inner, rim, up, down) in zip((True, False), chains):
        value = local_sum(ring, inner, rim, first) + up[...] + down[...]
        values += [value[:, at : at + area] for at in range(0, value.shape[1], area)]
    out[...] = jnp.swapaxes(jnp.stack(values), 0, 1)


def summed(kernel, ring, pieces, outs):
    specs, args = [], []
    for piece in pieces:
        if isinstance(piece, tuple):
            array, k = piece
            specs.append(pl.BlockSpec((1,) + array.shape[1:], lambda i, s, k=k: (s[k], 0, 0)))
            args.append(array)
        else:
            specs.append(whole(piece.shape))
            args.append(piece)
    return pl.pallas_call(
        kernel,
        grid_spec=pltpu.PrefetchScalarGridSpec(
            num_scalar_prefetch=1,
            grid=(1,),
            in_specs=specs,
            out_specs=[whole(o) for o in outs],
        ),
        out_shape=[jax.ShapeDtypeStruct(o, f32) for o in outs],
        cost_estimate=cost(0, sum(12 * math.prod(o) for o in outs)),
        compiler_params=limit(),
    )(ring, *args)


def shards(volume, filters, out_grad):
    chan, depth, area = volume.shape
    out_rows = filters.shape[1]
    channels = filters.shape[2]
    count = lax.axis_size("filt")
    slabs = lax.axis_size("slab")
    sizes = (depth, chan, area, channels, out_rows)

    order = list(range(0, count, 2)) + list(range(1, count, 2))[::-1]
    ring_up = [(order[i], order[(i + 1) % count]) for i in range(count)]
    ring_down = [(b, a) for a, b in ring_up]
    rows = [
        [order[(order.index(f) + k) % count] for k in range(count)]
        + [int(s > 0), int(s < slabs - 1), s % 2]
        for s in range(slabs)
        for f in range(count)
    ]
    here = lax.axis_index("slab") * count + lax.axis_index("filt")
    ring = lax.dynamic_index_in_dim(jnp.array(rows, jnp.int32), here, 0, keepdims=False)

    def send(x, pairs):
        return lax.ppermute(x, "filt", pairs)

    deeper = [(i, (i + 1) % slabs) for i in range(slabs)]
    shallower = [(b, a) for a, b in deeper]
    half = count // 2

    ahead, back_high, back_low = prepare(filters, chan)
    ahead = pltpu.with_memory_space_constraint(ahead, pltpu.HBM)

    carry = None
    up = down = volume
    rim_places, outer = (), None
    held, held_places = [], ()
    for step in range(half + 1):
        if step == 0:
            sets, places = [[volume]], (0,)
        elif step < half:
            up, down = send(up, ring_up), send(down, ring_down)
            sets, places = [[up], [down]], (count - step, step)
        else:
            up = send(up[: chan // 2], ring_up)
            down = send(down[chan // 2 :], ring_down)
            sets, places = [[up, down]], (half,)
        held += [b for blocks in sets for b in blocks]
        held_places += places
        carry = forward(ring, sets, places, rim_places, outer, ahead, carry, sizes)
        rim_places, outer = (), None
        if step not in (0, half - 1):
            last, top = rims(held)
            outer = lax.ppermute(last, "slab", deeper), lax.ppermute(top, "slab", shallower)
            rim_places, held, held_places = held_places, [], ()

    activated, spread, high_field, low_field = middle(
        ring, carry, out_grad, rim_places, outer, ahead, chan
    )

    below, above = outer_terms(spread, back_high, back_low, chan)
    from_below = lax.ppermute(above, "slab", deeper)
    from_above = lax.ppermute(below, "slab", shallower)
    run = depth // 2
    inner = []
    for c in range(2):
        inner.append(inner_terms(c * run, run, spread, back_high, back_low, chan))
    edge = [from_below, from_above]

    scale = math.sqrt(depth * slabs * area)

    def swap(x, bit):
        return lax.ppermute(x, "slab", [(i, i ^ bit) for i in range(slabs)])

    weight_grad = None
    for tap in range(3):
        keep, give = filter_terms(tap, ring, spread, high_field, low_field)
        keep = keep + swap(give, 1)
        bit = 2
        while bit < slabs:
            keep = keep + swap(keep, bit)
            bit *= 2
        other = swap(keep, 1)
        weight_grad = place(tap, ring, keep, other, weight_grad, scale)

    piece = (chan, run * area)
    part = (chan // 2, run * area)
    flows = []
    for c in range(2):
        kernel = functools.partial(opening_kernel, c == 0)
        flows.append(summed(kernel, ring, [(inner[c], half), (edge[c], half)], [part, part]))
    for step in range(half - 1, 0, -1):
        for c in range(2):
            up, down = flows[c]
            up, down = send(up, ring_up), send(down, ring_down)
            kernel = functools.partial(running_kernel, c == 0)
            pieces = [(x, p) for p in (step, count - step) for x in (inner[c], edge[c])]
            flows[c] = summed(kernel, ring, pieces + [up, down], [piece, piece])
    pieces = []
    for c in range(2):
        up, down = flows[c]
        pieces += [(inner[c], 0), (edge[c], 0), send(up, ring_up), send(down, ring_down)]
    (input_grad,) = summed(closing_kernel, ring, pieces, [(chan, depth, area)])
    return activated, input_grad, weight_grad.reshape(filters.shape)


def solution(mesh):
    placed = (P("filt", "slab", None), P(None, "filt", None), P("filt", "slab", None))

    def step(*args):
        return shards(*args)

    step = jax.shard_map(
        step,
        mesh=mesh,
        in_specs=placed,
        out_specs=(P("filt", "slab", None), P("filt", "slab", None), P(None, "filt", None)),
        check_vma=False,
    )
    return step
```

```python
import functools
import math

import jax
import jax.numpy as jnp
from jax import lax
from jax.experimental import pallas as pl
from jax.experimental.pallas import tpu as pltpu
from jax.sharding import PartitionSpec as P


WIDTH = 16


f32 = jnp.float32
bf16 = jnp.bfloat16


def parts_of(x):
    high = x.astype(bf16)
    low = (x - high.astype(f32)).astype(bf16)
    return high, low


def dot(a, b):
    return lax.dot_general(a, b, (((1,), (0,)), ((), ())), preferred_element_type=f32)


def dot_t(a, b):
    return lax.dot_general(a, b, (((1,), (1,)), ((), ())), preferred_element_type=f32)


def beside(ring, n, rim):
    return jnp.where(ring[ring.shape[0] - 3 + n] > 0, rim, 0.0)


def whole(shape):
    return pl.BlockSpec(shape, lambda *_: (0,) * len(shape))


def limit():
    return pltpu.CompilerParams(vmem_limit_bytes=28 * 2**20)


def cost(flops, moved):
    return pl.CostEstimate(flops=int(flops), bytes_accessed=int(moved), transcendentals=0)


def moved(x, down, across):
    size = x.shape[-1]
    place = lax.broadcasted_iota(jnp.int32, x.shape, 1)
    if across:
        column = place % WIDTH + across
        rolled = pltpu.roll(x, (-across) % size, 1)
        x = jnp.where((column >= 0) & (column < WIDTH), rolled, 0.0)
    if down:
        target = place + down * WIDTH
        rolled = pltpu.roll(x, (-down * WIDTH) % size, 1)
        x = jnp.where((target >= 0) & (target < size), rolled, 0.0)
    return x


def prepare_kernel(chan, filters, ahead, back_high, back_low):
    taps, out_rows, lanes = filters.shape
    third = taps * out_rows // 3
    for a in range(3):
        x = filters[a * 9 : (a + 1) * 9].reshape(third, lanes)
        high, low = parts_of(x)
        for k in range(lanes // chan):
            at = slice(k * chan, (k + 1) * chan)
            ahead[a, k] = jnp.concatenate([high[:, at], low[:, at], high[:, at]], axis=1)
    turned = [filters[a * 9 : (a + 1) * 9].reshape(third, lanes).T for a in (2, 1, 0)]
    high, low = parts_of(jnp.concatenate(turned, axis=1))
    back_high[...] = high
    back_low[...] = low


def prepare(filters, chan):
    taps, out_rows, channels = filters.shape
    lanes = min(128, channels)
    each = lanes // chan
    return pl.pallas_call(
        functools.partial(prepare_kernel, chan),
        grid=(channels // lanes,),
        in_specs=[pl.BlockSpec((taps, out_rows, lanes), lambda i: (0, 0, i))],
        out_specs=[
            pl.BlockSpec((3, each, 9 * out_rows, 3 * chan), lambda i: (0, i, 0, 0)),
            pl.BlockSpec((lanes, taps * out_rows), lambda i: (i, 0)),
            pl.BlockSpec((lanes, taps * out_rows), lambda i: (i, 0)),
        ],
        out_shape=[
            jax.ShapeDtypeStruct((3, channels // chan, 9 * out_rows, 3 * chan), bf16),
            jax.ShapeDtypeStruct((channels, taps * out_rows), bf16),
            jax.ShapeDtypeStruct((channels, taps * out_rows), bf16),
        ],
        cost_estimate=cost(0, 5 * 4 * filters.size),
        name="prepare",
    )(filters)


def rims_kernel(*refs):
    blocks, (last, top) = refs[:-2], refs[-2:]
    at = 0
    for block in blocks:
        rows, depth, _ = block.shape
        planes = jnp.swapaxes(block[...], 0, 1)
        last[at : at + rows] = planes[depth - 1]
        top[at : at + rows] = planes[0]
        at += rows


def rims(blocks):
    rows = sum(b.shape[0] for b in blocks)
    shape = jax.ShapeDtypeStruct((rows, blocks[0].shape[2]), f32)
    return pl.pallas_call(
        rims_kernel,
        out_shape=[shape, shape],
        cost_estimate=cost(0, 4 * sum(b.size for b in blocks)),
        compiler_params=limit(),
        name="rims",
    )(*blocks)


def gathered(answer, out_rows):
    rows = []
    for b in range(3):
        row = None
        for c in range(3):
            at = (3 * b + c) * out_rows
            term = moved(answer[at : at + out_rows], 0, c - 1)
            row = term if row is None else row + term
        rows.append(moved(row, b - 1, 0))
    return rows[0] + rows[1] + rows[2]


def forward_kernel(counts, places, rim_places, first, ring, *refs):
    refs = list(refs)

    def take(n):
        taken = refs[:n]
        del refs[:n]
        return taken

    blocks = take(sum(counts))
    (source,) = take(1)
    rims_in = take(2) if rim_places else []
    total_in = None if first else take(3)[0]
    total_out, high_all, low_all, field, high_part, low_part, high_rim, low_rim = take(8)
    weights, rim_weights, sems, fetch_sems = refs
    fetches = [
        pltpu.make_async_copy(source.at[:, ring[place]], weights.at[k], fetch_sems.at[k])
        for k, place in enumerate(places)
    ]
    for k, place in enumerate(rim_places):
        for n in range(2):
            sem = fetch_sems.at[len(fetches)]
            fetches.append(
                pltpu.make_async_copy(source.at[2 * n, ring[place]], rim_weights.at[n, k], sem)
            )
    for fetch in fetches:
        fetch.start()
    depth, out_rows, area = total_out.shape
    chan = field.shape[2] // 3
    copies = []

    def keep(part, target, place, lanes):
        at = pl.ds(pl.multiple_of(ring[place] * chan, chan), chan)
        copies.append(pltpu.make_async_copy(part, target.at[at, lanes], sems.at[len(copies)]))
        copies[-1].start()

    begin = 0
    for k, pieces in enumerate(counts):
        loaded = [jnp.swapaxes(b[...], 0, 1) for b in blocks[begin : begin + pieces]]
        begin += pieces
        for plane in range(depth):
            rows = [b[plane] for b in loaded]
            x = rows[0] if pieces == 1 else jnp.concatenate(rows, axis=0)
            high, low = parts_of(x)
            field[k, plane, 0:chan] = high
            field[k, plane, chan : 2 * chan] = high
            field[k, plane, 2 * chan : 3 * chan] = low
            high_part[k, :, plane * area : (plane + 1) * area] = high
            low_part[k, :, plane * area : (plane + 1) * area] = low
        lanes = pl.ds(area, depth * area)
        keep(high_part.at[k], high_all, places[k], lanes)
        keep(low_part.at[k], low_all, places[k], lanes)
    for n, rim in enumerate(rims_in):
        lanes = pl.ds(n * (depth + 1) * area, area)
        for k in range(len(rim_places)):
            high, low = parts_of(beside(ring, n, rim[k * chan : (k + 1) * chan]))
            high_rim[n, k] = high
            low_rim[n, k] = low
            keep(high_rim.at[n, k], high_all, rim_places[k], lanes)
            keep(low_rim.at[n, k], low_all, rim_places[k], lanes)

    for fetch in fetches:
        fetch.wait()
    for plane in range(depth):
        terms = []
        for a in range(3):
            if 0 <= plane + a - 1 < depth:
                for k in range(len(counts)):
                    terms.append((weights[k, a], field[k, plane + a - 1]))
        for n, edge in enumerate((0, depth - 1)):
            if plane == edge:
                for k in range(len(rim_places)):
                    right = [high_rim[n, k], high_rim[n, k], low_rim[n, k]]
                    terms.append((rim_weights[n, k], jnp.concatenate(right, axis=0)))
        answer = None
        for left, right in terms:
            term = dot(left, right)
            answer = term if answer is None else answer + term
        total = gathered(answer, out_rows)
        if total_in is not None:
            total = total + total_in[plane]
        total_out[plane] = total
    for copy in copies:
        copy.wait()


def forward(ring, sets, places, rim_places, outer, weights, carry, sizes):
    depth, chan, area, channels, out_rows = sizes
    counts = tuple(len(s) for s in sets)
    blocks = [b for s in sets for b in s]
    first = carry is None
    lanes = (depth + 2) * area
    keep = pl.BlockSpec(memory_space=pltpu.HBM)
    in_specs = [whole(b.shape) for b in blocks]
    args = list(blocks)
    in_specs.append(keep)
    args.append(weights)
    if rim_places:
        in_specs += [whole(o.shape) for o in outer]
        args += list(outer)
    aliases = {}
    if not first:
        base = len(args) + 1
        in_specs += [whole((depth, out_rows, area)), keep, keep]
        args += list(carry)
        aliases = {base: 0, base + 1: 1, base + 2: 2}
    rims_held = max(1, len(rim_places))
    return pl.pallas_call(
        functools.partial(forward_kernel, counts, places, rim_places, first),
        grid_spec=pltpu.PrefetchScalarGridSpec(
            num_scalar_prefetch=1,
            grid=(1,),
            in_specs=in_specs,
            out_specs=[whole((depth, out_rows, area)), keep, keep],
            scratch_shapes=[
                pltpu.VMEM((len(sets), depth, 3 * chan, area), bf16),
                pltpu.VMEM((len(sets), chan, depth * area), bf16),
                pltpu.VMEM((len(sets), chan, depth * area), bf16),
                pltpu.VMEM((2, rims_held, chan, area), bf16),
                pltpu.VMEM((2, rims_held, chan, area), bf16),
                pltpu.VMEM((len(sets), 3) + weights.shape[2:], bf16),
                pltpu.VMEM((2, rims_held) + weights.shape[2:], bf16),
                pltpu.SemaphoreType.DMA((2 * len(sets) + 4 * rims_held,)),
                pltpu.SemaphoreType.DMA((len(sets) + 2 * rims_held,)),
            ],
        ),
        out_shape=[
            jax.ShapeDtypeStruct((depth, out_rows, area), f32),
            jax.ShapeDtypeStruct((channels, lanes), bf16),
            jax.ShapeDtypeStruct((channels, lanes), bf16),
        ],
        input_output_aliases=aliases,
        cost_estimate=cost(
            len(sets) * 2 * 81 * out_rows * chan * depth * area, len(sets) * 8 * chan * lanes
        ),
        compiler_params=limit(),
        name="forward",
    )(ring, *args)


def middle_kernel(places, ring, total, grad, below, above, source, *refs):
    kept_out, spread_out, high_all, low_all, high_rim, low_rim, weights, sems, fetch_sems = refs[2:]
    depth, out_rows, area = total.shape
    chan = below.shape[0] // len(places)
    copies = []
    rim_sums = []
    fetches = {}
    for n in range(2):
        for k, place in enumerate(places):
            fetches[n, k] = pltpu.make_async_copy(
                source.at[2 * n, ring[place]], weights.at[n, k], fetch_sems.at[n, k]
            )
            fetches[n, k].start()
    for n, rim in enumerate((below, above)):
        answer = None
        for k, place in enumerate(places):
            value = beside(ring, n, rim[k * chan : (k + 1) * chan])
            high, low = parts_of(value)
            high_rim[n, k] = high
            low_rim[n, k] = low
            at = pl.ds(pl.multiple_of(ring[place] * chan, chan), chan)
            lanes = pl.ds(n * (depth + 1) * area, area)
            for m, (part, target) in enumerate(((high_rim, high_all), (low_rim, low_all))):
                copy = pltpu.make_async_copy(part.at[n, k], target.at[at, lanes], sems.at[n, k, m])
                copy.start()
                copies.append(copy)
            fetches[n, k].wait()
            term = dot(weights[n, k], jnp.concatenate([high, high, low], axis=0))
            answer = term if answer is None else answer + term
        rim_sums.append(gathered(answer, out_rows))
    nothing = jnp.zeros((9 * out_rows, area), bf16)
    for part in range(2):
        spread_out[part, 0] = nothing
        spread_out[part, depth + 1] = nothing
    for plane in range(depth):
        value = total[plane]
        if plane == 0:
            value = value + rim_sums[0]
        if plane == depth - 1:
            value = value + rim_sums[1]
        positive = jnp.maximum(value, 0.0)
        kept_out[plane] = positive
        pre_grad = 2.0 * positive * grad[plane]
        for c in range(3):
            across = moved(pre_grad, 0, 1 - c)
            for b in range(3):
                high, low = parts_of(moved(across, 1 - b, 0))
                at = (3 * b + c) * out_rows
                spread_out[0, plane + 1, at : at + out_rows] = high
                spread_out[1, plane + 1, at : at + out_rows] = low
    for copy in copies:
        copy.wait()


def middle(ring, carry, grad, places, outer, weights, chan):
    total, high_all, low_all = carry
    depth, out_rows, area = total.shape
    keep = pl.BlockSpec(memory_space=pltpu.HBM)
    return pl.pallas_call(
        functools.partial(middle_kernel, places),
        grid_spec=pltpu.PrefetchScalarGridSpec(
            num_scalar_prefetch=1,
            grid=(1,),
            in_specs=[whole(x.shape) for x in (total, grad, *outer)]
            + [keep, keep, keep],
            out_specs=[
                whole((depth, out_rows, area)),
                whole((2, depth + 2, 9 * out_rows, area)),
                keep,
                keep,
            ],
            scratch_shapes=[
                pltpu.VMEM((2, len(places), chan, area), bf16),
                pltpu.VMEM((2, len(places), chan, area), bf16),
                pltpu.VMEM((2, len(places)) + weights.shape[2:], bf16),
                pltpu.SemaphoreType.DMA((2, len(places), 2)),
                pltpu.SemaphoreType.DMA((2, len(places))),
            ],
        ),
        out_shape=[
            jax.ShapeDtypeStruct((depth, out_rows, area), f32),
            jax.ShapeDtypeStruct((2, depth + 2, 9 * out_rows, area), bf16),
            jax.ShapeDtypeStruct(high_all.shape, bf16),
            jax.ShapeDtypeStruct(low_all.shape, bf16),
        ],
        input_output_aliases={6: 2, 7: 3},
        cost_estimate=cost(0, 4 * 18 * out_rows * depth * area),
        compiler_params=limit(),
        name="middle",
    )(ring, total, grad, *outer, weights, high_all, low_all)


def turn_kernel(square, x, out):
    value = x[...]
    out[...] = jnp.swapaxes(value * value if square else value, 0, 1)


def turned(x, square):
    a, b, area = x.shape
    return pl.pallas_call(
        functools.partial(turn_kernel, square),
        out_shape=jax.ShapeDtypeStruct((b, a, area), f32),
        cost_estimate=cost(0, 8 * x.size),
        compiler_params=limit(),
    )(x)


def inner_kernel(begin, planes, spread, high, low, out):
    deep = high.shape[1]
    count, chan, _ = out.shape
    area = spread.shape[3]
    group = 2 - planes % 2

    def some(i, nothing):
        for j in range(group):
            near = spread[0, pl.ds(begin + i * group + j, 3)].reshape(deep, area)
            far = spread[1, pl.ds(begin + i * group + j, 3)].reshape(deep, area)
            value = dot(high[...], near) + dot(high[...], far) + dot(low[...], near)
            lanes = pl.ds(pl.multiple_of((i * group + j) * area, area), area)
            out[:, :, lanes] = value.reshape(count, chan, area)
        return nothing

    lax.fori_loop(0, planes // group, some, 0)


def outer_kernel(spread, high, low, below, above):
    depth = spread.shape[1] - 2
    third = high.shape[1] // 3
    for out, plane, at in ((below, 1, 2 * third), (above, depth, 0)):
        lanes = slice(at, at + third)
        value = dot(high[:, lanes], spread[0, plane]) + dot(high[:, lanes], spread[1, plane])
        value = value + dot(low[:, lanes], spread[0, plane])
        out[...] = value.reshape(out.shape)


def inner_terms(begin, planes, spread, high, low, chan):
    channels, deep = high.shape
    area = spread.shape[3]
    return pl.pallas_call(
        functools.partial(inner_kernel, begin, planes),
        out_shape=jax.ShapeDtypeStruct((channels // chan, chan, planes * area), f32),
        cost_estimate=cost(6 * channels * deep * planes * area, 2 * spread.size + 4 * high.size),
        compiler_params=limit(),
        name="inner_terms",
    )(spread, high, low)


def outer_terms(spread, high, low, chan):
    channels, deep = high.shape
    shape = jax.ShapeDtypeStruct((channels // chan, chan, spread.shape[3]), f32)
    return pl.pallas_call(
        outer_kernel,
        out_shape=[shape, shape],
        cost_estimate=cost(4 * channels * deep * spread.shape[3], spread.size),
        compiler_params=limit(),
        name="outer_terms",
    )(spread, high, low)


def filter_kernel(tap, ring, spread, high, low, keep_out, send_out, total):
    depth = spread.shape[1] - 2
    rows, area = spread.shape[2:]
    half = rows // 2
    channels = high.shape[0]
    step = min(256, channels)
    for at in range(0, channels, step):
        value = None
        for plane in range(depth):
            lanes = slice((tap + plane) * area, (tap + plane + 1) * area)
            right = high[at : at + step, lanes]
            term = dot_t(spread[0, plane + 1], right) + dot_t(spread[1, plane + 1], right)
            term = term + dot_t(spread[0, plane + 1], low[at : at + step, lanes])
            value = term if value is None else value + term
        total[:, at : at + step] = value
    side = ring[ring.shape[0] - 1]
    mine = pl.multiple_of(side * half, half)
    other = pl.multiple_of((1 - side) * half, half)
    keep_out[...] = total[pl.ds(mine, half), :]
    send_out[...] = total[pl.ds(other, half), :]


def filter_terms(tap, ring, spread, high, low):
    rows = spread.shape[2]
    channels = high.shape[0]
    return pl.pallas_call(
        functools.partial(filter_kernel, tap),
        grid_spec=pltpu.PrefetchScalarGridSpec(
            num_scalar_prefetch=1,
            grid=(1,),
            in_specs=[whole(spread.shape), whole(high.shape), whole(low.shape)],
            out_specs=[whole((rows // 2, channels))] * 2,
            scratch_shapes=[pltpu.VMEM((rows, channels), f32)],
        ),
        out_shape=[jax.ShapeDtypeStruct((rows // 2, channels), f32)] * 2,
        cost_estimate=cost(6 * rows * high.size, 4 * high.size + 2 * spread.size),
        compiler_params=limit(),
        name="filter_terms",
    )(ring, spread, high, low)


def place_kernel(scale, ring, *refs):
    mine, other, out = refs[0], refs[1], refs[-1]
    half = mine.shape[0]
    side = ring[ring.shape[0] - 1]
    out[0, pl.ds(pl.multiple_of(side * half, half), half), :] = mine[...] / scale
    out[0, pl.ds(pl.multiple_of((1 - side) * half, half), half), :] = other[...] / scale


def place(tap, ring, mine, other, carry, scale):
    half, channels = mine.shape
    args = [mine, other]
    in_specs = [whole(mine.shape)] * 2
    aliases = {}
    if carry is not None:
        args.append(carry)
        in_specs.append(pl.BlockSpec(memory_space=pl.ANY))
        aliases = {3: 0}
    return pl.pallas_call(
        functools.partial(place_kernel, scale),
        grid_spec=pltpu.PrefetchScalarGridSpec(
            num_scalar_prefetch=1,
            grid=(1,),
            in_specs=in_specs,
            out_specs=pl.BlockSpec((1, 2 * half, channels), lambda i, s: (tap, 0, 0)),
        ),
        out_shape=jax.ShapeDtypeStruct((3, 2 * half, channels), f32),
        input_output_aliases=aliases,
        cost_estimate=cost(0, 16 * half * channels),
        compiler_params=limit(),
        name="place",
    )(ring, *args)


def local_sum(ring, inner, rim, first):
    value, rim = inner[0], beside(ring, 0 if first else 1, rim[0])
    area = rim.shape[1]
    width = value.shape[1]
    if first:
        return jnp.concatenate([value[:, :area] + rim, value[:, area:]], axis=1)
    return jnp.concatenate([value[:, : width - area], value[:, width - area :] + rim], axis=1)


def opening_kernel(first, ring, inner, rim, up_out, down_out):
    value = local_sum(ring, inner, rim, first)
    half = value.shape[0] // 2
    up_out[...] = value[:half]
    down_out[...] = value[half:]


def running_kernel(first, ring, up_inner, up_rim, down_inner, down_rim, up, down, up_out, down_out):
    value = local_sum(ring, up_inner, up_rim, first)
    size = up.shape[0]
    up_out[0:size] = value[0:size] + up[...]
    if size < value.shape[0]:
        up_out[size:] = value[size:]
    value = local_sum(ring, down_inner, down_rim, first)
    rest = value.shape[0] - size
    down_out[rest:] = value[rest:] + down[...]
    if rest:
        down_out[0:rest] = value[0:rest]


def closing_kernel(ring, *refs):
    chains, out = (refs[0:4], refs[4:8]), refs[8]
    area = out.shape[2]
    values = []
    for first, (inner, rim, up, down) in zip((True, False), chains):
        value = local_sum(ring, inner, rim, first) + up[...] + down[...]
        values += [value[:, at : at + area] for at in range(0, value.shape[1], area)]
    out[...] = jnp.swapaxes(jnp.stack(values), 0, 1)


def summed(kernel, ring, pieces, outs):
    specs, args = [], []
    for piece in pieces:
        if isinstance(piece, tuple):
            array, k = piece
            specs.append(pl.BlockSpec((1,) + array.shape[1:], lambda i, s, k=k: (s[k], 0, 0)))
            args.append(array)
        else:
            specs.append(whole(piece.shape))
            args.append(piece)
    return pl.pallas_call(
        kernel,
        grid_spec=pltpu.PrefetchScalarGridSpec(
            num_scalar_prefetch=1,
            grid=(1,),
            in_specs=specs,
            out_specs=[whole(o) for o in outs],
        ),
        out_shape=[jax.ShapeDtypeStruct(o, f32) for o in outs],
        cost_estimate=cost(0, sum(12 * math.prod(o) for o in outs)),
        compiler_params=limit(),
    )(ring, *args)


def shards(volume, filters, out_grad):
    chan, depth, area = volume.shape
    out_rows = filters.shape[1]
    channels = filters.shape[2]
    count = lax.axis_size("filt")
    slabs = lax.axis_size("slab")
    sizes = (depth, chan, area, channels, out_rows)

    order = list(range(0, count, 2)) + list(range(1, count, 2))[::-1]
    ring_up = [(order[i], order[(i + 1) % count]) for i in range(count)]
    ring_down = [(b, a) for a, b in ring_up]
    rows = [
        [order[(order.index(f) + k) % count] for k in range(count)]
        + [int(s > 0), int(s < slabs - 1), s % 2]
        for s in range(slabs)
        for f in range(count)
    ]
    here = lax.axis_index("slab") * count + lax.axis_index("filt")
    ring = lax.dynamic_index_in_dim(jnp.array(rows, jnp.int32), here, 0, keepdims=False)

    def send(x, pairs):
        return lax.ppermute(x, "filt", pairs)

    deeper = [(i, (i + 1) % slabs) for i in range(slabs)]
    shallower = [(b, a) for a, b in deeper]
    half = count // 2

    ahead, back_high, back_low = prepare(filters, chan)
    ahead = pltpu.with_memory_space_constraint(ahead, pltpu.HBM)

    carry = None
    up = down = volume
    rim_places, outer = (), None
    held, held_places = [], ()
    for step in range(half + 1):
        if step == 0:
            sets, places = [[volume]], (0,)
        elif step < half:
            up, down = send(up, ring_up), send(down, ring_down)
            sets, places = [[up], [down]], (count - step, step)
        else:
            up = send(up[: chan // 2], ring_up)
            down = send(down[chan // 2 :], ring_down)
            sets, places = [[up, down]], (half,)
        held += [b for blocks in sets for b in blocks]
        held_places += places
        carry = forward(ring, sets, places, rim_places, outer, ahead, carry, sizes)
        rim_places, outer = (), None
        if step not in (0, half - 1):
            last, top = rims(held)
            outer = lax.ppermute(last, "slab", deeper), lax.ppermute(top, "slab", shallower)
            rim_places, held, held_places = held_places, [], ()

    grads = turned(out_grad, False)
    positives, spread, high_field, low_field = middle(
        ring, carry, grads, rim_places, outer, ahead, chan
    )
    activated = turned(positives, True)

    below, above = outer_terms(spread, back_high, back_low, chan)
    from_below = lax.ppermute(above, "slab", deeper)
    from_above = lax.ppermute(below, "slab", shallower)
    run = depth // 2
    inner = []
    for c in range(2):
        inner.append(inner_terms(c * run, run, spread, back_high, back_low, chan))
    edge = [from_below, from_above]

    scale = math.sqrt(depth * slabs * area)

    def swap(x, bit):
        return lax.ppermute(x, "slab", [(i, i ^ bit) for i in range(slabs)])

    weight_grad = None
    for tap in range(3):
        keep, give = filter_terms(tap, ring, spread, high_field, low_field)
        keep = keep + swap(give, 1)
        bit = 2
        while bit < slabs:
            keep = keep + swap(keep, bit)
            bit *= 2
        other = swap(keep, 1)
        weight_grad = place(tap, ring, keep, other, weight_grad, scale)

    piece = (chan, run * area)
    part = (chan // 2, run * area)
    flows = []
    for c in range(2):
        kernel = functools.partial(opening_kernel, c == 0)
        flows.append(summed(kernel, ring, [(inner[c], half), (edge[c], half)], [part, part]))
    for step in range(half - 1, 0, -1):
        for c in range(2):
            up, down = flows[c]
            up, down = send(up, ring_up), send(down, ring_down)
            kernel = functools.partial(running_kernel, c == 0)
            pieces = [(x, p) for p in (step, count - step) for x in (inner[c], edge[c])]
            flows[c] = summed(kernel, ring, pieces + [up, down], [piece, piece])
    pieces = []
    for c in range(2):
        up, down = flows[c]
        pieces += [(inner[c], 0), (edge[c], 0), send(up, ring_up), send(down, ring_down)]
    (input_grad,) = summed(closing_kernel, ring, pieces, [(chan, depth, area)])
    return activated, input_grad, weight_grad.reshape(filters.shape)


def solution(mesh):
    placed = (P("filt", "slab", None), P(None, "filt", None), P("filt", "slab", None))

    def step(*args):
        return shards(*args)

    step = jax.shard_map(
        step,
        mesh=mesh,
        in_specs=placed,
        out_specs=(P("filt", "slab", None), P("filt", "slab", None), P(None, "filt", None)),
        check_vma=False,
    )
    return step
```

```python
import functools
import math

import jax
import jax.numpy as jnp
from jax import lax
from jax.experimental import pallas as pl
from jax.experimental.pallas import tpu as pltpu
from jax.sharding import PartitionSpec as P


WIDTH = 16


f32 = jnp.float32
bf16 = jnp.bfloat16


def parts_of(x):
    high = x.astype(bf16)
    low = (x - high.astype(f32)).astype(bf16)
    return high, low


def dot(a, b):
    return lax.dot_general(a, b, (((1,), (0,)), ((), ())), preferred_element_type=f32)


def dot_t(a, b):
    return lax.dot_general(a, b, (((1,), (1,)), ((), ())), preferred_element_type=f32)


def beside(ring, n, rim):
    return jnp.where(ring[ring.shape[0] - 3 + n] > 0, rim, 0.0)


def whole(shape):
    return pl.BlockSpec(shape, lambda *_: (0,) * len(shape))


def limit():
    return pltpu.CompilerParams(vmem_limit_bytes=28 * 2**20)


def cost(flops, moved):
    return pl.CostEstimate(flops=int(flops), bytes_accessed=int(moved), transcendentals=0)


def moved(x, down, across):
    size = x.shape[-1]
    place = lax.broadcasted_iota(jnp.int32, x.shape, 1)
    if across:
        column = place % WIDTH + across
        rolled = pltpu.roll(x, (-across) % size, 1)
        x = jnp.where((column >= 0) & (column < WIDTH), rolled, 0.0)
    if down:
        target = place + down * WIDTH
        rolled = pltpu.roll(x, (-down * WIDTH) % size, 1)
        x = jnp.where((target >= 0) & (target < size), rolled, 0.0)
    return x


def prepare_kernel(chan, filters, ahead, back_high, back_low):
    taps, out_rows, lanes = filters.shape
    third = taps * out_rows // 3
    for a in range(3):
        x = filters[a * 9 : (a + 1) * 9].reshape(third, lanes)
        high, low = parts_of(x)
        for k in range(lanes // chan):
            at = slice(k * chan, (k + 1) * chan)
            ahead[a, k] = jnp.concatenate([high[:, at], low[:, at], high[:, at]], axis=1)
    turned = [filters[a * 9 : (a + 1) * 9].reshape(third, lanes).T for a in (2, 1, 0)]
    high, low = parts_of(jnp.concatenate(turned, axis=1))
    back_high[...] = high
    back_low[...] = low


def prepare(filters, chan):
    taps, out_rows, channels = filters.shape
    lanes = min(128, channels)
    each = lanes // chan
    return pl.pallas_call(
        functools.partial(prepare_kernel, chan),
        grid=(channels // lanes,),
        in_specs=[pl.BlockSpec((taps, out_rows, lanes), lambda i: (0, 0, i))],
        out_specs=[
            pl.BlockSpec((3, each, 9 * out_rows, 3 * chan), lambda i: (0, i, 0, 0)),
            pl.BlockSpec((lanes, taps * out_rows), lambda i: (i, 0)),
            pl.BlockSpec((lanes, taps * out_rows), lambda i: (i, 0)),
        ],
        out_shape=[
            jax.ShapeDtypeStruct((3, channels // chan, 9 * out_rows, 3 * chan), bf16),
            jax.ShapeDtypeStruct((channels, taps * out_rows), bf16),
            jax.ShapeDtypeStruct((channels, taps * out_rows), bf16),
        ],
        cost_estimate=cost(0, 5 * 4 * filters.size),
        name="prepare",
    )(filters)


def rims_kernel(*refs):
    blocks, (last, top) = refs[:-2], refs[-2:]
    at = 0
    for block in blocks:
        rows, depth, _ = block.shape
        planes = jnp.swapaxes(block[...], 0, 1)
        last[at : at + rows] = planes[depth - 1]
        top[at : at + rows] = planes[0]
        at += rows


def rims(blocks):
    rows = sum(b.shape[0] for b in blocks)
    shape = jax.ShapeDtypeStruct((rows, blocks[0].shape[2]), f32)
    return pl.pallas_call(
        rims_kernel,
        out_shape=[shape, shape],
        cost_estimate=cost(0, 4 * sum(b.size for b in blocks)),
        compiler_params=limit(),
        name="rims",
    )(*blocks)


def gathered(answer, out_rows):
    rows = []
    for b in range(3):
        row = None
        for c in range(3):
            at = (3 * b + c) * out_rows
            term = moved(answer[at : at + out_rows], 0, c - 1)
            row = term if row is None else row + term
        rows.append(moved(row, b - 1, 0))
    return rows[0] + rows[1] + rows[2]


def forward_kernel(counts, places, rim_places, first, ring, *refs):
    refs = list(refs)

    def take(n):
        taken = refs[:n]
        del refs[:n]
        return taken

    blocks = take(sum(counts))
    (source,) = take(1)
    rims_in = take(2) if rim_places else []
    total_in = None if first else take(3)[0]
    total_out, high_all, low_all, field, high_part, low_part, high_rim, low_rim = take(8)
    weights, rim_weights, sems, fetch_sems = refs
    fetches = [
        pltpu.make_async_copy(source.at[:, ring[place]], weights.at[k], fetch_sems.at[k])
        for k, place in enumerate(places)
    ]
    for k, place in enumerate(rim_places):
        for n in range(2):
            sem = fetch_sems.at[len(fetches)]
            fetches.append(
                pltpu.make_async_copy(source.at[2 * n, ring[place]], rim_weights.at[n, k], sem)
            )
    for fetch in fetches:
        fetch.start()
    depth, out_rows, area = total_out.shape
    chan = field.shape[2] // 3
    copies = []

    def keep(part, target, place, lanes):
        at = pl.ds(pl.multiple_of(ring[place] * chan, chan), chan)
        copies.append(pltpu.make_async_copy(part, target.at[at, lanes], sems.at[len(copies)]))
        copies[-1].start()

    begin = 0
    for k, pieces in enumerate(counts):
        loaded = [jnp.swapaxes(b[...], 0, 1) for b in blocks[begin : begin + pieces]]
        begin += pieces
        for plane in range(depth):
            rows = [b[plane] for b in loaded]
            x = rows[0] if pieces == 1 else jnp.concatenate(rows, axis=0)
            high, low = parts_of(x)
            field[k, plane, 0:chan] = high
            field[k, plane, chan : 2 * chan] = high
            field[k, plane, 2 * chan : 3 * chan] = low
            high_part[k, :, plane * area : (plane + 1) * area] = high
            low_part[k, :, plane * area : (plane + 1) * area] = low
        lanes = pl.ds(area, depth * area)
        keep(high_part.at[k], high_all, places[k], lanes)
        keep(low_part.at[k], low_all, places[k], lanes)
    for n, rim in enumerate(rims_in):
        lanes = pl.ds(n * (depth + 1) * area, area)
        for k in range(len(rim_places)):
            high, low = parts_of(beside(ring, n, rim[k * chan : (k + 1) * chan]))
            high_rim[n, k] = high
            low_rim[n, k] = low
            keep(high_rim.at[n, k], high_all, rim_places[k], lanes)
            keep(low_rim.at[n, k], low_all, rim_places[k], lanes)

    for fetch in fetches:
        fetch.wait()
    for plane in range(depth):
        terms = []
        for a in range(3):
            if 0 <= plane + a - 1 < depth:
                for k in range(len(counts)):
                    terms.append((weights[k, a], field[k, plane + a - 1]))
        for n, edge in enumerate((0, depth - 1)):
            if plane == edge:
                for k in range(len(rim_places)):
                    right = [high_rim[n, k], high_rim[n, k], low_rim[n, k]]
                    terms.append((rim_weights[n, k], jnp.concatenate(right, axis=0)))
        answer = None
        for left, right in terms:
            term = dot(left, right)
            answer = term if answer is None else answer + term
        total = gathered(answer, out_rows)
        if total_in is not None:
            total = total + total_in[plane]
        total_out[plane] = total
    for copy in copies:
        copy.wait()


def forward(ring, sets, places, rim_places, outer, weights, carry, sizes):
    depth, chan, area, channels, out_rows = sizes
    counts = tuple(len(s) for s in sets)
    blocks = [b for s in sets for b in s]
    first = carry is None
    lanes = (depth + 2) * area
    keep = pl.BlockSpec(memory_space=pltpu.HBM)
    in_specs = [whole(b.shape) for b in blocks]
    args = list(blocks)
    in_specs.append(keep)
    args.append(weights)
    if rim_places:
        in_specs += [whole(o.shape) for o in outer]
        args += list(outer)
    aliases = {}
    if not first:
        base = len(args) + 1
        in_specs += [whole((depth, out_rows, area)), keep, keep]
        args += list(carry)
        aliases = {base: 0, base + 1: 1, base + 2: 2}
    rims_held = max(1, len(rim_places))
    return pl.pallas_call(
        functools.partial(forward_kernel, counts, places, rim_places, first),
        grid_spec=pltpu.PrefetchScalarGridSpec(
            num_scalar_prefetch=1,
            grid=(1,),
            in_specs=in_specs,
            out_specs=[whole((depth, out_rows, area)), keep, keep],
            scratch_shapes=[
                pltpu.VMEM((len(sets), depth, 3 * chan, area), bf16),
                pltpu.VMEM((len(sets), chan, depth * area), bf16),
                pltpu.VMEM((len(sets), chan, depth * area), bf16),
                pltpu.VMEM((2, rims_held, chan, area), bf16),
                pltpu.VMEM((2, rims_held, chan, area), bf16),
                pltpu.VMEM((len(sets), 3) + weights.shape[2:], bf16),
                pltpu.VMEM((2, rims_held) + weights.shape[2:], bf16),
                pltpu.SemaphoreType.DMA((2 * len(sets) + 4 * rims_held,)),
                pltpu.SemaphoreType.DMA((len(sets) + 2 * rims_held,)),
            ],
        ),
        out_shape=[
            jax.ShapeDtypeStruct((depth, out_rows, area), f32),
            jax.ShapeDtypeStruct((channels, lanes), bf16),
            jax.ShapeDtypeStruct((channels, lanes), bf16),
        ],
        input_output_aliases=aliases,
        cost_estimate=cost(
            len(sets) * 2 * 81 * out_rows * chan * depth * area, len(sets) * 8 * chan * lanes
        ),
        compiler_params=limit(),
        name="forward",
    )(ring, *args)


def middle_kernel(places, ring, total, grad, below, above, source, *refs):
    kept_out, spread_out, high_all, low_all, high_rim, low_rim, weights, sems, fetch_sems = refs[2:]
    depth, out_rows, area = total.shape
    chan = below.shape[0] // len(places)
    copies = []
    fetches = {}
    for n in range(2):
        for k, place in enumerate(places):
            fetches[n, k] = pltpu.make_async_copy(
                source.at[2 * n, ring[place]], weights.at[n, k], fetch_sems.at[n, k]
            )
            fetches[n, k].start()
    nothing = jnp.zeros((9 * out_rows, area), bf16)
    for part in range(2):
        spread_out[part, 0] = nothing
        spread_out[part, depth + 1] = nothing

    def finish(plane, value):
        positive = jnp.maximum(value, 0.0)
        kept_out[plane] = positive
        pre_grad = 2.0 * positive * grad[plane]
        for c in range(3):
            across = moved(pre_grad, 0, 1 - c)
            for b in range(3):
                high, low = parts_of(moved(across, 1 - b, 0))
                at = (3 * b + c) * out_rows
                spread_out[0, plane + 1, at : at + out_rows] = high
                spread_out[1, plane + 1, at : at + out_rows] = low

    for plane in range(1, depth - 1):
        finish(plane, total[plane])
    for n, rim in enumerate((below, above)):
        answer = None
        for k, place in enumerate(places):
            value = beside(ring, n, rim[k * chan : (k + 1) * chan])
            high, low = parts_of(value)
            high_rim[n, k] = high
            low_rim[n, k] = low
            at = pl.ds(pl.multiple_of(ring[place] * chan, chan), chan)
            lanes = pl.ds(n * (depth + 1) * area, area)
            for m, (part, target) in enumerate(((high_rim, high_all), (low_rim, low_all))):
                copy = pltpu.make_async_copy(part.at[n, k], target.at[at, lanes], sems.at[n, k, m])
                copy.start()
                copies.append(copy)
            fetches[n, k].wait()
            term = dot(weights[n, k], jnp.concatenate([high, high, low], axis=0))
            answer = term if answer is None else answer + term
        edge = n * (depth - 1)
        finish(edge, total[edge] + gathered(answer, out_rows))
    for copy in copies:
        copy.wait()


def middle(ring, carry, grad, places, outer, weights, chan):
    total, high_all, low_all = carry
    depth, out_rows, area = total.shape
    keep = pl.BlockSpec(memory_space=pltpu.HBM)
    return pl.pallas_call(
        functools.partial(middle_kernel, places),
        grid_spec=pltpu.PrefetchScalarGridSpec(
            num_scalar_prefetch=1,
            grid=(1,),
            in_specs=[whole(x.shape) for x in (total, grad, *outer)]
            + [keep, keep, keep],
            out_specs=[
                whole((depth, out_rows, area)),
                whole((2, depth + 2, 9 * out_rows, area)),
                keep,
                keep,
            ],
            scratch_shapes=[
                pltpu.VMEM((2, len(places), chan, area), bf16),
                pltpu.VMEM((2, len(places), chan, area), bf16),
                pltpu.VMEM((2, len(places)) + weights.shape[2:], bf16),
                pltpu.SemaphoreType.DMA((2, len(places), 2)),
                pltpu.SemaphoreType.DMA((2, len(places))),
            ],
        ),
        out_shape=[
            jax.ShapeDtypeStruct((depth, out_rows, area), f32),
            jax.ShapeDtypeStruct((2, depth + 2, 9 * out_rows, area), bf16),
            jax.ShapeDtypeStruct(high_all.shape, bf16),
            jax.ShapeDtypeStruct(low_all.shape, bf16),
        ],
        input_output_aliases={6: 2, 7: 3},
        cost_estimate=cost(0, 4 * 18 * out_rows * depth * area),
        compiler_params=limit(),
        name="middle",
    )(ring, total, grad, *outer, weights, high_all, low_all)


def turn_kernel(square, x, out):
    value = x[...]
    out[...] = jnp.swapaxes(value * value if square else value, 0, 1)


def turned(x, square):
    a, b, area = x.shape
    return pl.pallas_call(
        functools.partial(turn_kernel, square),
        out_shape=jax.ShapeDtypeStruct((b, a, area), f32),
        cost_estimate=cost(0, 8 * x.size),
        compiler_params=limit(),
    )(x)


def inner_kernel(begin, planes, spread, high, low, out):
    deep = high.shape[1]
    count, chan, _ = out.shape
    area = spread.shape[3]
    group = 2 - planes % 2

    def some(i, nothing):
        for j in range(group):
            near = spread[0, pl.ds(begin + i * group + j, 3)].reshape(deep, area)
            far = spread[1, pl.ds(begin + i * group + j, 3)].reshape(deep, area)
            value = dot(high[...], near) + dot(high[...], far) + dot(low[...], near)
            lanes = pl.ds(pl.multiple_of((i * group + j) * area, area), area)
            out[:, :, lanes] = value.reshape(count, chan, area)
        return nothing

    lax.fori_loop(0, planes // group, some, 0)


def outer_kernel(spread, high, low, below, above):
    depth = spread.shape[1] - 2
    third = high.shape[1] // 3
    for out, plane, at in ((below, 1, 2 * third), (above, depth, 0)):
        lanes = slice(at, at + third)
        value = dot(high[:, lanes], spread[0, plane]) + dot(high[:, lanes], spread[1, plane])
        value = value + dot(low[:, lanes], spread[0, plane])
        out[...] = value.reshape(out.shape)


def inner_terms(begin, planes, spread, high, low, chan):
    channels, deep = high.shape
    area = spread.shape[3]
    return pl.pallas_call(
        functools.partial(inner_kernel, begin, planes),
        out_shape=jax.ShapeDtypeStruct((channels // chan, chan, planes * area), f32),
        cost_estimate=cost(6 * channels * deep * planes * area, 2 * spread.size + 4 * high.size),
        compiler_params=limit(),
        name="inner_terms",
    )(spread, high, low)


def outer_terms(spread, high, low, chan):
    channels, deep = high.shape
    shape = jax.ShapeDtypeStruct((channels // chan, chan, spread.shape[3]), f32)
    return pl.pallas_call(
        outer_kernel,
        out_shape=[shape, shape],
        cost_estimate=cost(4 * channels * deep * spread.shape[3], spread.size),
        compiler_params=limit(),
        name="outer_terms",
    )(spread, high, low)


def filter_kernel(begin, end, scale, ring, spread, high, low, keep_out, send_out, total):
    depth = spread.shape[1] - 2
    area = spread.shape[3]
    out_rows = spread.shape[2] // 9
    half = (end - begin) * out_rows // 2
    channels = high.shape[0]
    step = min(256, channels)
    for a in range(3):
        first, last = max(begin, 9 * a), min(end, 9 * a + 9)
        if first >= last:
            continue
        rows = slice((first - 9 * a) * out_rows, (last - 9 * a) * out_rows)
        into = slice((first - begin) * out_rows, (last - begin) * out_rows)
        for at in range(0, channels, step):
            value = None
            for plane in range(depth):
                lanes = slice((a + plane) * area, (a + plane + 1) * area)
                right = high[at : at + step, lanes]
                near = spread[0, plane + 1, rows]
                term = dot_t(near, right) + dot_t(spread[1, plane + 1, rows], right)
                term = term + dot_t(near, low[at : at + step, lanes])
                value = term if value is None else value + term
            total[into, at : at + step] = value * (1.0 / scale)
    side = ring[ring.shape[0] - 1]
    keep_out[...] = total[pl.ds(pl.multiple_of(side * half, half), half), :]
    send_out[...] = total[pl.ds(pl.multiple_of((1 - side) * half, half), half), :]


def filter_terms(begin, end, scale, ring, spread, high, low):
    channels = high.shape[0]
    rows = (end - begin) * (spread.shape[2] // 9)
    return pl.pallas_call(
        functools.partial(filter_kernel, begin, end, scale),
        grid_spec=pltpu.PrefetchScalarGridSpec(
            num_scalar_prefetch=1,
            grid=(1,),
            in_specs=[whole(spread.shape), whole(high.shape), whole(low.shape)],
            out_specs=[whole((rows // 2, channels))] * 2,
            scratch_shapes=[pltpu.VMEM((rows, channels), f32)],
        ),
        out_shape=[jax.ShapeDtypeStruct((rows // 2, channels), f32)] * 2,
        cost_estimate=cost(6 * rows * high.size, 4 * high.size + 2 * spread.size),
        compiler_params=limit(),
        name="filter_terms",
    )(ring, spread, high, low)


def place_kernel(begin, ring, *refs):
    mine, other, out, sems = refs[0], refs[1], refs[-2], refs[-1]
    half = mine.shape[0]
    side = ring[ring.shape[0] - 1]
    copies = []
    for n, (part, at) in enumerate(((mine, side), (other, 1 - side))):
        rows = pl.ds(pl.multiple_of(begin + at * half, 8), half)
        copies.append(pltpu.make_async_copy(part, out.at[rows], sems.at[n]))
        copies[-1].start()
    for copy in copies:
        copy.wait()


def place(begin, ring, mine, other, carry, rows):
    half, channels = mine.shape
    keep = pl.BlockSpec(memory_space=pltpu.HBM)
    args = [mine, other]
    in_specs = [whole(mine.shape)] * 2
    aliases = {}
    if carry is not None:
        args.append(carry)
        in_specs.append(keep)
        aliases = {3: 0}
    return pl.pallas_call(
        functools.partial(place_kernel, begin),
        grid_spec=pltpu.PrefetchScalarGridSpec(
            num_scalar_prefetch=1,
            grid=(1,),
            in_specs=in_specs,
            out_specs=keep,
            scratch_shapes=[pltpu.SemaphoreType.DMA((2,))],
        ),
        out_shape=jax.ShapeDtypeStruct((rows, channels), f32),
        input_output_aliases=aliases,
        cost_estimate=cost(0, 16 * half * channels),
        compiler_params=limit(),
        name="place",
    )(ring, *args)


def local_sum(ring, inner, rim, first):
    value, rim = inner[0], beside(ring, 0 if first else 1, rim[0])
    area = rim.shape[1]
    width = value.shape[1]
    if first:
        return jnp.concatenate([value[:, :area] + rim, value[:, area:]], axis=1)
    return jnp.concatenate([value[:, : width - area], value[:, width - area :] + rim], axis=1)


def opening_kernel(first, ring, inner, rim, up_out, down_out):
    value = local_sum(ring, inner, rim, first)
    half = value.shape[0] // 2
    up_out[...] = value[:half]
    down_out[...] = value[half:]


def running_kernel(first, ring, up_inner, up_rim, down_inner, down_rim, up, down, up_out, down_out):
    value = local_sum(ring, up_inner, up_rim, first)
    size = up.shape[0]
    up_out[0:size] = value[0:size] + up[...]
    if size < value.shape[0]:
        up_out[size:] = value[size:]
    value = local_sum(ring, down_inner, down_rim, first)
    rest = value.shape[0] - size
    down_out[rest:] = value[rest:] + down[...]
    if rest:
        down_out[0:rest] = value[0:rest]


def closing_kernel(ring, *refs):
    chains, out = (refs[0:4], refs[4:8]), refs[8]
    area = out.shape[2]
    values = []
    for first, (inner, rim, up, down) in zip((True, False), chains):
        value = local_sum(ring, inner, rim, first) + up[...] + down[...]
        values += [value[:, at : at + area] for at in range(0, value.shape[1], area)]
    out[...] = jnp.swapaxes(jnp.stack(values), 0, 1)


def summed(kernel, ring, pieces, outs):
    specs, args = [], []
    for piece in pieces:
        if isinstance(piece, tuple):
            array, k = piece
            specs.append(pl.BlockSpec((1,) + array.shape[1:], lambda i, s, k=k: (s[k], 0, 0)))
            args.append(array)
        else:
            specs.append(whole(piece.shape))
            args.append(piece)
    return pl.pallas_call(
        kernel,
        grid_spec=pltpu.PrefetchScalarGridSpec(
            num_scalar_prefetch=1,
            grid=(1,),
            in_specs=specs,
            out_specs=[whole(o) for o in outs],
        ),
        out_shape=[jax.ShapeDtypeStruct(o, f32) for o in outs],
        cost_estimate=cost(0, sum(12 * math.prod(o) for o in outs)),
        compiler_params=limit(),
    )(ring, *args)


def shards(volume, filters, out_grad):
    chan, depth, area = volume.shape
    out_rows = filters.shape[1]
    channels = filters.shape[2]
    count = lax.axis_size("filt")
    slabs = lax.axis_size("slab")
    sizes = (depth, chan, area, channels, out_rows)

    order = list(range(0, count, 2)) + list(range(1, count, 2))[::-1]
    ring_up = [(order[i], order[(i + 1) % count]) for i in range(count)]
    ring_down = [(b, a) for a, b in ring_up]
    rows = [
        [order[(order.index(f) + k) % count] for k in range(count)]
        + [int(s > 0), int(s < slabs - 1), s % 2]
        for s in range(slabs)
        for f in range(count)
    ]
    here = lax.axis_index("slab") * count + lax.axis_index("filt")
    ring = lax.dynamic_index_in_dim(jnp.array(rows, jnp.int32), here, 0, keepdims=False)

    def send(x, pairs):
        return lax.ppermute(x, "filt", pairs)

    deeper = [(i, (i + 1) % slabs) for i in range(slabs)]
    shallower = [(b, a) for a, b in deeper]
    half = count // 2

    ahead, back_high, back_low = prepare(filters, chan)
    ahead = pltpu.with_memory_space_constraint(ahead, pltpu.HBM)

    carry = None
    up = down = volume
    rim_places, outer = (), None
    held, held_places = [], ()
    for step in range(half + 1):
        if step == 0:
            sets, places = [[volume]], (0,)
        elif step < half:
            up, down = send(up, ring_up), send(down, ring_down)
            sets, places = [[up], [down]], (count - step, step)
        else:
            up = send(up[: chan // 2], ring_up)
            down = send(down[chan // 2 :], ring_down)
            sets, places = [[up, down]], (half,)
        held += [b for blocks in sets for b in blocks]
        held_places += places
        carry = forward(ring, sets, places, rim_places, outer, ahead, carry, sizes)
        rim_places, outer = (), None
        if step not in (0, half - 1):
            last, top = rims(held)
            outer = lax.ppermute(last, "slab", deeper), lax.ppermute(top, "slab", shallower)
            rim_places, held, held_places = held_places, [], ()

    grads = turned(out_grad, False)
    positives, spread, high_field, low_field = middle(
        ring, carry, grads, rim_places, outer, ahead, chan
    )
    activated = turned(positives, True)

    below, above = outer_terms(spread, back_high, back_low, chan)
    from_below = lax.ppermute(above, "slab", deeper)
    from_above = lax.ppermute(below, "slab", shallower)
    run = depth // 2
    inner = []
    for c in range(2):
        inner.append(inner_terms(c * run, run, spread, back_high, back_low, chan))
    edge = [from_below, from_above]

    scale = math.sqrt(depth * slabs * area)

    def swap(x, bit):
        return lax.ppermute(x, "slab", [(i, i ^ bit) for i in range(slabs)])

    weight_grad = None
    taps = filters.shape[0]
    cuts = (0, 12, 18, taps)
    for begin, end in zip(cuts, cuts[1:]):
        keep, give = filter_terms(begin, end, scale, ring, spread, high_field, low_field)
        keep = keep + swap(give, 1)
        bit = 2
        while bit < slabs:
            keep = keep + swap(keep, bit)
            bit *= 2
        other = swap(keep, 1)
        weight_grad = place(
            begin * out_rows, ring, keep, other, weight_grad, taps * out_rows
        )

    piece = (chan, run * area)
    part = (chan // 2, run * area)
    flows = []
    for c in range(2):
        kernel = functools.partial(opening_kernel, c == 0)
        flows.append(summed(kernel, ring, [(inner[c], half), (edge[c], half)], [part, part]))
    for step in range(half - 1, 0, -1):
        for c in range(2):
            up, down = flows[c]
            up, down = send(up, ring_up), send(down, ring_down)
            kernel = functools.partial(running_kernel, c == 0)
            pieces = [(x, p) for p in (step, count - step) for x in (inner[c], edge[c])]
            flows[c] = summed(kernel, ring, pieces + [up, down], [piece, piece])
    pieces = []
    for c in range(2):
        up, down = flows[c]
        pieces += [(inner[c], 0), (edge[c], 0), send(up, ring_up), send(down, ring_down)]
    (input_grad,) = summed(closing_kernel, ring, pieces, [(chan, depth, area)])
    return activated, input_grad, weight_grad.reshape(filters.shape)


def solution(mesh):
    placed = (P("filt", "slab", None), P(None, "filt", None), P("filt", "slab", None))

    def step(*args):
        return shards(*args)

    step = jax.shard_map(
        step,
        mesh=mesh,
        in_specs=placed,
        out_specs=(P("filt", "slab", None), P("filt", "slab", None), P(None, "filt", None)),
        check_vma=False,
    )
    return step
```

```python
import functools
import math

import jax
import jax.numpy as jnp
from jax import lax
from jax.experimental import pallas as pl
from jax.experimental.pallas import tpu as pltpu
from jax.sharding import PartitionSpec as P


WIDTH = 16


f32 = jnp.float32
bf16 = jnp.bfloat16


def parts_of(x):
    high = x.astype(bf16)
    low = (x - high.astype(f32)).astype(bf16)
    return high, low


def dot(a, b):
    return lax.dot_general(a, b, (((1,), (0,)), ((), ())), preferred_element_type=f32)


def dot_t(a, b):
    return lax.dot_general(a, b, (((1,), (1,)), ((), ())), preferred_element_type=f32)


def beside(ring, n, rim):
    return jnp.where(ring[ring.shape[0] - 3 + n] > 0, rim, 0.0)


def whole(shape):
    return pl.BlockSpec(shape, lambda *_: (0,) * len(shape))


def limit():
    return pltpu.CompilerParams(vmem_limit_bytes=28 * 2**20)


def cost(flops, moved):
    return pl.CostEstimate(flops=int(flops), bytes_accessed=int(moved), transcendentals=0)


def moved(x, down, across):
    size = x.shape[-1]
    place = lax.broadcasted_iota(jnp.int32, x.shape, 1)
    if across:
        column = place % WIDTH + across
        rolled = pltpu.roll(x, (-across) % size, 1)
        x = jnp.where((column >= 0) & (column < WIDTH), rolled, 0.0)
    if down:
        target = place + down * WIDTH
        rolled = pltpu.roll(x, (-down * WIDTH) % size, 1)
        x = jnp.where((target >= 0) & (target < size), rolled, 0.0)
    return x


def prepare_kernel(chan, filters, ahead, back_high, back_low):
    taps, out_rows, lanes = filters.shape
    third = taps * out_rows // 3
    for a in range(3):
        x = filters[a * 9 : (a + 1) * 9].reshape(third, lanes)
        high, low = parts_of(x)
        for k in range(lanes // chan):
            at = slice(k * chan, (k + 1) * chan)
            ahead[a, k] = jnp.concatenate([high[:, at], low[:, at], high[:, at]], axis=1)
    turned = [filters[a * 9 : (a + 1) * 9].reshape(third, lanes).T for a in (2, 1, 0)]
    high, low = parts_of(jnp.concatenate(turned, axis=1))
    back_high[...] = high
    back_low[...] = low


def prepare(filters, chan):
    taps, out_rows, channels = filters.shape
    lanes = min(128, channels)
    each = lanes // chan
    return pl.pallas_call(
        functools.partial(prepare_kernel, chan),
        grid=(channels // lanes,),
        in_specs=[pl.BlockSpec((taps, out_rows, lanes), lambda i: (0, 0, i))],
        out_specs=[
            pl.BlockSpec((3, each, 9 * out_rows, 3 * chan), lambda i: (0, i, 0, 0)),
            pl.BlockSpec((lanes, taps * out_rows), lambda i: (i, 0)),
            pl.BlockSpec((lanes, taps * out_rows), lambda i: (i, 0)),
        ],
        out_shape=[
            jax.ShapeDtypeStruct((3, channels // chan, 9 * out_rows, 3 * chan), bf16),
            jax.ShapeDtypeStruct((channels, taps * out_rows), bf16),
            jax.ShapeDtypeStruct((channels, taps * out_rows), bf16),
        ],
        cost_estimate=cost(0, 5 * 4 * filters.size),
        name="prepare",
    )(filters)


def rims_kernel(*refs):
    blocks, (last, top) = refs[:-2], refs[-2:]
    at = 0
    for block in blocks:
        rows, depth, _ = block.shape
        planes = jnp.swapaxes(block[...], 0, 1)
        last[at : at + rows] = planes[depth - 1]
        top[at : at + rows] = planes[0]
        at += rows


def rims(blocks):
    rows = sum(b.shape[0] for b in blocks)
    shape = jax.ShapeDtypeStruct((rows, blocks[0].shape[2]), f32)
    return pl.pallas_call(
        rims_kernel,
        out_shape=[shape, shape],
        cost_estimate=cost(0, 4 * sum(b.size for b in blocks)),
        compiler_params=limit(),
        name="rims",
    )(*blocks)


def gathered(answer, out_rows):
    rows = []
    for b in range(3):
        row = None
        for c in range(3):
            at = (3 * b + c) * out_rows
            term = moved(answer[at : at + out_rows], 0, c - 1)
            row = term if row is None else row + term
        rows.append(moved(row, b - 1, 0))
    return rows[0] + rows[1] + rows[2]


def forward_kernel(counts, places, rim_places, first, ring, *refs):
    refs = list(refs)

    def take(n):
        taken = refs[:n]
        del refs[:n]
        return taken

    blocks = take(sum(counts))
    (source,) = take(1)
    rims_in = take(2) if rim_places else []
    total_in = None if first else take(3)[0]
    total_out, high_all, low_all, field, high_part, low_part, high_rim, low_rim = take(8)
    weights, rim_weights, sems, fetch_sems = refs
    fetches = [
        pltpu.make_async_copy(source.at[:, ring[place]], weights.at[k], fetch_sems.at[k])
        for k, place in enumerate(places)
    ]
    for k, place in enumerate(rim_places):
        for n in range(2):
            sem = fetch_sems.at[len(fetches)]
            fetches.append(
                pltpu.make_async_copy(source.at[2 * n, ring[place]], rim_weights.at[n, k], sem)
            )
    for fetch in fetches:
        fetch.start()
    depth, out_rows, area = total_out.shape
    chan = field.shape[2] // 3
    copies = []

    def keep(part, target, place, lanes):
        at = pl.ds(pl.multiple_of(ring[place] * chan, chan), chan)
        copies.append(pltpu.make_async_copy(part, target.at[at, lanes], sems.at[len(copies)]))
        copies[-1].start()

    begin = 0
    for k, pieces in enumerate(counts):
        loaded = [jnp.swapaxes(b[...], 0, 1) for b in blocks[begin : begin + pieces]]
        begin += pieces
        for plane in range(depth):
            rows = [b[plane] for b in loaded]
            x = rows[0] if pieces == 1 else jnp.concatenate(rows, axis=0)
            high, low = parts_of(x)
            field[k, plane, 0:chan] = high
            field[k, plane, chan : 2 * chan] = high
            field[k, plane, 2 * chan : 3 * chan] = low
            high_part[k, :, plane * area : (plane + 1) * area] = high
            low_part[k, :, plane * area : (plane + 1) * area] = low
        lanes = pl.ds(area, depth * area)
        keep(high_part.at[k], high_all, places[k], lanes)
        keep(low_part.at[k], low_all, places[k], lanes)
    for n, rim in enumerate(rims_in):
        lanes = pl.ds(n * (depth + 1) * area, area)
        for k in range(len(rim_places)):
            high, low = parts_of(beside(ring, n, rim[k * chan : (k + 1) * chan]))
            high_rim[n, k] = high
            low_rim[n, k] = low
            keep(high_rim.at[n, k], high_all, rim_places[k], lanes)
            keep(low_rim.at[n, k], low_all, rim_places[k], lanes)

    for fetch in fetches:
        fetch.wait()
    for plane in range(depth):
        terms = []
        for a in range(3):
            if 0 <= plane + a - 1 < depth:
                for k in range(len(counts)):
                    terms.append((weights[k, a], field[k, plane + a - 1]))
        for n, edge in enumerate((0, depth - 1)):
            if plane == edge:
                for k in range(len(rim_places)):
                    right = [high_rim[n, k], high_rim[n, k], low_rim[n, k]]
                    terms.append((rim_weights[n, k], jnp.concatenate(right, axis=0)))
        answer = None
        for left, right in terms:
            term = dot(left, right)
            answer = term if answer is None else answer + term
        total = gathered(answer, out_rows)
        if total_in is not None:
            total = total + total_in[plane]
        total_out[plane] = total
    for copy in copies:
        copy.wait()


def forward(ring, sets, places, rim_places, outer, weights, carry, sizes):
    depth, chan, area, channels, out_rows = sizes
    counts = tuple(len(s) for s in sets)
    blocks = [b for s in sets for b in s]
    first = carry is None
    lanes = (depth + 2) * area
    keep = pl.BlockSpec(memory_space=pltpu.HBM)
    in_specs = [whole(b.shape) for b in blocks]
    args = list(blocks)
    in_specs.append(keep)
    args.append(weights)
    if rim_places:
        in_specs += [whole(o.shape) for o in outer]
        args += list(outer)
    aliases = {}
    if not first:
        base = len(args) + 1
        in_specs += [whole((depth, out_rows, area)), keep, keep]
        args += list(carry)
        aliases = {base: 0, base + 1: 1, base + 2: 2}
    rims_held = max(1, len(rim_places))
    return pl.pallas_call(
        functools.partial(forward_kernel, counts, places, rim_places, first),
        grid_spec=pltpu.PrefetchScalarGridSpec(
            num_scalar_prefetch=1,
            grid=(1,),
            in_specs=in_specs,
            out_specs=[whole((depth, out_rows, area)), keep, keep],
            scratch_shapes=[
                pltpu.VMEM((len(sets), depth, 3 * chan, area), bf16),
                pltpu.VMEM((len(sets), chan, depth * area), bf16),
                pltpu.VMEM((len(sets), chan, depth * area), bf16),
                pltpu.VMEM((2, rims_held, chan, area), bf16),
                pltpu.VMEM((2, rims_held, chan, area), bf16),
                pltpu.VMEM((len(sets), 3) + weights.shape[2:], bf16),
                pltpu.VMEM((2, rims_held) + weights.shape[2:], bf16),
                pltpu.SemaphoreType.DMA((2 * len(sets) + 4 * rims_held,)),
                pltpu.SemaphoreType.DMA((len(sets) + 2 * rims_held,)),
            ],
        ),
        out_shape=[
            jax.ShapeDtypeStruct((depth, out_rows, area), f32),
            jax.ShapeDtypeStruct((channels, lanes), bf16),
            jax.ShapeDtypeStruct((channels, lanes), bf16),
        ],
        input_output_aliases=aliases,
        cost_estimate=cost(
            len(sets) * 2 * 81 * out_rows * chan * depth * area, len(sets) * 8 * chan * lanes
        ),
        compiler_params=limit(),
        name="forward",
    )(ring, *args)


def middle_kernel(places, ring, total, grad, below, above, source, *refs):
    kept_out, spread_out, high_all, low_all, high_rim, low_rim, weights, sems, fetch_sems = refs[2:]
    depth, out_rows, area = total.shape
    chan = below.shape[0] // len(places)
    copies = []
    fetches = {}
    for n in range(2):
        for k, place in enumerate(places):
            fetches[n, k] = pltpu.make_async_copy(
                source.at[2 * n, ring[place]], weights.at[n, k], fetch_sems.at[n, k]
            )
            fetches[n, k].start()
    nothing = jnp.zeros((9 * out_rows, area), bf16)
    for part in range(2):
        spread_out[part, 0] = nothing
        spread_out[part, depth + 1] = nothing

    def finish(plane, value):
        positive = jnp.maximum(value, 0.0)
        kept_out[plane] = positive
        pre_grad = 2.0 * positive * grad[plane]
        for c in range(3):
            across = moved(pre_grad, 0, 1 - c)
            for b in range(3):
                high, low = parts_of(moved(across, 1 - b, 0))
                at = (3 * b + c) * out_rows
                spread_out[0, plane + 1, at : at + out_rows] = high
                spread_out[1, plane + 1, at : at + out_rows] = low

    for plane in range(1, depth - 1):
        finish(plane, total[plane])
    for n, rim in enumerate((below, above)):
        answer = None
        for k, place in enumerate(places):
            value = beside(ring, n, rim[k * chan : (k + 1) * chan])
            high, low = parts_of(value)
            high_rim[n, k] = high
            low_rim[n, k] = low
            at = pl.ds(pl.multiple_of(ring[place] * chan, chan), chan)
            lanes = pl.ds(n * (depth + 1) * area, area)
            for m, (part, target) in enumerate(((high_rim, high_all), (low_rim, low_all))):
                copy = pltpu.make_async_copy(part.at[n, k], target.at[at, lanes], sems.at[n, k, m])
                copy.start()
                copies.append(copy)
            fetches[n, k].wait()
            term = dot(weights[n, k], jnp.concatenate([high, high, low], axis=0))
            answer = term if answer is None else answer + term
        edge = n * (depth - 1)
        finish(edge, total[edge] + gathered(answer, out_rows))
    for copy in copies:
        copy.wait()


def middle(ring, carry, grad, places, outer, weights, chan):
    total, high_all, low_all = carry
    depth, out_rows, area = total.shape
    keep = pl.BlockSpec(memory_space=pltpu.HBM)
    return pl.pallas_call(
        functools.partial(middle_kernel, places),
        grid_spec=pltpu.PrefetchScalarGridSpec(
            num_scalar_prefetch=1,
            grid=(1,),
            in_specs=[whole(x.shape) for x in (total, grad, *outer)]
            + [keep, keep, keep],
            out_specs=[
                whole((depth, out_rows, area)),
                whole((2, depth + 2, 9 * out_rows, area)),
                keep,
                keep,
            ],
            scratch_shapes=[
                pltpu.VMEM((2, len(places), chan, area), bf16),
                pltpu.VMEM((2, len(places), chan, area), bf16),
                pltpu.VMEM((2, len(places)) + weights.shape[2:], bf16),
                pltpu.SemaphoreType.DMA((2, len(places), 2)),
                pltpu.SemaphoreType.DMA((2, len(places))),
            ],
        ),
        out_shape=[
            jax.ShapeDtypeStruct((depth, out_rows, area), f32),
            jax.ShapeDtypeStruct((2, depth + 2, 9 * out_rows, area), bf16),
            jax.ShapeDtypeStruct(high_all.shape, bf16),
            jax.ShapeDtypeStruct(low_all.shape, bf16),
        ],
        input_output_aliases={6: 2, 7: 3},
        cost_estimate=cost(0, 4 * 18 * out_rows * depth * area),
        compiler_params=limit(),
        name="middle",
    )(ring, total, grad, *outer, weights, high_all, low_all)


def turn_kernel(square, x, out):
    value = x[...]
    out[...] = jnp.swapaxes(value * value if square else value, 0, 1)


def turned(x, square):
    a, b, area = x.shape
    return pl.pallas_call(
        functools.partial(turn_kernel, square),
        out_shape=jax.ShapeDtypeStruct((b, a, area), f32),
        cost_estimate=cost(0, 8 * x.size),
        compiler_params=limit(),
    )(x)


def inner_kernel(begin, planes, spread, high, low, out):
    deep = high.shape[1]
    count, chan, _ = out.shape
    area = spread.shape[3]
    group = 2 - planes % 2

    def some(i, nothing):
        for j in range(group):
            near = spread[0, pl.ds(begin + i * group + j, 3)].reshape(deep, area)
            far = spread[1, pl.ds(begin + i * group + j, 3)].reshape(deep, area)
            value = dot(high[...], near) + dot(high[...], far) + dot(low[...], near)
            lanes = pl.ds(pl.multiple_of((i * group + j) * area, area), area)
            out[:, :, lanes] = value.reshape(count, chan, area)
        return nothing

    lax.fori_loop(0, planes // group, some, 0)


def outer_kernel(spread, high, low, below, above):
    depth = spread.shape[1] - 2
    third = high.shape[1] // 3
    for out, plane, at in ((below, 1, 2 * third), (above, depth, 0)):
        lanes = slice(at, at + third)
        value = dot(high[:, lanes], spread[0, plane]) + dot(high[:, lanes], spread[1, plane])
        value = value + dot(low[:, lanes], spread[0, plane])
        out[...] = value.reshape(out.shape)


def inner_terms(begin, planes, spread, high, low, chan):
    channels, deep = high.shape
    area = spread.shape[3]
    return pl.pallas_call(
        functools.partial(inner_kernel, begin, planes),
        out_shape=jax.ShapeDtypeStruct((channels // chan, chan, planes * area), f32),
        cost_estimate=cost(6 * channels * deep * planes * area, 2 * spread.size + 4 * high.size),
        compiler_params=limit(),
        name="inner_terms",
    )(spread, high, low)


def outer_terms(spread, high, low, chan):
    channels, deep = high.shape
    shape = jax.ShapeDtypeStruct((channels // chan, chan, spread.shape[3]), f32)
    return pl.pallas_call(
        outer_kernel,
        out_shape=[shape, shape],
        cost_estimate=cost(4 * channels * deep * spread.shape[3], spread.size),
        compiler_params=limit(),
        name="outer_terms",
    )(spread, high, low)


def filter_kernel(begin, end, scale, ring, spread, high, low, keep_out, send_out, total):
    depth = spread.shape[1] - 2
    area = spread.shape[3]
    out_rows = spread.shape[2] // 9
    half = (end - begin) * out_rows // 2
    channels = high.shape[0]
    step = min(256, channels)
    for a in range(3):
        first, last = max(begin, 9 * a), min(end, 9 * a + 9)
        if first >= last:
            continue
        rows = slice((first - 9 * a) * out_rows, (last - 9 * a) * out_rows)
        into = slice((first - begin) * out_rows, (last - begin) * out_rows)
        for at in range(0, channels, step):
            value = None
            for plane in range(depth):
                lanes = slice((a + plane) * area, (a + plane + 1) * area)
                right = high[at : at + step, lanes]
                near = spread[0, plane + 1, rows]
                term = dot_t(near, right) + dot_t(spread[1, plane + 1, rows], right)
                term = term + dot_t(near, low[at : at + step, lanes])
                value = term if value is None else value + term
            total[into, at : at + step] = value * (1.0 / scale)
    side = ring[ring.shape[0] - 1]
    keep_out[...] = total[pl.ds(pl.multiple_of(side * half, half), half), :]
    send_out[...] = total[pl.ds(pl.multiple_of((1 - side) * half, half), half), :]


def filter_terms(begin, end, scale, ring, spread, high, low):
    channels = high.shape[0]
    rows = (end - begin) * (spread.shape[2] // 9)
    return pl.pallas_call(
        functools.partial(filter_kernel, begin, end, scale),
        grid_spec=pltpu.PrefetchScalarGridSpec(
            num_scalar_prefetch=1,
            grid=(1,),
            in_specs=[whole(spread.shape), whole(high.shape), whole(low.shape)],
            out_specs=[whole((rows // 2, channels))] * 2,
            scratch_shapes=[pltpu.VMEM((rows, channels), f32)],
        ),
        out_shape=[jax.ShapeDtypeStruct((rows // 2, channels), f32)] * 2,
        cost_estimate=cost(6 * rows * high.size, 4 * high.size + 2 * spread.size),
        compiler_params=limit(),
        name="filter_terms",
    )(ring, spread, high, low)


def place_kernel(begin, ring, *refs):
    mine, other, out, sems = refs[0], refs[1], refs[-2], refs[-1]
    half = mine.shape[0]
    side = ring[ring.shape[0] - 1]
    copies = []
    for n, (part, at) in enumerate(((mine, side), (other, 1 - side))):
        rows = pl.ds(pl.multiple_of(begin + at * half, 8), half)
        copies.append(pltpu.make_async_copy(part, out.at[rows], sems.at[n]))
        copies[-1].start()
    for copy in copies:
        copy.wait()


def place(begin, ring, mine, other, carry, rows):
    half, channels = mine.shape
    keep = pl.BlockSpec(memory_space=pltpu.HBM)
    args = [mine, other]
    in_specs = [whole(mine.shape)] * 2
    aliases = {}
    if carry is not None:
        args.append(carry)
        in_specs.append(keep)
        aliases = {3: 0}
    return pl.pallas_call(
        functools.partial(place_kernel, begin),
        grid_spec=pltpu.PrefetchScalarGridSpec(
            num_scalar_prefetch=1,
            grid=(1,),
            in_specs=in_specs,
            out_specs=keep,
            scratch_shapes=[pltpu.SemaphoreType.DMA((2,))],
        ),
        out_shape=jax.ShapeDtypeStruct((rows, channels), f32),
        input_output_aliases=aliases,
        cost_estimate=cost(0, 16 * half * channels),
        compiler_params=limit(),
        name="place",
    )(ring, *args)


def local_sum(ring, inner, rim, first):
    value, rim = inner[0], beside(ring, 0 if first else 1, rim[0])
    area = rim.shape[1]
    width = value.shape[1]
    if first:
        return jnp.concatenate([value[:, :area] + rim, value[:, area:]], axis=1)
    return jnp.concatenate([value[:, : width - area], value[:, width - area :] + rim], axis=1)


def opening_kernel(first, ring, inner, rim, up_out, down_out):
    value = local_sum(ring, inner, rim, first)
    half = value.shape[0] // 2
    up_out[...] = value[:half]
    down_out[...] = value[half:]


def running_kernel(first, ring, up_inner, up_rim, down_inner, down_rim, up, down, up_out, down_out):
    value = local_sum(ring, up_inner, up_rim, first)
    size = up.shape[0]
    up_out[0:size] = value[0:size] + up[...]
    if size < value.shape[0]:
        up_out[size:] = value[size:]
    value = local_sum(ring, down_inner, down_rim, first)
    rest = value.shape[0] - size
    down_out[rest:] = value[rest:] + down[...]
    if rest:
        down_out[0:rest] = value[0:rest]


def closing_kernel(begin, ring, *refs):
    chains, (mine, other, _, out, whole_out, sems) = (refs[0:4], refs[4:8]), refs[8:]
    half = mine.shape[0]
    side = ring[ring.shape[0] - 1]
    copies = []
    for n, (part, at) in enumerate(((mine, side), (other, 1 - side))):
        rows = pl.ds(pl.multiple_of(begin + at * half, 8), half)
        copies.append(pltpu.make_async_copy(part, whole_out.at[rows], sems.at[n]))
        copies[-1].start()
    area = out.shape[2]
    values = []
    for first, (inner, rim, up, down) in zip((True, False), chains):
        value = local_sum(ring, inner, rim, first) + up[...] + down[...]
        values += [value[:, at : at + area] for at in range(0, value.shape[1], area)]
    out[...] = jnp.swapaxes(jnp.stack(values), 0, 1)
    for copy in copies:
        copy.wait()


def closing(ring, pieces, shape, begin, mine, other, carry):
    keep = pl.BlockSpec(memory_space=pltpu.HBM)
    specs, args = [], []
    for piece in pieces:
        if isinstance(piece, tuple):
            array, k = piece
            specs.append(pl.BlockSpec((1,) + array.shape[1:], lambda i, s, k=k: (s[k], 0, 0)))
            args.append(array)
        else:
            specs.append(whole(piece.shape))
            args.append(piece)
    return pl.pallas_call(
        functools.partial(closing_kernel, begin),
        grid_spec=pltpu.PrefetchScalarGridSpec(
            num_scalar_prefetch=1,
            grid=(1,),
            in_specs=specs + [whole(mine.shape), whole(other.shape), keep],
            out_specs=[whole(shape), keep],
            scratch_shapes=[pltpu.SemaphoreType.DMA((2,))],
        ),
        out_shape=[
            jax.ShapeDtypeStruct(shape, f32),
            jax.ShapeDtypeStruct(carry.shape, f32),
        ],
        input_output_aliases={len(args) + 3: 1},
        cost_estimate=cost(0, 12 * math.prod(shape)),
        compiler_params=limit(),
        name="closing",
    )(ring, *args, mine, other, carry)


def summed(kernel, ring, pieces, outs):
    specs, args = [], []
    for piece in pieces:
        if isinstance(piece, tuple):
            array, k = piece
            specs.append(pl.BlockSpec((1,) + array.shape[1:], lambda i, s, k=k: (s[k], 0, 0)))
            args.append(array)
        else:
            specs.append(whole(piece.shape))
            args.append(piece)
    return pl.pallas_call(
        kernel,
        grid_spec=pltpu.PrefetchScalarGridSpec(
            num_scalar_prefetch=1,
            grid=(1,),
            in_specs=specs,
            out_specs=[whole(o) for o in outs],
        ),
        out_shape=[jax.ShapeDtypeStruct(o, f32) for o in outs],
        cost_estimate=cost(0, sum(12 * math.prod(o) for o in outs)),
        compiler_params=limit(),
    )(ring, *args)


def shards(volume, filters, out_grad):
    chan, depth, area = volume.shape
    out_rows = filters.shape[1]
    channels = filters.shape[2]
    count = lax.axis_size("filt")
    slabs = lax.axis_size("slab")
    sizes = (depth, chan, area, channels, out_rows)

    order = list(range(0, count, 2)) + list(range(1, count, 2))[::-1]
    ring_up = [(order[i], order[(i + 1) % count]) for i in range(count)]
    ring_down = [(b, a) for a, b in ring_up]
    rows = [
        [order[(order.index(f) + k) % count] for k in range(count)]
        + [int(s > 0), int(s < slabs - 1), s % 2]
        for s in range(slabs)
        for f in range(count)
    ]
    here = lax.axis_index("slab") * count + lax.axis_index("filt")
    ring = lax.dynamic_index_in_dim(jnp.array(rows, jnp.int32), here, 0, keepdims=False)

    def send(x, pairs):
        return lax.ppermute(x, "filt", pairs)

    deeper = [(i, (i + 1) % slabs) for i in range(slabs)]
    shallower = [(b, a) for a, b in deeper]
    half = count // 2

    ahead, back_high, back_low = prepare(filters, chan)
    ahead = pltpu.with_memory_space_constraint(ahead, pltpu.HBM)

    carry = None
    up = down = volume
    rim_places, outer = (), None
    held, held_places = [], ()
    for step in range(half + 1):
        if step == 0:
            sets, places = [[volume]], (0,)
        elif step < half:
            up, down = send(up, ring_up), send(down, ring_down)
            sets, places = [[up], [down]], (count - step, step)
        else:
            up = send(up[: chan // 2], ring_up)
            down = send(down[chan // 2 :], ring_down)
            sets, places = [[up, down]], (half,)
        held += [b for blocks in sets for b in blocks]
        held_places += places
        carry = forward(ring, sets, places, rim_places, outer, ahead, carry, sizes)
        rim_places, outer = (), None
        if step not in (0, half - 1):
            last, top = rims(held)
            outer = lax.ppermute(last, "slab", deeper), lax.ppermute(top, "slab", shallower)
            rim_places, held, held_places = held_places, [], ()

    grads = turned(out_grad, False)
    positives, spread, high_field, low_field = middle(
        ring, carry, grads, rim_places, outer, ahead, chan
    )
    activated = turned(positives, True)

    below, above = outer_terms(spread, back_high, back_low, chan)
    from_below = lax.ppermute(above, "slab", deeper)
    from_above = lax.ppermute(below, "slab", shallower)
    runs = (depth * 5 // 8, depth - depth * 5 // 8)
    inner = []
    for c in range(2):
        begin = 0 if c == 0 else runs[0]
        inner.append(inner_terms(begin, runs[c], spread, back_high, back_low, chan))
    edge = [from_below, from_above]

    scale = math.sqrt(depth * slabs * area)

    def swap(x, bit):
        return lax.ppermute(x, "slab", [(i, i ^ bit) for i in range(slabs)])

    weight_grad = None
    taps = filters.shape[0]
    cuts = (0, 13, 20, taps)
    for begin, end in zip(cuts, cuts[1:]):
        keep, give = filter_terms(begin, end, scale, ring, spread, high_field, low_field)
        keep = keep + swap(give, 1)
        bit = 2
        while bit < slabs:
            keep = keep + swap(keep, bit)
            bit *= 2
        other = swap(keep, 1)
        if end < taps:
            weight_grad = place(begin * out_rows, ring, keep, other, weight_grad, taps * out_rows)

    pieces_of = [(chan, run * area) for run in runs]
    parts_for = [(chan // 2, run * area) for run in runs]
    flows = []
    for c in range(2):
        kernel = functools.partial(opening_kernel, c == 0)
        flows.append(summed(kernel, ring, [(inner[c], half), (edge[c], half)], [parts_for[c]] * 2))
    for step in range(half - 1, 0, -1):
        for c in range(2):
            up, down = flows[c]
            up, down = send(up, ring_up), send(down, ring_down)
            kernel = functools.partial(running_kernel, c == 0)
            pieces = [(x, p) for p in (step, count - step) for x in (inner[c], edge[c])]
            flows[c] = summed(kernel, ring, pieces + [up, down], [pieces_of[c]] * 2)
    pieces = []
    for c in range(2):
        up, down = flows[c]
        pieces += [(inner[c], 0), (edge[c], 0), send(up, ring_up), send(down, ring_down)]
    input_grad, weight_grad = closing(
        ring, pieces, (chan, depth, area), cuts[-2] * out_rows, keep, other, weight_grad
    )
    return activated, input_grad, weight_grad.reshape(filters.shape)


def solution(mesh):
    placed = (P("filt", "slab", None), P(None, "filt", None), P("filt", "slab", None))

    def step(*args):
        return shards(*args)

    step = jax.shard_map(
        step,
        mesh=mesh,
        in_specs=placed,
        out_specs=(P("filt", "slab", None), P("filt", "slab", None), P(None, "filt", None)),
        check_vma=False,
    )
    return step
```

```python
import functools
import math

import jax
import jax.numpy as jnp
from jax import lax
from jax.experimental import pallas as pl
from jax.experimental.pallas import tpu as pltpu
from jax.sharding import PartitionSpec as P


WIDTH = 16


f32 = jnp.float32
bf16 = jnp.bfloat16


def parts_of(x):
    high = x.astype(bf16)
    low = (x - high.astype(f32)).astype(bf16)
    return high, low


def dot(a, b):
    return lax.dot_general(a, b, (((1,), (0,)), ((), ())), preferred_element_type=f32)


def dot_t(a, b):
    return lax.dot_general(a, b, (((1,), (1,)), ((), ())), preferred_element_type=f32)


def beside(ring, n, rim):
    return jnp.where(ring[ring.shape[0] - 3 + n] > 0, rim, 0.0)


def whole(shape):
    return pl.BlockSpec(shape, lambda *_: (0,) * len(shape))


def limit():
    return pltpu.CompilerParams(vmem_limit_bytes=28 * 2**20)


def cost(flops, moved):
    return pl.CostEstimate(flops=int(flops), bytes_accessed=int(moved), transcendentals=0)


def moved(x, down, across):
    size = x.shape[-1]
    place = lax.broadcasted_iota(jnp.int32, x.shape, 1)
    if across:
        column = place % WIDTH + across
        rolled = pltpu.roll(x, (-across) % size, 1)
        x = jnp.where((column >= 0) & (column < WIDTH), rolled, 0.0)
    if down:
        target = place + down * WIDTH
        rolled = pltpu.roll(x, (-down * WIDTH) % size, 1)
        x = jnp.where((target >= 0) & (target < size), rolled, 0.0)
    return x


def prepare_kernel(chan, filters, ahead, back_high, back_low):
    taps, out_rows, lanes = filters.shape
    third = taps * out_rows // 3
    for a in range(3):
        x = filters[a * 9 : (a + 1) * 9].reshape(third, lanes)
        high, low = parts_of(x)
        for k in range(lanes // chan):
            at = slice(k * chan, (k + 1) * chan)
            ahead[a, k] = jnp.concatenate([high[:, at], low[:, at], high[:, at]], axis=1)
    turned = [filters[a * 9 : (a + 1) * 9].reshape(third, lanes).T for a in (2, 1, 0)]
    high, low = parts_of(jnp.concatenate(turned, axis=1))
    back_high[...] = high
    back_low[...] = low


def prepare(filters, chan):
    taps, out_rows, channels = filters.shape
    lanes = min(128, channels)
    each = lanes // chan
    return pl.pallas_call(
        functools.partial(prepare_kernel, chan),
        grid=(channels // lanes,),
        in_specs=[pl.BlockSpec((taps, out_rows, lanes), lambda i: (0, 0, i))],
        out_specs=[
            pl.BlockSpec((3, each, 9 * out_rows, 3 * chan), lambda i: (0, i, 0, 0)),
            pl.BlockSpec((lanes, taps * out_rows), lambda i: (i, 0)),
            pl.BlockSpec((lanes, taps * out_rows), lambda i: (i, 0)),
        ],
        out_shape=[
            jax.ShapeDtypeStruct((3, channels // chan, 9 * out_rows, 3 * chan), bf16),
            jax.ShapeDtypeStruct((channels, taps * out_rows), bf16),
            jax.ShapeDtypeStruct((channels, taps * out_rows), bf16),
        ],
        cost_estimate=cost(0, 5 * 4 * filters.size),
        name="prepare",
    )(filters)


def rims_kernel(*refs):
    blocks, (last, top) = refs[:-2], refs[-2:]
    at = 0
    for block in blocks:
        rows, depth, _ = block.shape
        planes = jnp.swapaxes(block[...], 0, 1)
        last[at : at + rows] = planes[depth - 1]
        top[at : at + rows] = planes[0]
        at += rows


def rims(blocks):
    rows = sum(b.shape[0] for b in blocks)
    shape = jax.ShapeDtypeStruct((rows, blocks[0].shape[2]), f32)
    return pl.pallas_call(
        rims_kernel,
        out_shape=[shape, shape],
        cost_estimate=cost(0, 4 * sum(b.size for b in blocks)),
        compiler_params=limit(),
        name="rims",
    )(*blocks)


def gathered(answer, out_rows):
    rows = []
    for b in range(3):
        row = None
        for c in range(3):
            at = (3 * b + c) * out_rows
            term = moved(answer[at : at + out_rows], 0, c - 1)
            row = term if row is None else row + term
        rows.append(moved(row, b - 1, 0))
    return rows[0] + rows[1] + rows[2]


def forward_kernel(counts, places, rim_places, first, ring, *refs):
    refs = list(refs)

    def take(n):
        taken = refs[:n]
        del refs[:n]
        return taken

    blocks = take(sum(counts))
    (source,) = take(1)
    rims_in = take(2) if rim_places else []
    total_in = None if first else take(3)[0]
    total_out, high_all, low_all, field, high_part, low_part, high_rim, low_rim = take(8)
    weights, rim_weights, sems, fetch_sems = refs
    fetches = [
        pltpu.make_async_copy(source.at[:, ring[place]], weights.at[k], fetch_sems.at[k])
        for k, place in enumerate(places)
    ]
    for k, place in enumerate(rim_places):
        for n in range(2):
            sem = fetch_sems.at[len(fetches)]
            fetches.append(
                pltpu.make_async_copy(source.at[2 * n, ring[place]], rim_weights.at[n, k], sem)
            )
    for fetch in fetches:
        fetch.start()
    depth, out_rows, area = total_out.shape
    chan = field.shape[2] // 3
    copies = []

    def keep(part, target, place, lanes):
        at = pl.ds(pl.multiple_of(ring[place] * chan, chan), chan)
        copies.append(pltpu.make_async_copy(part, target.at[at, lanes], sems.at[len(copies)]))
        copies[-1].start()

    begin = 0
    for k, pieces in enumerate(counts):
        loaded = [jnp.swapaxes(b[...], 0, 1) for b in blocks[begin : begin + pieces]]
        begin += pieces
        for plane in range(depth):
            rows = [b[plane] for b in loaded]
            x = rows[0] if pieces == 1 else jnp.concatenate(rows, axis=0)
            high, low = parts_of(x)
            field[k, plane, 0:chan] = high
            field[k, plane, chan : 2 * chan] = high
            field[k, plane, 2 * chan : 3 * chan] = low
            high_part[k, :, plane * area : (plane + 1) * area] = high
            low_part[k, :, plane * area : (plane + 1) * area] = low
        lanes = pl.ds(area, depth * area)
        keep(high_part.at[k], high_all, places[k], lanes)
        keep(low_part.at[k], low_all, places[k], lanes)
    for n, rim in enumerate(rims_in):
        lanes = pl.ds(n * (depth + 1) * area, area)
        for k in range(len(rim_places)):
            high, low = parts_of(beside(ring, n, rim[k * chan : (k + 1) * chan]))
            high_rim[n, k] = high
            low_rim[n, k] = low
            keep(high_rim.at[n, k], high_all, rim_places[k], lanes)
            keep(low_rim.at[n, k], low_all, rim_places[k], lanes)

    for fetch in fetches:
        fetch.wait()
    for plane in range(depth):
        terms = []
        for a in range(3):
            if 0 <= plane + a - 1 < depth:
                for k in range(len(counts)):
                    terms.append((weights[k, a], field[k, plane + a - 1]))
        for n, edge in enumerate((0, depth - 1)):
            if plane == edge:
                for k in range(len(rim_places)):
                    right = [high_rim[n, k], high_rim[n, k], low_rim[n, k]]
                    terms.append((rim_weights[n, k], jnp.concatenate(right, axis=0)))
        answer = None
        for left, right in terms:
            term = dot(left, right)
            answer = term if answer is None else answer + term
        total = gathered(answer, out_rows)
        if total_in is not None:
            total = total + total_in[plane]
        total_out[plane] = total
    for copy in copies:
        copy.wait()


def forward(ring, sets, places, rim_places, outer, weights, carry, sizes):
    depth, chan, area, channels, out_rows = sizes
    counts = tuple(len(s) for s in sets)
    blocks = [b for s in sets for b in s]
    first = carry is None
    lanes = (depth + 2) * area
    keep = pl.BlockSpec(memory_space=pltpu.HBM)
    in_specs = [whole(b.shape) for b in blocks]
    args = list(blocks)
    in_specs.append(keep)
    args.append(weights)
    if rim_places:
        in_specs += [whole(o.shape) for o in outer]
        args += list(outer)
    aliases = {}
    if not first:
        base = len(args) + 1
        in_specs += [whole((depth, out_rows, area)), keep, keep]
        args += list(carry)
        aliases = {base: 0, base + 1: 1, base + 2: 2}
    rims_held = max(1, len(rim_places))
    return pl.pallas_call(
        functools.partial(forward_kernel, counts, places, rim_places, first),
        grid_spec=pltpu.PrefetchScalarGridSpec(
            num_scalar_prefetch=1,
            grid=(1,),
            in_specs=in_specs,
            out_specs=[whole((depth, out_rows, area)), keep, keep],
            scratch_shapes=[
                pltpu.VMEM((len(sets), depth, 3 * chan, area), bf16),
                pltpu.VMEM((len(sets), chan, depth * area), bf16),
                pltpu.VMEM((len(sets), chan, depth * area), bf16),
                pltpu.VMEM((2, rims_held, chan, area), bf16),
                pltpu.VMEM((2, rims_held, chan, area), bf16),
                pltpu.VMEM((len(sets), 3) + weights.shape[2:], bf16),
                pltpu.VMEM((2, rims_held) + weights.shape[2:], bf16),
                pltpu.SemaphoreType.DMA((2 * len(sets) + 4 * rims_held,)),
                pltpu.SemaphoreType.DMA((len(sets) + 2 * rims_held,)),
            ],
        ),
        out_shape=[
            jax.ShapeDtypeStruct((depth, out_rows, area), f32),
            jax.ShapeDtypeStruct((channels, lanes), bf16),
            jax.ShapeDtypeStruct((channels, lanes), bf16),
        ],
        input_output_aliases=aliases,
        cost_estimate=cost(
            len(sets) * 2 * 81 * out_rows * chan * depth * area, len(sets) * 8 * chan * lanes
        ),
        compiler_params=limit(),
        name="forward",
    )(ring, *args)


def middle_kernel(places, ring, total, grad, shifts, below, above, source, *refs):
    kept_out, spread_out, high_all, low_all, high_rim, low_rim, weights = refs[2:9]
    sems, fetch_sems = refs[9:]
    left = {}
    depth, out_rows, area = total.shape
    chan = below.shape[0] // len(places)
    copies = []
    fetches = {}
    for n in range(2):
        for k, place in enumerate(places):
            fetches[n, k] = pltpu.make_async_copy(
                source.at[2 * n, ring[place]], weights.at[n, k], fetch_sems.at[n, k]
            )
            fetches[n, k].start()
    nothing = jnp.zeros((9 * out_rows, area), bf16)
    for part in range(2):
        spread_out[part, 0] = nothing
        spread_out[part, depth + 1] = nothing

    def keep(plane, value):
        positive = jnp.maximum(value, 0.0)
        kept_out[plane] = positive
        high, low = parts_of(2.0 * positive * grad[plane])
        left[plane] = [high, low]

    def scatter(planes, lines):
        for t in range(9):
            copies_of = lines if t == 4 else dot(lines, shifts[t]).astype(bf16)
            at = slice(t * out_rows, (t + 1) * out_rows)
            for k, plane in enumerate(planes):
                for part in range(2):
                    from_row = (2 * k + part) * out_rows
                    spread_out[part, plane + 1, at] = copies_of[from_row : from_row + out_rows]

    for plane in range(1, depth - 1):
        keep(plane, total[plane])
    middle_of = depth // 2
    for planes in (range(1, middle_of), range(middle_of, depth - 1)):
        scatter(planes, jnp.concatenate([x for p in planes for x in left[p]], axis=0))
    for n, rim in enumerate((below, above)):
        answer = None
        for k, place in enumerate(places):
            value = beside(ring, n, rim[k * chan : (k + 1) * chan])
            high, low = parts_of(value)
            high_rim[n, k] = high
            low_rim[n, k] = low
            at = pl.ds(pl.multiple_of(ring[place] * chan, chan), chan)
            lanes = pl.ds(n * (depth + 1) * area, area)
            for m, (part, target) in enumerate(((high_rim, high_all), (low_rim, low_all))):
                copy = pltpu.make_async_copy(part.at[n, k], target.at[at, lanes], sems.at[n, k, m])
                copy.start()
                copies.append(copy)
            fetches[n, k].wait()
            term = dot(weights[n, k], jnp.concatenate([high, high, low], axis=0))
            answer = term if answer is None else answer + term
        edge = n * (depth - 1)
        keep(edge, total[edge] + gathered(answer, out_rows))
    scatter((0, depth - 1), jnp.concatenate(left[0] + left[depth - 1], axis=0))
    for copy in copies:
        copy.wait()


def middle(ring, carry, grad, shifts, places, outer, weights, chan):
    total, high_all, low_all = carry
    depth, out_rows, area = total.shape
    keep = pl.BlockSpec(memory_space=pltpu.HBM)
    return pl.pallas_call(
        functools.partial(middle_kernel, places),
        grid_spec=pltpu.PrefetchScalarGridSpec(
            num_scalar_prefetch=1,
            grid=(1,),
            in_specs=[whole(x.shape) for x in (total, grad, shifts, *outer)]
            + [keep, keep, keep],
            out_specs=[
                whole((depth, out_rows, area)),
                whole((2, depth + 2, 9 * out_rows, area)),
                keep,
                keep,
            ],
            scratch_shapes=[
                pltpu.VMEM((2, len(places), chan, area), bf16),
                pltpu.VMEM((2, len(places), chan, area), bf16),
                pltpu.VMEM((2, len(places)) + weights.shape[2:], bf16),
                pltpu.SemaphoreType.DMA((2, len(places), 2)),
                pltpu.SemaphoreType.DMA((2, len(places))),
            ],
        ),
        out_shape=[
            jax.ShapeDtypeStruct((depth, out_rows, area), f32),
            jax.ShapeDtypeStruct((2, depth + 2, 9 * out_rows, area), bf16),
            jax.ShapeDtypeStruct(high_all.shape, bf16),
            jax.ShapeDtypeStruct(low_all.shape, bf16),
        ],
        input_output_aliases={7: 2, 8: 3},
        cost_estimate=cost(0, 4 * 18 * out_rows * depth * area),
        compiler_params=limit(),
        name="middle",
    )(ring, total, grad, shifts, *outer, weights, high_all, low_all)


def turn_kernel(square, x, out):
    value = x[...]
    out[...] = jnp.swapaxes(value * value if square else value, 0, 1)


def turned(x, square):
    a, b, area = x.shape
    return pl.pallas_call(
        functools.partial(turn_kernel, square),
        out_shape=jax.ShapeDtypeStruct((b, a, area), f32),
        cost_estimate=cost(0, 8 * x.size),
        compiler_params=limit(),
    )(x)


def opening_turn_kernel(x, out, shifts):
    out[...] = jnp.swapaxes(x[...], 0, 1)
    area = x.shape[2]
    source = lax.broadcasted_iota(jnp.int32, (area, area), 0)
    target = lax.broadcasted_iota(jnp.int32, (area, area), 1)
    down = target // WIDTH - source // WIDTH
    across = target % WIDTH - source % WIDTH
    for t in range(9):
        hit = (down == t // 3 - 1) & (across == t % 3 - 1)
        shifts[t] = jnp.where(hit, 1.0, 0.0).astype(bf16)


def opening_turn(x):
    a, b, area = x.shape
    return pl.pallas_call(
        opening_turn_kernel,
        out_shape=[
            jax.ShapeDtypeStruct((b, a, area), f32),
            jax.ShapeDtypeStruct((9, area, area), bf16),
        ],
        cost_estimate=cost(0, 8 * x.size),
        compiler_params=limit(),
        name="turn",
    )(x)


def inner_kernel(begin, planes, spread, high, low, out):
    deep = high.shape[1]
    count, chan, _ = out.shape
    area = spread.shape[3]
    group = 2 - planes % 2

    def some(i, nothing):
        for j in range(group):
            near = spread[0, pl.ds(begin + i * group + j, 3)].reshape(deep, area)
            far = spread[1, pl.ds(begin + i * group + j, 3)].reshape(deep, area)
            value = dot(high[...], near) + dot(high[...], far) + dot(low[...], near)
            lanes = pl.ds(pl.multiple_of((i * group + j) * area, area), area)
            out[:, :, lanes] = value.reshape(count, chan, area)
        return nothing

    lax.fori_loop(0, planes // group, some, 0)


def outer_kernel(spread, high, low, below, above):
    depth = spread.shape[1] - 2
    third = high.shape[1] // 3
    for out, plane, at in ((below, 1, 2 * third), (above, depth, 0)):
        lanes = slice(at, at + third)
        value = dot(high[:, lanes], spread[0, plane]) + dot(high[:, lanes], spread[1, plane])
        value = value + dot(low[:, lanes], spread[0, plane])
        out[...] = value.reshape(out.shape)


def inner_terms(begin, planes, spread, high, low, chan):
    channels, deep = high.shape
    area = spread.shape[3]
    return pl.pallas_call(
        functools.partial(inner_kernel, begin, planes),
        out_shape=jax.ShapeDtypeStruct((channels // chan, chan, planes * area), f32),
        cost_estimate=cost(6 * channels * deep * planes * area, 2 * spread.size + 4 * high.size),
        compiler_params=limit(),
        name="inner_terms",
    )(spread, high, low)


def outer_terms(spread, high, low, chan):
    channels, deep = high.shape
    shape = jax.ShapeDtypeStruct((channels // chan, chan, spread.shape[3]), f32)
    return pl.pallas_call(
        outer_kernel,
        out_shape=[shape, shape],
        cost_estimate=cost(4 * channels * deep * spread.shape[3], spread.size),
        compiler_params=limit(),
        name="outer_terms",
    )(spread, high, low)


def filter_kernel(begin, end, scale, ring, spread, high, low, keep_out, send_out, total):
    depth = spread.shape[1] - 2
    area = spread.shape[3]
    out_rows = spread.shape[2] // 9
    half = (end - begin) * out_rows // 2
    channels = high.shape[0]
    step = min(256, channels)
    for a in range(3):
        first, last = max(begin, 9 * a), min(end, 9 * a + 9)
        if first >= last:
            continue
        rows = slice((first - 9 * a) * out_rows, (last - 9 * a) * out_rows)
        into = slice((first - begin) * out_rows, (last - begin) * out_rows)
        for at in range(0, channels, step):
            value = None
            for plane in range(depth):
                lanes = slice((a + plane) * area, (a + plane + 1) * area)
                right = high[at : at + step, lanes]
                near = spread[0, plane + 1, rows]
                term = dot_t(near, right) + dot_t(spread[1, plane + 1, rows], right)
                term = term + dot_t(near, low[at : at + step, lanes])
                value = term if value is None else value + term
            total[into, at : at + step] = value * (1.0 / scale)
    side = ring[ring.shape[0] - 1]
    keep_out[...] = total[pl.ds(pl.multiple_of(side * half, half), half), :]
    send_out[...] = total[pl.ds(pl.multiple_of((1 - side) * half, half), half), :]


def filter_terms(begin, end, scale, ring, spread, high, low):
    channels = high.shape[0]
    rows = (end - begin) * (spread.shape[2] // 9)
    return pl.pallas_call(
        functools.partial(filter_kernel, begin, end, scale),
        grid_spec=pltpu.PrefetchScalarGridSpec(
            num_scalar_prefetch=1,
            grid=(1,),
            in_specs=[whole(spread.shape), whole(high.shape), whole(low.shape)],
            out_specs=[whole((rows // 2, channels))] * 2,
            scratch_shapes=[pltpu.VMEM((rows, channels), f32)],
        ),
        out_shape=[jax.ShapeDtypeStruct((rows // 2, channels), f32)] * 2,
        cost_estimate=cost(6 * rows * high.size, 4 * high.size + 2 * spread.size),
        compiler_params=limit(),
        name="filter_terms",
    )(ring, spread, high, low)


def place_kernel(begin, ring, *refs):
    mine, other, out, sems = refs[0], refs[1], refs[-2], refs[-1]
    half = mine.shape[0]
    side = ring[ring.shape[0] - 1]
    copies = []
    for n, (part, at) in enumerate(((mine, side), (other, 1 - side))):
        rows = pl.ds(pl.multiple_of(begin + at * half, 8), half)
        copies.append(pltpu.make_async_copy(part, out.at[rows], sems.at[n]))
        copies[-1].start()
    for copy in copies:
        copy.wait()


def place(begin, ring, mine, other, carry, rows):
    half, channels = mine.shape
    keep = pl.BlockSpec(memory_space=pltpu.HBM)
    args = [mine, other]
    in_specs = [whole(mine.shape)] * 2
    aliases = {}
    if carry is not None:
        args.append(carry)
        in_specs.append(keep)
        aliases = {3: 0}
    return pl.pallas_call(
        functools.partial(place_kernel, begin),
        grid_spec=pltpu.PrefetchScalarGridSpec(
            num_scalar_prefetch=1,
            grid=(1,),
            in_specs=in_specs,
            out_specs=keep,
            scratch_shapes=[pltpu.SemaphoreType.DMA((2,))],
        ),
        out_shape=jax.ShapeDtypeStruct((rows, channels), f32),
        input_output_aliases=aliases,
        cost_estimate=cost(0, 16 * half * channels),
        compiler_params=limit(),
        name="place",
    )(ring, *args)


def local_sum(ring, inner, rim, first):
    value, rim = inner[0], beside(ring, 0 if first else 1, rim[0])
    area = rim.shape[1]
    width = value.shape[1]
    if first:
        return jnp.concatenate([value[:, :area] + rim, value[:, area:]], axis=1)
    return jnp.concatenate([value[:, : width - area], value[:, width - area :] + rim], axis=1)


def opening_kernel(first, ring, inner, rim, up_out, down_out):
    value = local_sum(ring, inner, rim, first)
    half = value.shape[0] // 2
    up_out[...] = value[:half]
    down_out[...] = value[half:]


def running_kernel(first, ring, up_inner, up_rim, down_inner, down_rim, up, down, up_out, down_out):
    value = local_sum(ring, up_inner, up_rim, first)
    size = up.shape[0]
    up_out[0:size] = value[0:size] + up[...]
    if size < value.shape[0]:
        up_out[size:] = value[size:]
    value = local_sum(ring, down_inner, down_rim, first)
    rest = value.shape[0] - size
    down_out[rest:] = value[rest:] + down[...]
    if rest:
        down_out[0:rest] = value[0:rest]


def closing_kernel(begin, ring, *refs):
    chains, (mine, other, _, out, whole_out, sems) = (refs[0:4], refs[4:8]), refs[8:]
    half = mine.shape[0]
    side = ring[ring.shape[0] - 1]
    copies = []
    for n, (part, at) in enumerate(((mine, side), (other, 1 - side))):
        rows = pl.ds(pl.multiple_of(begin + at * half, 8), half)
        copies.append(pltpu.make_async_copy(part, whole_out.at[rows], sems.at[n]))
        copies[-1].start()
    area = out.shape[2]
    values = []
    for first, (inner, rim, up, down) in zip((True, False), chains):
        value = local_sum(ring, inner, rim, first) + up[...] + down[...]
        values += [value[:, at : at + area] for at in range(0, value.shape[1], area)]
    out[...] = jnp.swapaxes(jnp.stack(values), 0, 1)
    for copy in copies:
        copy.wait()


def closing(ring, pieces, shape, begin, mine, other, carry):
    keep = pl.BlockSpec(memory_space=pltpu.HBM)
    specs, args = [], []
    for piece in pieces:
        if isinstance(piece, tuple):
            array, k = piece
            specs.append(pl.BlockSpec((1,) + array.shape[1:], lambda i, s, k=k: (s[k], 0, 0)))
            args.append(array)
        else:
            specs.append(whole(piece.shape))
            args.append(piece)
    return pl.pallas_call(
        functools.partial(closing_kernel, begin),
        grid_spec=pltpu.PrefetchScalarGridSpec(
            num_scalar_prefetch=1,
            grid=(1,),
            in_specs=specs + [whole(mine.shape), whole(other.shape), keep],
            out_specs=[whole(shape), keep],
            scratch_shapes=[pltpu.SemaphoreType.DMA((2,))],
        ),
        out_shape=[
            jax.ShapeDtypeStruct(shape, f32),
            jax.ShapeDtypeStruct(carry.shape, f32),
        ],
        input_output_aliases={len(args) + 3: 1},
        cost_estimate=cost(0, 12 * math.prod(shape)),
        compiler_params=limit(),
        name="closing",
    )(ring, *args, mine, other, carry)


def summed(kernel, ring, pieces, outs):
    specs, args = [], []
    for piece in pieces:
        if isinstance(piece, tuple):
            array, k = piece
            specs.append(pl.BlockSpec((1,) + array.shape[1:], lambda i, s, k=k: (s[k], 0, 0)))
            args.append(array)
        else:
            specs.append(whole(piece.shape))
            args.append(piece)
    return pl.pallas_call(
        kernel,
        grid_spec=pltpu.PrefetchScalarGridSpec(
            num_scalar_prefetch=1,
            grid=(1,),
            in_specs=specs,
            out_specs=[whole(o) for o in outs],
        ),
        out_shape=[jax.ShapeDtypeStruct(o, f32) for o in outs],
        cost_estimate=cost(0, sum(12 * math.prod(o) for o in outs)),
        compiler_params=limit(),
    )(ring, *args)


def shards(volume, filters, out_grad):
    chan, depth, area = volume.shape
    out_rows = filters.shape[1]
    channels = filters.shape[2]
    count = lax.axis_size("filt")
    slabs = lax.axis_size("slab")
    sizes = (depth, chan, area, channels, out_rows)

    order = list(range(0, count, 2)) + list(range(1, count, 2))[::-1]
    ring_up = [(order[i], order[(i + 1) % count]) for i in range(count)]
    ring_down = [(b, a) for a, b in ring_up]
    rows = [
        [order[(order.index(f) + k) % count] for k in range(count)]
        + [int(s > 0), int(s < slabs - 1), s % 2]
        for s in range(slabs)
        for f in range(count)
    ]
    here = lax.axis_index("slab") * count + lax.axis_index("filt")
    ring = lax.dynamic_index_in_dim(jnp.array(rows, jnp.int32), here, 0, keepdims=False)

    def send(x, pairs):
        return lax.ppermute(x, "filt", pairs)

    deeper = [(i, (i + 1) % slabs) for i in range(slabs)]
    shallower = [(b, a) for a, b in deeper]
    half = count // 2

    ahead, back_high, back_low = prepare(filters, chan)
    ahead = pltpu.with_memory_space_constraint(ahead, pltpu.HBM)

    carry = None
    up = down = volume
    rim_places, outer = (), None
    held, held_places = [], ()
    for step in range(half + 1):
        if step == 0:
            sets, places = [[volume]], (0,)
        elif step < half:
            up, down = send(up, ring_up), send(down, ring_down)
            sets, places = [[up], [down]], (count - step, step)
        else:
            up = send(up[: chan // 2], ring_up)
            down = send(down[chan // 2 :], ring_down)
            sets, places = [[up, down]], (half,)
        held += [b for blocks in sets for b in blocks]
        held_places += places
        carry = forward(ring, sets, places, rim_places, outer, ahead, carry, sizes)
        rim_places, outer = (), None
        if step not in (0, half - 1):
            last, top = rims(held)
            outer = lax.ppermute(last, "slab", deeper), lax.ppermute(top, "slab", shallower)
            rim_places, held, held_places = held_places, [], ()

    grads, shifts = opening_turn(out_grad)
    positives, spread, high_field, low_field = middle(
        ring, carry, grads, shifts, rim_places, outer, ahead, chan
    )
    activated = turned(positives, True)

    below, above = outer_terms(spread, back_high, back_low, chan)
    from_below = lax.ppermute(above, "slab", deeper)
    from_above = lax.ppermute(below, "slab", shallower)
    runs = (depth * 5 // 8, depth - depth * 5 // 8)
    inner = []
    for c in range(2):
        begin = 0 if c == 0 else runs[0]
        inner.append(inner_terms(begin, runs[c], spread, back_high, back_low, chan))
    edge = [from_below, from_above]

    scale = math.sqrt(depth * slabs * area)

    def swap(x, bit):
        return lax.ppermute(x, "slab", [(i, i ^ bit) for i in range(slabs)])

    weight_grad = None
    taps = filters.shape[0]
    cuts = (0, 13, 20, taps)
    for begin, end in zip(cuts, cuts[1:]):
        keep, give = filter_terms(begin, end, scale, ring, spread, high_field, low_field)
        keep = keep + swap(give, 1)
        bit = 2
        while bit < slabs:
            keep = keep + swap(keep, bit)
            bit *= 2
        other = swap(keep, 1)
        if end < taps:
            weight_grad = place(begin * out_rows, ring, keep, other, weight_grad, taps * out_rows)

    pieces_of = [(chan, run * area) for run in runs]
    parts_for = [(chan // 2, run * area) for run in runs]
    flows = []
    for c in range(2):
        kernel = functools.partial(opening_kernel, c == 0)
        flows.append(summed(kernel, ring, [(inner[c], half), (edge[c], half)], [parts_for[c]] * 2))
    for step in range(half - 1, 0, -1):
        for c in range(2):
            up, down = flows[c]
            up, down = send(up, ring_up), send(down, ring_down)
            kernel = functools.partial(running_kernel, c == 0)
            pieces = [(x, p) for p in (step, count - step) for x in (inner[c], edge[c])]
            flows[c] = summed(kernel, ring, pieces + [up, down], [pieces_of[c]] * 2)
    pieces = []
    for c in range(2):
        up, down = flows[c]
        pieces += [(inner[c], 0), (edge[c], 0), send(up, ring_up), send(down, ring_down)]
    input_grad, weight_grad = closing(
        ring, pieces, (chan, depth, area), cuts[-2] * out_rows, keep, other, weight_grad
    )
    return activated, input_grad, weight_grad.reshape(filters.shape)


def solution(mesh):
    placed = (P("filt", "slab", None), P(None, "filt", None), P("filt", "slab", None))

    def step(*args):
        return shards(*args)

    step = jax.shard_map(
        step,
        mesh=mesh,
        in_specs=placed,
        out_specs=(P("filt", "slab", None), P("filt", "slab", None), P(None, "filt", None)),
        check_vma=False,
    )
    return step
```
